512 devices in a mesh: space: 128 (over y_hi, x, z, core), filt: 4 (over y_lo).
Axes of the slice: x: 4, y: 8 (y_hi: 2, y_lo: 4; y = y_hi * 4 + y_lo), z: 8, core: 2. Of those that a mesh axis runs over, the one named last changes fastest.
Arguments:
- image: bfloat16 [96, 512, 1024], P(None, 'space', 'filt'), may hold values from -6 to 6
- cotangent: bfloat16 [96, 512, 1024], P(None, 'space', 'filt'), may hold values from -6 to 6
- kernel: float32 [96, 7, 7], replicated, may hold values from -0.875 to 0.875
- dw_bias: float32 [96], replicated, may hold values from -0.5 to 0.5
- layer_norm_gain: float32 [96], replicated, may hold values from 0.5 to 1.5
- layer_norm_bias: float32 [96], replicated, may hold values from -3 to 3
- w_expand: bfloat16 [384, 96], replicated, may hold values from -0.625 to 0.625
- b_expand: bfloat16 [384], replicated, may hold values from -3 to 3
- w_reduce: bfloat16 [384, 96], replicated, may hold values from -0.3125 to 0.3125
- b_reduce: float32 [96], replicated, may hold values from -3 to 3
- layer_scale: float32 [96], replicated, may hold values from 0.2 to 1
Outputs:
- output: bfloat16 [96, 512, 1024], P(None, 'space', 'filt')
- image_grad: bfloat16 [96, 512, 1024], P(None, 'space', 'filt')
- kernel_grad: float32 [96, 7, 7], replicated
- dw_bias_grad: float32 [96], replicated
- gain_grad: float32 [96], replicated
- ln_bias_grad: float32 [96], replicated
- expand_grad: float32 [384, 96], P('filt')
- expand_bias_grad: float32 [384], P('filt')
- reduce_grad: float32 [384, 96], P('filt')
- reduce_bias_grad: float32 [96], replicated
- scale_grad: float32 [96], replicated
The draws below stay inside these ranges and needn't reach their ends.
All inputs are finite; a program needn't handle non-finite values.
Results may differ from the reference program's by a relative error of at most 0.011.
Values may be sent and summed in bfloat16 or wider, within the bound.
A program may use at most 64 MiB of HBM per device.

```python
import math
import jax
import jax.numpy as jnp
from jax import lax

C = 96
HID = 384
KSIZE = 7
HEIGHT = 512
WIDTH = 1024
TOKENS = 524288


def block_scale(own_key, extent, split, smallest, top_value):
    def one(axis_at, parts):
        heights = jax.random.uniform(jax.random.fold_in(jax.random.fold_in(own_key, 6), axis_at), (parts,), jnp.float32, smallest / len(split), top_value / len(split))
        return jnp.repeat(jnp.exp(heights), extent[axis_at] // parts).reshape((-1,) + (1,) * (len(extent) - axis_at - 1))

    factor_of = one(*split[0])
    for cut in split[1:]:
        factor_of = factor_of * one(*cut)
    return factor_of


def centred(own_key, extent, deviation, most, pieces=(), kind=jnp.bfloat16):
    result = jax.random.normal(own_key, extent, jnp.float32) * deviation
    if len(pieces) > 0:
        result = block_scale(own_key, extent, pieces, -0.22, 0.18) * result
    return jnp.clip(result, min=-most, max=most).astype(kind)


def setup_inputs(seed: int = 0) -> dict:
    splits = jax.random.split(jax.random.key(seed), 12)
    image = centred(splits[0], (C, HEIGHT, WIDTH), 1.0, 6.0, ((1, 128), (2, 4)))
    cotangent = centred(splits[1], (C, HEIGHT, WIDTH), 1.0, 6.0, ((1, 128), (2, 4)))
    kernel = centred(splits[2], (C, KSIZE, KSIZE), (KSIZE * KSIZE) ** -0.5, 0.875, (), jnp.float32)
    dw_bias = jnp.clip(jax.random.uniform(splits[3], (C,), jnp.float32, -0.5, 0.5), -0.5, 0.5)
    layer_norm_gain = jnp.clip(jax.random.uniform(splits[4], (C,), jnp.float32, 0.5, 1.5), 0.5, 1.5)
    layer_norm_bias = centred(splits[5], (C,), 0.5, 3.0, (), jnp.float32)
    w_expand = centred(splits[6], (HID, C), C ** -0.5, 0.625)
    b_expand = centred(splits[7], (HID,), 0.5, 3.0)
    w_reduce = centred(splits[8], (HID, C), HID ** -0.5, 0.3125)
    b_reduce = centred(splits[9], (C,), 0.5, 3.0, (), jnp.float32)
    layer_scale = jnp.clip(jnp.exp(jax.random.uniform(splits[10], (C,), jnp.float32, math.log(0.2), math.log(1.0))), 0.2, 1.0)
    return {"image": image, "cotangent": cotangent, "kernel": kernel, "dw_bias": dw_bias, "layer_norm_gain": layer_norm_gain, "layer_norm_bias": layer_norm_bias, "w_expand": w_expand, "b_expand": b_expand, "w_reduce": w_reduce, "b_reduce": b_reduce, "layer_scale": layer_scale}


def depthwise(padded, kernel, row_count, col_count):
    total = jnp.zeros((padded.shape[0], row_count, col_count), jnp.float32)
    for shift_row in range(7):
        for shift_col in range(7):
            piece = padded[:, shift_row:shift_row + row_count, shift_col:shift_col + col_count].astype(jnp.float32)
            total = total + kernel[:, shift_row, shift_col][:, None, None] * piece
    return total

def conv_back(padded, kernel, row_count, col_count):
    total = jnp.zeros((padded.shape[0], row_count, col_count), jnp.float32)
    for shift_row in range(7):
        for shift_col in range(7):
            piece = padded[:, 6 - shift_row:6 - shift_row + row_count, 6 - shift_col:6 - shift_col + col_count].astype(jnp.float32)
            total = total + kernel[:, shift_row, shift_col][:, None, None] * piece
    return total

def kernel_terms(padded, convolution_gradient, row_count, col_count):
    lines = []
    for shift_row in range(7):
        entries = []
        for shift_col in range(7):
            piece = padded[:, shift_row:shift_row + row_count, shift_col:shift_col + col_count].astype(jnp.float32)
            entries.append(lax.optimization_barrier(jnp.sum(piece * convolution_gradient, axis=(1, 2))))
        lines.append(jnp.stack(entries, axis=1))
    return jnp.stack(lines, axis=1)

def gelu_exact(value):
    return value * (1.0 + jax.scipy.special.erf(value / math.sqrt(2.0))) * 0.5

def gelu_slope(value):
    return (1.0 + jax.scipy.special.erf(value / math.sqrt(2.0))) * 0.5 + value * jnp.exp(-0.5 * value * value) / math.sqrt(2.0 * math.pi)

def local_pass(padded, incoming, kernel, dw_bias, layer_norm_gain, layer_norm_bias, w_expand, b_expand, w_reduce, b_reduce, layer_scale):
    channels = incoming.shape[0]
    row_count = incoming.shape[1]
    col_count = incoming.shape[2]
    tok_count = row_count * col_count
    conv = depthwise(padded, kernel, row_count, col_count) + dw_bias[:, None, None]
    flat = conv.reshape(channels, tok_count)
    average = lax.optimization_barrier(jnp.mean(flat, axis=0, keepdims=True))
    mean_removed = flat - average
    inverse_deviation = lax.rsqrt(lax.optimization_barrier(jnp.mean(mean_removed * mean_removed, axis=0, keepdims=True)) + 1e-06)
    standardized_input = mean_removed * inverse_deviation
    normalized_input = (standardized_input * layer_norm_gain[:, None] + layer_norm_bias[:, None]).astype(jnp.bfloat16)
    hidden = jnp.dot(w_expand, normalized_input, preferred_element_type=jnp.float32) + b_expand.astype(jnp.float32)[:, None]
    active = gelu_exact(hidden).astype(jnp.bfloat16)
    branch = lax.dot_general(w_reduce, active, (((0,), (0,)), ((), ())), preferred_element_type=jnp.float32) + b_reduce[:, None]
    resid = padded[:, 3:3 + row_count, 3:3 + col_count].reshape(channels, tok_count).astype(jnp.float32)
    output = (resid + layer_scale[:, None] * branch).astype(jnp.bfloat16).reshape(channels, row_count, col_count)
    cot_flat = incoming.reshape(channels, tok_count).astype(jnp.float32)
    scaled = layer_scale[:, None] * cot_flat
    g_scale = lax.optimization_barrier(jnp.sum(cot_flat * branch, axis=1))
    g_rbias = lax.optimization_barrier(jnp.sum(scaled, axis=1))
    d_branch = scaled.astype(jnp.bfloat16)
    g_reduce = lax.dot_general(active, d_branch, (((1,), (1,)), ((), ())), preferred_element_type=jnp.float32)
    d_active = jnp.dot(w_reduce, d_branch, preferred_element_type=jnp.float32)
    d_hidden = (d_active * gelu_slope(hidden)).astype(jnp.bfloat16)
    g_ebias = lax.optimization_barrier(jnp.sum(d_hidden.astype(jnp.float32), axis=1))
    g_expand = lax.dot_general(d_hidden, normalized_input, (((1,), (1,)), ((), ())), preferred_element_type=jnp.float32)
    normalized_gradient = lax.dot_general(w_expand, d_hidden, (((0,), (0,)), ((), ())), preferred_element_type=jnp.float32)
    norm_gain_gradient = lax.optimization_barrier(jnp.sum(normalized_gradient * standardized_input, axis=1))
    g_lbias = lax.optimization_barrier(jnp.sum(normalized_gradient, axis=1))
    standardized_gradient = normalized_gradient * layer_norm_gain[:, None]
    convolution_gradient = inverse_deviation * (standardized_gradient - lax.optimization_barrier(jnp.mean(standardized_gradient, axis=0, keepdims=True)) - standardized_input * lax.optimization_barrier(jnp.mean(standardized_gradient * standardized_input, axis=0, keepdims=True)))
    convolution_gradient = convolution_gradient.astype(jnp.bfloat16).reshape(channels, row_count, col_count)
    g_dbias = lax.optimization_barrier(jnp.sum(convolution_gradient.astype(jnp.float32), axis=(1, 2)))
    return (output, convolution_gradient, (g_scale, g_rbias, g_reduce, g_ebias, g_expand, norm_gain_gradient, g_lbias, g_dbias))

def reference(image, cotangent, kernel, dw_bias, layer_norm_gain, layer_norm_bias, w_expand, b_expand, w_reduce, b_reduce, layer_scale):
    block = math.gcd(HEIGHT, 32)
    count = HEIGHT // block
    padded_image = jnp.pad(image, ((0, 0), (3, 3), (3, 3)))
    zeros_c = jnp.zeros((C,), jnp.float32)
    zeros_h = jnp.zeros((HID,), jnp.float32)
    zeros_w = jnp.zeros((HID, C), jnp.float32)
    init = (zeros_c, zeros_c, zeros_w, zeros_h, zeros_w, zeros_c, zeros_c, zeros_c)

    def first(carry, index):
        start = (index * block).astype(jnp.int32)
        xblock = lax.dynamic_slice_in_dim(padded_image, start, block + 6, 1)
        cblock = lax.dynamic_slice_in_dim(cotangent, start, block, 1)
        output, convolution_gradient, terms = local_pass(xblock, cblock, kernel, dw_bias, layer_norm_gain, layer_norm_bias, w_expand, b_expand, w_reduce, b_reduce, layer_scale)
        carry = jax.tree.map(lambda left, right: left + right, carry, terms)
        return (carry, (output, convolution_gradient))
    indices = jnp.arange(count, dtype=jnp.int32)
    sums, stacked = lax.scan(first, init, indices)
    output = jnp.transpose(stacked[0], (1, 0, 2, 3)).reshape(C, HEIGHT, WIDTH)
    convolution_gradient = jnp.transpose(stacked[1], (1, 0, 2, 3)).reshape(C, HEIGHT, WIDTH)
    padded_grad = jnp.pad(convolution_gradient, ((0, 0), (3, 3), (3, 3)))

    def second(carry, index):
        start = (index * block).astype(jnp.int32)
        xblock = lax.dynamic_slice_in_dim(padded_image, start, block + 6, 1)
        gblock = lax.dynamic_slice_in_dim(padded_grad, start, block + 6, 1)
        dblock = lax.dynamic_slice_in_dim(convolution_gradient, start, block, 1).astype(jnp.float32)
        cblock = lax.dynamic_slice_in_dim(cotangent, start, block, 1).astype(jnp.float32)
        grad_block = (cblock + conv_back(gblock, kernel, block, WIDTH)).astype(jnp.bfloat16)
        carry = carry + kernel_terms(xblock, dblock, block, WIDTH)
        return (carry, grad_block)
    kernel_sum, grad_blocks = lax.scan(second, jnp.zeros((C, 7, 7), jnp.float32), indices)
    image_grad = jnp.transpose(grad_blocks, (1, 0, 2, 3)).reshape(C, HEIGHT, WIDTH)
    factor = 1.0 / math.sqrt(TOKENS)
    g_scale, g_rbias, g_reduce, g_ebias, g_expand, norm_gain_gradient, g_lbias, g_dbias = sums
    return (output, image_grad, kernel_sum * factor, g_dbias * factor, norm_gain_gradient * factor, g_lbias * factor, g_expand * factor, g_ebias * factor, g_reduce * factor, g_rbias * factor, g_scale * factor)
```

```python
import math

import jax
import jax.numpy as jnp
from jax import lax
from jax.sharding import PartitionSpec as P


def padded_2(x, sides, width):
    for axis, dim in sides:
        size, length = (lax.axis_size(axis), x.shape[dim])
        up = [(i, (i + 1) % size) for i in range(size - 1)]
        down = [(j, i) for i, j in up]
        last = lax.slice_in_dim(x, length - width, length, axis=dim)
        initial = lax.slice_in_dim(x, 0, width, axis=dim)
        before = lax.ppermute(last, axis, up)
        after = lax.ppermute(initial, axis, down)
        x = jnp.concatenate([before, x, after], axis=dim)
    return x


def depthwise(padded, kernel, row_count, col_count):
    total = jnp.zeros((padded.shape[0], row_count, col_count), jnp.float32)
    for shift_row in range(7):
        for shift_col in range(7):
            piece = padded[
                :, shift_row : shift_row + row_count, shift_col : shift_col + col_count
            ].astype(jnp.float32)
            total = total + kernel[:, shift_row, shift_col][:, None, None] * piece
    return total


def conv_back(padded, kernel, row_count, col_count):
    total = jnp.zeros((padded.shape[0], row_count, col_count), jnp.float32)
    for shift_row in range(7):
        for shift_col in range(7):
            piece = padded[
                :,
                6 - shift_row : 6 - shift_row + row_count,
                6 - shift_col : 6 - shift_col + col_count,
            ].astype(jnp.float32)
            total = total + kernel[:, shift_row, shift_col][:, None, None] * piece
    return total


def kernel_terms(padded, convolution_gradient, row_count, col_count):
    lines = []
    for shift_row in range(7):
        entries = []
        for shift_col in range(7):
            piece = padded[
                :, shift_row : shift_row + row_count, shift_col : shift_col + col_count
            ].astype(jnp.float32)
            entries.append(jnp.sum(piece * convolution_gradient, axis=(1, 2)))
        lines.append(jnp.stack(entries, axis=1))
    return jnp.stack(lines, axis=1)


def gelu_exact(value):
    return value * (1.0 + jax.scipy.special.erf(value / math.sqrt(2.0))) * 0.5


def gelu_slope(value):
    return (1.0 + jax.scipy.special.erf(value / math.sqrt(2.0))) * 0.5 + value * jnp.exp(
        -0.5 * value * value
    ) / math.sqrt(2.0 * math.pi)


def shards(
    image,
    cotangent,
    kernel,
    dw_bias,
    layer_norm_gain,
    layer_norm_bias,
    w_expand,
    b_expand,
    w_reduce,
    b_reduce,
    layer_scale,
):
    channels, row_count, col_count = image.shape
    panel_rows = w_expand.shape[0] // lax.axis_size("filt")
    tok_count = row_count * col_count
    padded = padded_2(image, (("space", 1), ("filt", 2)), 3)
    conv = depthwise(padded, kernel, row_count, col_count)
    conv = conv + dw_bias[:, None, None]
    flat = conv.reshape(channels, tok_count)
    average = jnp.mean(flat, axis=0, keepdims=True)
    mean_removed = flat - average
    inverse_deviation = lax.rsqrt(
        jnp.mean(mean_removed * mean_removed, axis=0, keepdims=True) + 1e-06
    )
    standardized_input = mean_removed * inverse_deviation
    normalized_input = (
        standardized_input * layer_norm_gain[:, None] + layer_norm_bias[:, None]
    ).astype(jnp.bfloat16)
    hidden = (
        jnp.dot(w_expand, normalized_input, preferred_element_type=jnp.float32)
        + b_expand.astype(jnp.float32)[:, None]
    )
    active = gelu_exact(hidden).astype(jnp.bfloat16)
    branch = (
        lax.dot_general(
            w_reduce, active, (((0,), (0,)), ((), ())), preferred_element_type=jnp.float32
        )
        + b_reduce[:, None]
    )
    resid = image.reshape(channels, tok_count).astype(jnp.float32)
    output = (
        (resid + layer_scale[:, None] * branch)
        .astype(jnp.bfloat16)
        .reshape(channels, row_count, col_count)
    )
    cot_flat = cotangent.reshape(channels, tok_count).astype(jnp.float32)
    scaled = layer_scale[:, None] * cot_flat
    g_scale = jnp.sum(cot_flat * branch, axis=1)
    g_rbias = jnp.sum(scaled, axis=1)
    d_branch = scaled.astype(jnp.bfloat16)
    g_reduce = lax.dot_general(
        active, d_branch, (((1,), (1,)), ((), ())), preferred_element_type=jnp.float32
    )
    d_active = jnp.dot(w_reduce, d_branch, preferred_element_type=jnp.float32)
    d_hidden = (d_active * gelu_slope(hidden)).astype(jnp.bfloat16)
    g_ebias = jnp.sum(d_hidden.astype(jnp.float32), axis=1)
    g_expand = lax.dot_general(
        d_hidden, normalized_input, (((1,), (1,)), ((), ())), preferred_element_type=jnp.float32
    )
    normalized_gradient = lax.dot_general(
        w_expand, d_hidden, (((0,), (0,)), ((), ())), preferred_element_type=jnp.float32
    )
    norm_gain_gradient = jnp.sum(normalized_gradient * standardized_input, axis=1)
    g_lbias = jnp.sum(normalized_gradient, axis=1)
    standardized_gradient = normalized_gradient * layer_norm_gain[:, None]
    convolution_gradient = inverse_deviation * (
        standardized_gradient
        - jnp.mean(standardized_gradient, axis=0, keepdims=True)
        - standardized_input
        * jnp.mean(standardized_gradient * standardized_input, axis=0, keepdims=True)
    )
    convolution_gradient = convolution_gradient.astype(jnp.bfloat16).reshape(
        channels, row_count, col_count
    )
    d_float = convolution_gradient.astype(jnp.float32)
    g_dbias = jnp.sum(d_float, axis=(1, 2))
    padded_grad = padded_2(convolution_gradient, (("space", 1), ("filt", 2)), 3)
    back = conv_back(padded_grad, kernel, row_count, col_count)
    image_grad = (cotangent.astype(jnp.float32) + back).astype(jnp.bfloat16)
    g_kernel = kernel_terms(padded, d_float, row_count, col_count)
    factor = 1.0 / math.sqrt(tok_count * lax.axis_size("space") * lax.axis_size("filt"))
    parts = lax.axis_size("filt")
    panels = jnp.concatenate(
        [
            g_reduce.reshape(parts, panel_rows * channels),
            g_expand.reshape(parts, panel_rows * channels),
            g_ebias.reshape(parts, panel_rows),
        ],
        axis=1,
    )
    small = jnp.concatenate(
        [
            g_kernel.reshape(-1),
            g_dbias,
            norm_gain_gradient,
            g_lbias,
            g_scale,
            g_rbias,
        ]
    )
    panel, small = filt_reduce(panels, small)
    total = space_butterfly(jnp.concatenate([panel, small]))
    total = total * factor
    cut = [panel_rows * channels, panel_rows * channels, panel_rows]
    g_reduce = total[: cut[0]].reshape(panel_rows, channels)
    g_expand = total[cut[0] : cut[0] + cut[1]].reshape(panel_rows, channels)
    g_ebias = total[cut[0] + cut[1] : sum(cut)]
    rest = total[sum(cut) :]
    ksq = kernel.shape[1] * kernel.shape[2]
    g_kernel = rest[: channels * ksq].reshape(kernel.shape)
    g_dbias, norm_gain_gradient, g_lbias, g_scale, g_rbias = (
        rest[channels * ksq + channels * i : channels * ksq + channels * (i + 1)]
        for i in range(5)
    )
    return (
        output,
        image_grad,
        g_kernel,
        g_dbias,
        norm_gain_gradient,
        g_lbias,
        g_expand,
        g_ebias,
        g_reduce,
        g_rbias,
        g_scale,
    )


def filt_reduce(panels, small):
    parts = lax.axis_size("filt")
    me = lax.axis_index("filt")
    width = panels.shape[1]
    count = parts
    bit = parts // 2
    held = panels
    while bit >= 1:
        half = count // 2
        upper = (me // bit) % 2
        mine = lax.dynamic_slice_in_dim(held, upper * half, half, 0)
        other = lax.dynamic_slice_in_dim(held, (1 - upper) * half, half, 0)
        send = jnp.concatenate([other.reshape(-1), small])
        got = lax.ppermute(send, "filt", [(i, i ^ bit) for i in range(parts)])
        held = mine + got[: half * width].reshape(half, width)
        small = small + got[half * width :]
        count = half
        bit //= 2
    return held.reshape(-1), small


def space_butterfly(buf):
    size = lax.axis_size("space")
    bit = 1
    while bit < size:
        buf = buf + lax.ppermute(buf, "space", [(i, i ^ bit) for i in range(size)])
        bit *= 2
    return buf


def solution(mesh):
    in_specs = (
        P(None, "space", "filt"),
        P(None, "space", "filt"),
        P(),
        P(),
        P(),
        P(),
        P(),
        P(),
        P(),
        P(),
        P(),
    )
    out_specs = (
        P(None, "space", "filt"),
        P(None, "space", "filt"),
        P(),
        P(),
        P(),
        P(),
        P("filt", None),
        P("filt"),
        P("filt", None),
        P(),
        P(),
    )
    return jax.shard_map(shards, mesh=mesh, in_specs=in_specs, out_specs=out_specs, check_vma=False)
```

```python
import functools
import math

import jax
import jax.numpy as jnp
from jax import lax
from jax.experimental import pallas as pl
from jax.experimental.pallas import tpu as pltpu
from jax.sharding import PartitionSpec as P

MESH = pl.DeviceIdType.MESH
LANES = 128


def padded_2(x, sides, width):
    for axis, dim in sides:
        size, length = (lax.axis_size(axis), x.shape[dim])
        up = [(i, (i + 1) % size) for i in range(size - 1)]
        down = [(j, i) for i, j in up]
        last = lax.slice_in_dim(x, length - width, length, axis=dim)
        initial = lax.slice_in_dim(x, 0, width, axis=dim)
        before = lax.ppermute(last, axis, up)
        after = lax.ppermute(initial, axis, down)
        x = jnp.concatenate([before, x, after], axis=dim)
    return x


def depthwise(padded, kernel, row_count, col_count):
    total = jnp.zeros((padded.shape[0], row_count, col_count), jnp.float32)
    for shift_row in range(7):
        for shift_col in range(7):
            piece = padded[
                :, shift_row : shift_row + row_count, shift_col : shift_col + col_count
            ].astype(jnp.float32)
            total = total + kernel[:, shift_row, shift_col][:, None, None] * piece
    return total


def conv_back(padded, kernel, row_count, col_count):
    total = jnp.zeros((padded.shape[0], row_count, col_count), jnp.float32)
    for shift_row in range(7):
        for shift_col in range(7):
            piece = padded[
                :,
                6 - shift_row : 6 - shift_row + row_count,
                6 - shift_col : 6 - shift_col + col_count,
            ].astype(jnp.float32)
            total = total + kernel[:, shift_row, shift_col][:, None, None] * piece
    return total


def kernel_terms(padded, convolution_gradient, row_count, col_count):
    lines = []
    for shift_row in range(7):
        entries = []
        for shift_col in range(7):
            piece = padded[
                :, shift_row : shift_row + row_count, shift_col : shift_col + col_count
            ].astype(jnp.float32)
            entries.append(jnp.sum(piece * convolution_gradient, axis=(1, 2)))
        lines.append(jnp.stack(entries, axis=1))
    return jnp.stack(lines, axis=1)


def gelu_exact(value):
    return value * (1.0 + jax.scipy.special.erf(value / math.sqrt(2.0))) * 0.5


def gelu_slope(value):
    return (1.0 + jax.scipy.special.erf(value / math.sqrt(2.0))) * 0.5 + value * jnp.exp(
        -0.5 * value * value
    ) / math.sqrt(2.0 * math.pi)


def shards(
    image,
    cotangent,
    kernel,
    dw_bias,
    layer_norm_gain,
    layer_norm_bias,
    w_expand,
    b_expand,
    w_reduce,
    b_reduce,
    layer_scale,
):
    channels, row_count, col_count = image.shape
    panel_rows = w_expand.shape[0] // lax.axis_size("filt")
    tok_count = row_count * col_count
    padded = padded_2(image, (("space", 1), ("filt", 2)), 3)
    conv = depthwise(padded, kernel, row_count, col_count)
    conv = conv + dw_bias[:, None, None]
    flat = conv.reshape(channels, tok_count)
    average = jnp.mean(flat, axis=0, keepdims=True)
    mean_removed = flat - average
    inverse_deviation = lax.rsqrt(
        jnp.mean(mean_removed * mean_removed, axis=0, keepdims=True) + 1e-06
    )
    standardized_input = mean_removed * inverse_deviation
    normalized_input = (
        standardized_input * layer_norm_gain[:, None] + layer_norm_bias[:, None]
    ).astype(jnp.bfloat16)
    hidden = (
        jnp.dot(w_expand, normalized_input, preferred_element_type=jnp.float32)
        + b_expand.astype(jnp.float32)[:, None]
    )
    active = gelu_exact(hidden).astype(jnp.bfloat16)
    branch = (
        lax.dot_general(
            w_reduce, active, (((0,), (0,)), ((), ())), preferred_element_type=jnp.float32
        )
        + b_reduce[:, None]
    )
    resid = image.reshape(channels, tok_count).astype(jnp.float32)
    output = (
        (resid + layer_scale[:, None] * branch)
        .astype(jnp.bfloat16)
        .reshape(channels, row_count, col_count)
    )
    cot_flat = cotangent.reshape(channels, tok_count).astype(jnp.float32)
    scaled = layer_scale[:, None] * cot_flat
    g_scale = jnp.sum(cot_flat * branch, axis=1)
    g_rbias = jnp.sum(scaled, axis=1)
    d_branch = scaled.astype(jnp.bfloat16)
    g_reduce = lax.dot_general(
        active, d_branch, (((1,), (1,)), ((), ())), preferred_element_type=jnp.float32
    )
    d_active = jnp.dot(w_reduce, d_branch, preferred_element_type=jnp.float32)
    d_hidden = (d_active * gelu_slope(hidden)).astype(jnp.bfloat16)
    g_ebias = jnp.sum(d_hidden.astype(jnp.float32), axis=1)
    g_expand = lax.dot_general(
        d_hidden, normalized_input, (((1,), (1,)), ((), ())), preferred_element_type=jnp.float32
    )
    normalized_gradient = lax.dot_general(
        w_expand, d_hidden, (((0,), (0,)), ((), ())), preferred_element_type=jnp.float32
    )
    norm_gain_gradient = jnp.sum(normalized_gradient * standardized_input, axis=1)
    g_lbias = jnp.sum(normalized_gradient, axis=1)
    standardized_gradient = normalized_gradient * layer_norm_gain[:, None]
    convolution_gradient = inverse_deviation * (
        standardized_gradient
        - jnp.mean(standardized_gradient, axis=0, keepdims=True)
        - standardized_input
        * jnp.mean(standardized_gradient * standardized_input, axis=0, keepdims=True)
    )
    convolution_gradient = convolution_gradient.astype(jnp.bfloat16).reshape(
        channels, row_count, col_count
    )
    d_float = convolution_gradient.astype(jnp.float32)
    g_dbias = jnp.sum(d_float, axis=(1, 2))
    padded_grad = padded_2(convolution_gradient, (("space", 1), ("filt", 2)), 3)
    back = conv_back(padded_grad, kernel, row_count, col_count)
    image_grad = (cotangent.astype(jnp.float32) + back).astype(jnp.bfloat16)
    g_kernel = kernel_terms(padded, d_float, row_count, col_count)
    factor = 1.0 / math.sqrt(tok_count * lax.axis_size("space") * lax.axis_size("filt"))
    parts = lax.axis_size("filt")
    panels = jnp.concatenate(
        [
            g_reduce.reshape(parts, panel_rows * channels),
            g_expand.reshape(parts, panel_rows * channels),
            g_ebias.reshape(parts, panel_rows),
        ],
        axis=1,
    )
    small = jnp.concatenate(
        [
            g_kernel.reshape(-1),
            g_dbias,
            norm_gain_gradient,
            g_lbias,
            g_scale,
            g_rbias,
        ]
    )
    panel, small = grad_reduce(panels, small)
    total = jnp.concatenate([panel, small])
    total = total * factor
    cut = [panel_rows * channels, panel_rows * channels, panel_rows]
    g_reduce = total[: cut[0]].reshape(panel_rows, channels)
    g_expand = total[cut[0] : cut[0] + cut[1]].reshape(panel_rows, channels)
    g_ebias = total[cut[0] + cut[1] : sum(cut)]
    rest = total[sum(cut) :]
    ksq = kernel.shape[1] * kernel.shape[2]
    g_kernel = rest[: channels * ksq].reshape(kernel.shape)
    g_dbias, norm_gain_gradient, g_lbias, g_scale, g_rbias = (
        rest[channels * ksq + channels * i : channels * ksq + channels * (i + 1)]
        for i in range(5)
    )
    return (
        output,
        image_grad,
        g_kernel,
        g_dbias,
        norm_gain_gradient,
        g_lbias,
        g_expand,
        g_ebias,
        g_reduce,
        g_rbias,
        g_scale,
    )


def _rows(length):
    return -(-length // (8 * LANES)) * 8


def _flip(index, bit):
    return index + bit - 2 * bit * ((index // bit) % 2)


def reduce_kernel(nfilt, nspace, pr, sr, buf_ref, out_ref, *scratch):
    levels = nfilt.bit_length() - 1
    steps = nspace.bit_length() - 1
    recvs = scratch[:levels]
    stages = scratch[levels : 2 * levels]
    recv_s, send_sem, recv_sem = scratch[2 * levels :]
    s = lax.axis_index("space")
    f = lax.axis_index("filt")

    peers = []
    bit = nfilt // 2
    while bit >= 1:
        peers.append((s, _flip(f, bit)))
        bit //= 2
    for k in range(steps):
        peers.append((_flip(s, 1 << k), f))
    barrier = pltpu.get_barrier_semaphore()
    for peer in peers:
        pl.semaphore_signal(barrier, inc=1, device_id=peer, device_id_type=MESH)
    pl.semaphore_wait(barrier, len(peers))

    held = buf_ref
    count = nfilt
    bit = nfilt // 2
    sem = 0
    for level in range(levels):
        half = count // 2
        upper = (f // bit) % 2
        rows = half * pr
        peer = peers[level]
        send_panels = pltpu.make_async_remote_copy(
            src_ref=held.at[pl.ds(pl.multiple_of((1 - upper) * rows, 8), rows)],
            dst_ref=recvs[level].at[pl.ds(0, rows)],
            send_sem=send_sem.at[sem],
            recv_sem=recv_sem.at[sem],
            device_id=peer,
            device_id_type=MESH,
        )
        send_small = pltpu.make_async_remote_copy(
            src_ref=held.at[pl.ds(count * pr, sr)],
            dst_ref=recvs[level].at[pl.ds(rows, sr)],
            send_sem=send_sem.at[sem + 1],
            recv_sem=recv_sem.at[sem + 1],
            device_id=peer,
            device_id_type=MESH,
        )
        send_panels.start()
        send_small.start()
        send_panels.wait()
        send_small.wait()
        sem += 2
        stage = stages[level]
        stage[pl.ds(0, rows)] = (
            held[pl.ds(pl.multiple_of(upper * rows, 8), rows)] + recvs[level][pl.ds(0, rows)]
        )
        stage[pl.ds(rows, sr)] = held[pl.ds(count * pr, sr)] + recvs[level][pl.ds(rows, sr)]
        held = stage
        count = half
        bit //= 2

    if levels == 0:
        out_ref[...] = buf_ref[...]
    else:
        out_ref[...] = held[...]
    for k in range(steps):
        copy = pltpu.make_async_remote_copy(
            src_ref=out_ref,
            dst_ref=recv_s.at[k],
            send_sem=send_sem.at[sem],
            recv_sem=recv_sem.at[sem],
            device_id=peers[levels + k],
            device_id_type=MESH,
        )
        copy.start()
        copy.wait()
        sem += 1
        out_ref[...] = out_ref[...] + recv_s[k]


def grad_reduce(panels, small):
    nfilt = lax.axis_size("filt")
    nspace = lax.axis_size("space")
    width = panels.shape[1]
    pr = _rows(width)
    sr = _rows(small.shape[0])
    buf = jnp.concatenate(
        [
            jnp.pad(panels, ((0, 0), (0, pr * LANES - width))).reshape(nfilt * pr, LANES),
            jnp.pad(small, (0, sr * LANES - small.shape[0])).reshape(sr, LANES),
        ]
    )
    levels = nfilt.bit_length() - 1
    steps = nspace.bit_length() - 1
    scratch = []
    count = nfilt
    for _ in range(levels):
        count //= 2
        scratch.append(pltpu.VMEM((count * pr + sr, LANES), jnp.float32))
    count = nfilt
    for _ in range(levels):
        count //= 2
        scratch.append(pltpu.VMEM((count * pr + sr, LANES), jnp.float32))
    ncopies = 2 * levels + steps
    scratch += [
        pltpu.VMEM((max(steps, 1), pr + sr, LANES), jnp.float32),
        pltpu.SemaphoreType.DMA((ncopies,)),
        pltpu.SemaphoreType.DMA((ncopies,)),
    ]
    out = pl.pallas_call(
        functools.partial(reduce_kernel, nfilt, nspace, pr, sr),
        out_shape=jax.ShapeDtypeStruct((pr + sr, LANES), jnp.float32),
        in_specs=[pl.BlockSpec(memory_space=pltpu.VMEM)],
        out_specs=pl.BlockSpec(memory_space=pltpu.VMEM),
        scratch_shapes=scratch,
        compiler_params=pltpu.CompilerParams(collective_id=0, has_side_effects=True),
    )(buf)
    panel = out[:pr].reshape(-1)[:width]
    small = out[pr:].reshape(-1)[: small.shape[0]]
    return panel, small


def solution(mesh):
    in_specs = (
        P(None, "space", "filt"),
        P(None, "space", "filt"),
        P(),
        P(),
        P(),
        P(),
        P(),
        P(),
        P(),
        P(),
        P(),
    )
    out_specs = (
        P(None, "space", "filt"),
        P(None, "space", "filt"),
        P(),
        P(),
        P(),
        P(),
        P("filt", None),
        P("filt"),
        P("filt", None),
        P(),
        P(),
    )
    return jax.shard_map(shards, mesh=mesh, in_specs=in_specs, out_specs=out_specs, check_vma=False)
```

```python
import functools
import math

import jax
import jax.numpy as jnp
from jax import lax
from jax.experimental import pallas as pl
from jax.experimental.pallas import tpu as pltpu
from jax.sharding import PartitionSpec as P

MESH = pl.DeviceIdType.MESH
LANES = 128


def padded_2(x, sides, width):
    for axis, dim in sides:
        size, length = (lax.axis_size(axis), x.shape[dim])
        up = [(i, (i + 1) % size) for i in range(size - 1)]
        down = [(j, i) for i, j in up]
        last = lax.slice_in_dim(x, length - width, length, axis=dim)
        initial = lax.slice_in_dim(x, 0, width, axis=dim)
        before = lax.ppermute(last, axis, up)
        after = lax.ppermute(initial, axis, down)
        x = jnp.concatenate([before, x, after], axis=dim)
    return x


def depthwise(padded, kernel, row_count, col_count):
    total = jnp.zeros((padded.shape[0], row_count, col_count), jnp.float32)
    for shift_row in range(7):
        for shift_col in range(7):
            piece = padded[
                :, shift_row : shift_row + row_count, shift_col : shift_col + col_count
            ].astype(jnp.float32)
            total = total + kernel[:, shift_row, shift_col][:, None, None] * piece
    return total


def conv_back(padded, kernel, row_count, col_count):
    total = jnp.zeros((padded.shape[0], row_count, col_count), jnp.float32)
    for shift_row in range(7):
        for shift_col in range(7):
            piece = padded[
                :,
                6 - shift_row : 6 - shift_row + row_count,
                6 - shift_col : 6 - shift_col + col_count,
            ].astype(jnp.float32)
            total = total + kernel[:, shift_row, shift_col][:, None, None] * piece
    return total


def kernel_terms(padded, convolution_gradient, row_count, col_count):
    lines = []
    for shift_row in range(7):
        entries = []
        for shift_col in range(7):
            piece = padded[
                :, shift_row : shift_row + row_count, shift_col : shift_col + col_count
            ].astype(jnp.float32)
            entries.append(jnp.sum(piece * convolution_gradient, axis=(1, 2)))
        lines.append(jnp.stack(entries, axis=1))
    return jnp.stack(lines, axis=1)


def gelu_exact(value):
    return value * (1.0 + jax.scipy.special.erf(value / math.sqrt(2.0))) * 0.5


def gelu_slope(value):
    return (1.0 + jax.scipy.special.erf(value / math.sqrt(2.0))) * 0.5 + value * jnp.exp(
        -0.5 * value * value
    ) / math.sqrt(2.0 * math.pi)


def shards(
    image,
    cotangent,
    kernel,
    dw_bias,
    layer_norm_gain,
    layer_norm_bias,
    w_expand,
    b_expand,
    w_reduce,
    b_reduce,
    layer_scale,
):
    channels, row_count, col_count = image.shape
    panel_rows = w_expand.shape[0] // lax.axis_size("filt")
    tok_count = row_count * col_count
    padded = padded_2(image, (("space", 1), ("filt", 2)), 3)
    conv = depthwise(padded, kernel, row_count, col_count)
    conv = conv + dw_bias[:, None, None]
    flat = conv.reshape(channels, tok_count)
    average = jnp.mean(flat, axis=0, keepdims=True)
    mean_removed = flat - average
    inverse_deviation = lax.rsqrt(
        jnp.mean(mean_removed * mean_removed, axis=0, keepdims=True) + 1e-06
    )
    standardized_input = mean_removed * inverse_deviation
    normalized_input = (
        standardized_input * layer_norm_gain[:, None] + layer_norm_bias[:, None]
    ).astype(jnp.bfloat16)
    hidden = (
        jnp.dot(w_expand, normalized_input, preferred_element_type=jnp.float32)
        + b_expand.astype(jnp.float32)[:, None]
    )
    active = gelu_exact(hidden).astype(jnp.bfloat16)
    branch = (
        lax.dot_general(
            w_reduce, active, (((0,), (0,)), ((), ())), preferred_element_type=jnp.float32
        )
        + b_reduce[:, None]
    )
    resid = image.reshape(channels, tok_count).astype(jnp.float32)
    output = (
        (resid + layer_scale[:, None] * branch)
        .astype(jnp.bfloat16)
        .reshape(channels, row_count, col_count)
    )
    cot_flat = cotangent.reshape(channels, tok_count).astype(jnp.float32)
    scaled = layer_scale[:, None] * cot_flat
    g_scale = jnp.sum(cot_flat * branch, axis=1)
    g_rbias = jnp.sum(scaled, axis=1)
    d_branch = scaled.astype(jnp.bfloat16)
    g_reduce = lax.dot_general(
        active, d_branch, (((1,), (1,)), ((), ())), preferred_element_type=jnp.float32
    )
    d_active = jnp.dot(w_reduce, d_branch, preferred_element_type=jnp.float32)
    d_hidden = (d_active * gelu_slope(hidden)).astype(jnp.bfloat16)
    g_ebias = jnp.sum(d_hidden.astype(jnp.float32), axis=1)
    g_expand = lax.dot_general(
        d_hidden, normalized_input, (((1,), (1,)), ((), ())), preferred_element_type=jnp.float32
    )
    normalized_gradient = lax.dot_general(
        w_expand, d_hidden, (((0,), (0,)), ((), ())), preferred_element_type=jnp.float32
    )
    norm_gain_gradient = jnp.sum(normalized_gradient * standardized_input, axis=1)
    g_lbias = jnp.sum(normalized_gradient, axis=1)
    standardized_gradient = normalized_gradient * layer_norm_gain[:, None]
    convolution_gradient = inverse_deviation * (
        standardized_gradient
        - jnp.mean(standardized_gradient, axis=0, keepdims=True)
        - standardized_input
        * jnp.mean(standardized_gradient * standardized_input, axis=0, keepdims=True)
    )
    convolution_gradient = convolution_gradient.astype(jnp.bfloat16).reshape(
        channels, row_count, col_count
    )
    d_float = convolution_gradient.astype(jnp.float32)
    g_dbias = jnp.sum(d_float, axis=(1, 2))
    padded_grad = padded_2(convolution_gradient, (("space", 1), ("filt", 2)), 3)
    g_kernel = kernel_terms(padded, d_float, row_count, col_count)
    factor = 1.0 / math.sqrt(tok_count * lax.axis_size("space") * lax.axis_size("filt"))
    parts = lax.axis_size("filt")
    panels = jnp.concatenate(
        [
            g_reduce.reshape(parts, panel_rows * channels),
            g_expand.reshape(parts, panel_rows * channels),
            g_ebias.reshape(parts, panel_rows),
        ],
        axis=1,
    )
    small = jnp.concatenate(
        [
            g_kernel.reshape(-1),
            g_dbias,
            norm_gain_gradient,
            g_lbias,
            g_scale,
            g_rbias,
        ]
    )
    panels, small, padded_grad = lax.optimization_barrier((panels, small, padded_grad))
    back = conv_back(padded_grad, kernel, row_count, col_count)
    image_grad = (cotangent.astype(jnp.float32) + back).astype(jnp.bfloat16)
    panel, small = grad_reduce(panels, small)
    total = jnp.concatenate([panel, small])
    total = total * factor
    cut = [panel_rows * channels, panel_rows * channels, panel_rows]
    g_reduce = total[: cut[0]].reshape(panel_rows, channels)
    g_expand = total[cut[0] : cut[0] + cut[1]].reshape(panel_rows, channels)
    g_ebias = total[cut[0] + cut[1] : sum(cut)]
    rest = total[sum(cut) :]
    ksq = kernel.shape[1] * kernel.shape[2]
    g_kernel = rest[: channels * ksq].reshape(kernel.shape)
    g_dbias, norm_gain_gradient, g_lbias, g_scale, g_rbias = (
        rest[channels * ksq + channels * i : channels * ksq + channels * (i + 1)]
        for i in range(5)
    )
    return (
        output,
        image_grad,
        g_kernel,
        g_dbias,
        norm_gain_gradient,
        g_lbias,
        g_expand,
        g_ebias,
        g_reduce,
        g_rbias,
        g_scale,
    )


def _rows(length):
    return -(-length // (8 * LANES)) * 8


def _flip(index, bit):
    return index + bit - 2 * bit * ((index // bit) % 2)


def reduce_kernel(nfilt, nspace, pr, sr, buf_ref, out_ref, *scratch):
    levels = nfilt.bit_length() - 1
    steps = nspace.bit_length() - 1
    recvs = scratch[:levels]
    stages = scratch[levels : 2 * levels]
    recv_s, send_sem, recv_sem = scratch[2 * levels :]
    s = lax.axis_index("space")
    f = lax.axis_index("filt")

    peers = []
    bit = nfilt // 2
    while bit >= 1:
        peers.append((s, _flip(f, bit)))
        bit //= 2
    for k in range(steps):
        peers.append((_flip(s, 1 << k), f))
    barrier = pltpu.get_barrier_semaphore()
    for peer in peers:
        pl.semaphore_signal(barrier, inc=1, device_id=peer, device_id_type=MESH)
    pl.semaphore_wait(barrier, len(peers))

    held = buf_ref
    count = nfilt
    bit = nfilt // 2
    sem = 0
    for level in range(levels):
        half = count // 2
        upper = (f // bit) % 2
        rows = half * pr
        peer = peers[level]
        send_panels = pltpu.make_async_remote_copy(
            src_ref=held.at[pl.ds(pl.multiple_of((1 - upper) * rows, 8), rows)],
            dst_ref=recvs[level].at[pl.ds(0, rows)],
            send_sem=send_sem.at[sem],
            recv_sem=recv_sem.at[sem],
            device_id=peer,
            device_id_type=MESH,
        )
        send_small = pltpu.make_async_remote_copy(
            src_ref=held.at[pl.ds(count * pr, sr)],
            dst_ref=recvs[level].at[pl.ds(rows, sr)],
            send_sem=send_sem.at[sem + 1],
            recv_sem=recv_sem.at[sem + 1],
            device_id=peer,
            device_id_type=MESH,
        )
        send_panels.start()
        send_small.start()
        send_panels.wait()
        send_small.wait()
        sem += 2
        stage = stages[level]
        stage[pl.ds(0, rows)] = (
            held[pl.ds(pl.multiple_of(upper * rows, 8), rows)] + recvs[level][pl.ds(0, rows)]
        )
        stage[pl.ds(rows, sr)] = held[pl.ds(count * pr, sr)] + recvs[level][pl.ds(rows, sr)]
        held = stage
        count = half
        bit //= 2

    if levels == 0:
        out_ref[...] = buf_ref[...]
    else:
        out_ref[...] = held[...]
    for k in range(steps):
        copy = pltpu.make_async_remote_copy(
            src_ref=out_ref,
            dst_ref=recv_s.at[k],
            send_sem=send_sem.at[sem],
            recv_sem=recv_sem.at[sem],
            device_id=peers[levels + k],
            device_id_type=MESH,
        )
        copy.start()
        copy.wait()
        sem += 1
        out_ref[...] = out_ref[...] + recv_s[k]


def grad_reduce(panels, small):
    nfilt = lax.axis_size("filt")
    nspace = lax.axis_size("space")
    width = panels.shape[1]
    pr = _rows(width)
    sr = _rows(small.shape[0])
    buf = jnp.concatenate(
        [
            jnp.pad(panels, ((0, 0), (0, pr * LANES - width))).reshape(nfilt * pr, LANES),
            jnp.pad(small, (0, sr * LANES - small.shape[0])).reshape(sr, LANES),
        ]
    )
    levels = nfilt.bit_length() - 1
    steps = nspace.bit_length() - 1
    scratch = []
    count = nfilt
    for _ in range(levels):
        count //= 2
        scratch.append(pltpu.VMEM((count * pr + sr, LANES), jnp.float32))
    count = nfilt
    for _ in range(levels):
        count //= 2
        scratch.append(pltpu.VMEM((count * pr + sr, LANES), jnp.float32))
    ncopies = 2 * levels + steps
    scratch += [
        pltpu.VMEM((max(steps, 1), pr + sr, LANES), jnp.float32),
        pltpu.SemaphoreType.DMA((ncopies,)),
        pltpu.SemaphoreType.DMA((ncopies,)),
    ]
    out = pl.pallas_call(
        functools.partial(reduce_kernel, nfilt, nspace, pr, sr),
        out_shape=jax.ShapeDtypeStruct((pr + sr, LANES), jnp.float32),
        in_specs=[pl.BlockSpec(memory_space=pltpu.VMEM)],
        out_specs=pl.BlockSpec(memory_space=pltpu.VMEM),
        scratch_shapes=scratch,
        compiler_params=pltpu.CompilerParams(collective_id=0, has_side_effects=True),
        cost_estimate=pl.CostEstimate(
            flops=0, transcendentals=0, bytes_accessed=200 * 1024 * 1024
        ),
    )(buf)
    panel = out[:pr].reshape(-1)[:width]
    small = out[pr:].reshape(-1)[: small.shape[0]]
    return panel, small


def solution(mesh):
    in_specs = (
        P(None, "space", "filt"),
        P(None, "space", "filt"),
        P(),
        P(),
        P(),
        P(),
        P(),
        P(),
        P(),
        P(),
        P(),
    )
    out_specs = (
        P(None, "space", "filt"),
        P(None, "space", "filt"),
        P(),
        P(),
        P(),
        P(),
        P("filt", None),
        P("filt"),
        P("filt", None),
        P(),
        P(),
    )
    return jax.shard_map(shards, mesh=mesh, in_specs=in_specs, out_specs=out_specs, check_vma=False)
```

```python
import functools
import math

import jax
import jax.numpy as jnp
from jax import lax
from jax.experimental import pallas as pl
from jax.experimental.pallas import tpu as pltpu
from jax.sharding import PartitionSpec as P

MESH = pl.DeviceIdType.MESH
LANES = 128


def padded_2(x, sides, width):
    for axis, dim in sides:
        size, length = (lax.axis_size(axis), x.shape[dim])
        up = [(i, (i + 1) % size) for i in range(size - 1)]
        down = [(j, i) for i, j in up]
        last = lax.slice_in_dim(x, length - width, length, axis=dim)
        initial = lax.slice_in_dim(x, 0, width, axis=dim)
        before = lax.ppermute(last, axis, up)
        after = lax.ppermute(initial, axis, down)
        x = jnp.concatenate([before, x, after], axis=dim)
    return x


def depthwise(padded, kernel, row_count, col_count):
    total = jnp.zeros((padded.shape[0], row_count, col_count), jnp.float32)
    for shift_row in range(7):
        for shift_col in range(7):
            piece = padded[
                :, shift_row : shift_row + row_count, shift_col : shift_col + col_count
            ].astype(jnp.float32)
            total = total + kernel[:, shift_row, shift_col][:, None, None] * piece
    return total


def conv_back(padded, kernel, row_count, col_count):
    total = jnp.zeros((padded.shape[0], row_count, col_count), jnp.float32)
    for shift_row in range(7):
        for shift_col in range(7):
            piece = padded[
                :,
                6 - shift_row : 6 - shift_row + row_count,
                6 - shift_col : 6 - shift_col + col_count,
            ].astype(jnp.float32)
            total = total + kernel[:, shift_row, shift_col][:, None, None] * piece
    return total


def kernel_terms(padded, convolution_gradient, row_count, col_count):
    ksize = 7
    columns = []
    for shift_col in range(ksize):
        corr = jnp.einsum(
            "crj,cij->cri",
            padded[:, :, shift_col : shift_col + col_count],
            convolution_gradient,
            preferred_element_type=jnp.float32,
        )
        total = corr[:, 0:ksize, 0]
        for row in range(1, row_count):
            total = total + corr[:, row : row + ksize, row]
        columns.append(total)
    return jnp.stack(columns, axis=2)


def gelu_exact(value):
    return value * (1.0 + jax.scipy.special.erf(value / math.sqrt(2.0))) * 0.5


def gelu_slope(value):
    return (1.0 + jax.scipy.special.erf(value / math.sqrt(2.0))) * 0.5 + value * jnp.exp(
        -0.5 * value * value
    ) / math.sqrt(2.0 * math.pi)


def shards(
    image,
    cotangent,
    kernel,
    dw_bias,
    layer_norm_gain,
    layer_norm_bias,
    w_expand,
    b_expand,
    w_reduce,
    b_reduce,
    layer_scale,
):
    channels, row_count, col_count = image.shape
    panel_rows = w_expand.shape[0] // lax.axis_size("filt")
    tok_count = row_count * col_count
    padded = padded_2(image, (("space", 1), ("filt", 2)), 3)
    conv = depthwise(padded, kernel, row_count, col_count)
    conv = conv + dw_bias[:, None, None]
    flat = conv.reshape(channels, tok_count)
    average = jnp.mean(flat, axis=0, keepdims=True)
    mean_removed = flat - average
    inverse_deviation = lax.rsqrt(
        jnp.mean(mean_removed * mean_removed, axis=0, keepdims=True) + 1e-06
    )
    standardized_input = mean_removed * inverse_deviation
    normalized_input = (
        standardized_input * layer_norm_gain[:, None] + layer_norm_bias[:, None]
    ).astype(jnp.bfloat16)
    hidden = (
        jnp.dot(w_expand, normalized_input, preferred_element_type=jnp.float32)
        + b_expand.astype(jnp.float32)[:, None]
    )
    active = gelu_exact(hidden).astype(jnp.bfloat16)
    branch = (
        lax.dot_general(
            w_reduce, active, (((0,), (0,)), ((), ())), preferred_element_type=jnp.float32
        )
        + b_reduce[:, None]
    )
    resid = image.reshape(channels, tok_count).astype(jnp.float32)
    output = (
        (resid + layer_scale[:, None] * branch)
        .astype(jnp.bfloat16)
        .reshape(channels, row_count, col_count)
    )
    cot_flat = cotangent.reshape(channels, tok_count).astype(jnp.float32)
    scaled = layer_scale[:, None] * cot_flat
    g_scale = jnp.sum(cot_flat * branch, axis=1)
    g_rbias = jnp.sum(scaled, axis=1)
    d_branch = scaled.astype(jnp.bfloat16)
    g_reduce = lax.dot_general(
        active, d_branch, (((1,), (1,)), ((), ())), preferred_element_type=jnp.float32
    )
    d_active = jnp.dot(w_reduce, d_branch, preferred_element_type=jnp.float32)
    d_hidden = (d_active * gelu_slope(hidden)).astype(jnp.bfloat16)
    g_ebias = jnp.sum(d_hidden.astype(jnp.float32), axis=1)
    g_expand = lax.dot_general(
        d_hidden, normalized_input, (((1,), (1,)), ((), ())), preferred_element_type=jnp.float32
    )
    normalized_gradient = lax.dot_general(
        w_expand, d_hidden, (((0,), (0,)), ((), ())), preferred_element_type=jnp.float32
    )
    norm_gain_gradient = jnp.sum(normalized_gradient * standardized_input, axis=1)
    g_lbias = jnp.sum(normalized_gradient, axis=1)
    standardized_gradient = normalized_gradient * layer_norm_gain[:, None]
    convolution_gradient = inverse_deviation * (
        standardized_gradient
        - jnp.mean(standardized_gradient, axis=0, keepdims=True)
        - standardized_input
        * jnp.mean(standardized_gradient * standardized_input, axis=0, keepdims=True)
    )
    convolution_gradient = convolution_gradient.astype(jnp.bfloat16).reshape(
        channels, row_count, col_count
    )
    d_float = convolution_gradient.astype(jnp.float32)
    g_dbias = jnp.sum(d_float, axis=(1, 2))
    padded_grad = padded_2(convolution_gradient, (("space", 1), ("filt", 2)), 3)
    g_kernel = kernel_terms(padded, convolution_gradient, row_count, col_count)
    factor = 1.0 / math.sqrt(tok_count * lax.axis_size("space") * lax.axis_size("filt"))
    parts = lax.axis_size("filt")
    panels = jnp.concatenate(
        [
            g_reduce.reshape(parts, panel_rows * channels),
            g_expand.reshape(parts, panel_rows * channels),
            g_ebias.reshape(parts, panel_rows),
        ],
        axis=1,
    )
    small = jnp.concatenate(
        [
            g_kernel.reshape(-1),
            g_dbias,
            norm_gain_gradient,
            g_lbias,
            g_scale,
            g_rbias,
        ]
    )
    panels, small, padded_grad = lax.optimization_barrier((panels, small, padded_grad))
    back = conv_back(padded_grad, kernel, row_count, col_count)
    image_grad = (cotangent.astype(jnp.float32) + back).astype(jnp.bfloat16)
    panel, small = grad_reduce(panels, small)
    total = jnp.concatenate([panel, small])
    total = total * factor
    cut = [panel_rows * channels, panel_rows * channels, panel_rows]
    g_reduce = total[: cut[0]].reshape(panel_rows, channels)
    g_expand = total[cut[0] : cut[0] + cut[1]].reshape(panel_rows, channels)
    g_ebias = total[cut[0] + cut[1] : sum(cut)]
    rest = total[sum(cut) :]
    ksq = kernel.shape[1] * kernel.shape[2]
    g_kernel = rest[: channels * ksq].reshape(kernel.shape)
    g_dbias, norm_gain_gradient, g_lbias, g_scale, g_rbias = (
        rest[channels * ksq + channels * i : channels * ksq + channels * (i + 1)]
        for i in range(5)
    )
    return (
        output,
        image_grad,
        g_kernel,
        g_dbias,
        norm_gain_gradient,
        g_lbias,
        g_expand,
        g_ebias,
        g_reduce,
        g_rbias,
        g_scale,
    )


def _rows(length):
    return -(-length // (8 * LANES)) * 8


def _flip(index, bit):
    return index + bit - 2 * bit * ((index // bit) % 2)


def reduce_kernel(nfilt, nspace, pr, sr, buf_ref, out_ref, *scratch):
    levels = nfilt.bit_length() - 1
    steps = nspace.bit_length() - 1
    recvs = scratch[:levels]
    stages = scratch[levels : 2 * levels]
    recv_s, send_sem, recv_sem = scratch[2 * levels :]
    s = lax.axis_index("space")
    f = lax.axis_index("filt")

    peers = []
    bit = nfilt // 2
    while bit >= 1:
        peers.append((s, _flip(f, bit)))
        bit //= 2
    for k in range(steps):
        peers.append((_flip(s, 1 << k), f))
    barrier = pltpu.get_barrier_semaphore()
    for peer in peers:
        pl.semaphore_signal(barrier, inc=1, device_id=peer, device_id_type=MESH)
    pl.semaphore_wait(barrier, len(peers))

    held = buf_ref
    count = nfilt
    bit = nfilt // 2
    sem = 0
    for level in range(levels):
        half = count // 2
        upper = (f // bit) % 2
        rows = half * pr
        peer = peers[level]
        send_panels = pltpu.make_async_remote_copy(
            src_ref=held.at[pl.ds(pl.multiple_of((1 - upper) * rows, 8), rows)],
            dst_ref=recvs[level].at[pl.ds(0, rows)],
            send_sem=send_sem.at[sem],
            recv_sem=recv_sem.at[sem],
            device_id=peer,
            device_id_type=MESH,
        )
        send_small = pltpu.make_async_remote_copy(
            src_ref=held.at[pl.ds(count * pr, sr)],
            dst_ref=recvs[level].at[pl.ds(rows, sr)],
            send_sem=send_sem.at[sem + 1],
            recv_sem=recv_sem.at[sem + 1],
            device_id=peer,
            device_id_type=MESH,
        )
        send_panels.start()
        send_small.start()
        send_panels.wait()
        send_small.wait()
        sem += 2
        stage = stages[level]
        stage[pl.ds(0, rows)] = (
            held[pl.ds(pl.multiple_of(upper * rows, 8), rows)] + recvs[level][pl.ds(0, rows)]
        )
        stage[pl.ds(rows, sr)] = held[pl.ds(count * pr, sr)] + recvs[level][pl.ds(rows, sr)]
        held = stage
        count = half
        bit //= 2

    if levels == 0:
        out_ref[...] = buf_ref[...]
    else:
        out_ref[...] = held[...]
    for k in range(steps):
        copy = pltpu.make_async_remote_copy(
            src_ref=out_ref,
            dst_ref=recv_s.at[k],
            send_sem=send_sem.at[sem],
            recv_sem=recv_sem.at[sem],
            device_id=peers[levels + k],
            device_id_type=MESH,
        )
        copy.start()
        copy.wait()
        sem += 1
        out_ref[...] = out_ref[...] + recv_s[k]


def grad_reduce(panels, small):
    nfilt = lax.axis_size("filt")
    nspace = lax.axis_size("space")
    width = panels.shape[1]
    pr = _rows(width)
    sr = _rows(small.shape[0])
    buf = jnp.concatenate(
        [
            jnp.pad(panels, ((0, 0), (0, pr * LANES - width))).reshape(nfilt * pr, LANES),
            jnp.pad(small, (0, sr * LANES - small.shape[0])).reshape(sr, LANES),
        ]
    )
    levels = nfilt.bit_length() - 1
    steps = nspace.bit_length() - 1
    scratch = []
    count = nfilt
    for _ in range(levels):
        count //= 2
        scratch.append(pltpu.VMEM((count * pr + sr, LANES), jnp.float32))
    count = nfilt
    for _ in range(levels):
        count //= 2
        scratch.append(pltpu.VMEM((count * pr + sr, LANES), jnp.float32))
    ncopies = 2 * levels + steps
    scratch += [
        pltpu.VMEM((max(steps, 1), pr + sr, LANES), jnp.float32),
        pltpu.SemaphoreType.DMA((ncopies,)),
        pltpu.SemaphoreType.DMA((ncopies,)),
    ]
    out = pl.pallas_call(
        functools.partial(reduce_kernel, nfilt, nspace, pr, sr),
        out_shape=jax.ShapeDtypeStruct((pr + sr, LANES), jnp.float32),
        in_specs=[pl.BlockSpec(memory_space=pltpu.VMEM)],
        out_specs=pl.BlockSpec(memory_space=pltpu.VMEM),
        scratch_shapes=scratch,
        compiler_params=pltpu.CompilerParams(collective_id=0, has_side_effects=True),
        cost_estimate=pl.CostEstimate(
            flops=0, transcendentals=0, bytes_accessed=200 * 1024 * 1024
        ),
    )(buf)
    panel = out[:pr].reshape(-1)[:width]
    small = out[pr:].reshape(-1)[: small.shape[0]]
    return panel, small


def solution(mesh):
    in_specs = (
        P(None, "space", "filt"),
        P(None, "space", "filt"),
        P(),
        P(),
        P(),
        P(),
        P(),
        P(),
        P(),
        P(),
        P(),
    )
    out_specs = (
        P(None, "space", "filt"),
        P(None, "space", "filt"),
        P(),
        P(),
        P(),
        P(),
        P("filt", None),
        P("filt"),
        P("filt", None),
        P(),
        P(),
    )
    return jax.shard_map(shards, mesh=mesh, in_specs=in_specs, out_specs=out_specs, check_vma=False)
```

```python
import functools
import math

import jax
import jax.numpy as jnp
from jax import lax
from jax.experimental import pallas as pl
from jax.experimental.pallas import tpu as pltpu
from jax.sharding import PartitionSpec as P

MESH = pl.DeviceIdType.MESH
LANES = 128


def _pairs(ds, df):
    ns, nf = lax.axis_size("space"), lax.axis_size("filt")
    pairs = []
    for s in range(ns):
        for f in range(nf):
            t, g = s + ds, f + df
            if 0 <= t < ns and 0 <= g < nf:
                pairs.append((s * nf + f, t * nf + g))
    return pairs


def padded_2(x, sides, width):
    del sides
    axes = ("space", "filt")
    rows, cols = x.shape[1], x.shape[2]
    lo_r, hi_r = slice(0, width), slice(rows - width, rows)
    lo_c, hi_c = slice(0, width), slice(cols - width, cols)
    above = lax.ppermute(x[:, hi_r, :], axes, _pairs(1, 0))
    below = lax.ppermute(x[:, lo_r, :], axes, _pairs(-1, 0))
    left = lax.ppermute(x[:, :, hi_c], axes, _pairs(0, 1))
    right = lax.ppermute(x[:, :, lo_c], axes, _pairs(0, -1))
    top_left = lax.ppermute(x[:, hi_r, hi_c], axes, _pairs(1, 1))
    top_right = lax.ppermute(x[:, hi_r, lo_c], axes, _pairs(1, -1))
    bottom_left = lax.ppermute(x[:, lo_r, hi_c], axes, _pairs(-1, 1))
    bottom_right = lax.ppermute(x[:, lo_r, lo_c], axes, _pairs(-1, -1))
    return jnp.concatenate(
        [
            jnp.concatenate([top_left, above, top_right], axis=2),
            jnp.concatenate([left, x, right], axis=2),
            jnp.concatenate([bottom_left, below, bottom_right], axis=2),
        ],
        axis=1,
    )


def depthwise(padded, kernel, row_count, col_count):
    total = jnp.zeros((padded.shape[0], row_count, col_count), jnp.float32)
    for shift_row in range(7):
        for shift_col in range(7):
            piece = padded[
                :, shift_row : shift_row + row_count, shift_col : shift_col + col_count
            ].astype(jnp.float32)
            total = total + kernel[:, shift_row, shift_col][:, None, None] * piece
    return total


def conv_back(padded, kernel, row_count, col_count):
    total = jnp.zeros((padded.shape[0], row_count, col_count), jnp.float32)
    for shift_row in range(7):
        for shift_col in range(7):
            piece = padded[
                :,
                6 - shift_row : 6 - shift_row + row_count,
                6 - shift_col : 6 - shift_col + col_count,
            ].astype(jnp.float32)
            total = total + kernel[:, shift_row, shift_col][:, None, None] * piece
    return total


def kernel_terms(padded, convolution_gradient, row_count, col_count):
    ksize = 7
    columns = []
    for shift_col in range(ksize):
        corr = jnp.einsum(
            "crj,cij->cri",
            padded[:, :, shift_col : shift_col + col_count],
            convolution_gradient,
            preferred_element_type=jnp.float32,
        )
        total = corr[:, 0:ksize, 0]
        for row in range(1, row_count):
            total = total + corr[:, row : row + ksize, row]
        columns.append(total)
    return jnp.stack(columns, axis=2)


def gelu_exact(value):
    return value * (1.0 + jax.scipy.special.erf(value / math.sqrt(2.0))) * 0.5


def gelu_slope(value):
    return (1.0 + jax.scipy.special.erf(value / math.sqrt(2.0))) * 0.5 + value * jnp.exp(
        -0.5 * value * value
    ) / math.sqrt(2.0 * math.pi)


def shards(
    image,
    cotangent,
    kernel,
    dw_bias,
    layer_norm_gain,
    layer_norm_bias,
    w_expand,
    b_expand,
    w_reduce,
    b_reduce,
    layer_scale,
):
    channels, row_count, col_count = image.shape
    panel_rows = w_expand.shape[0] // lax.axis_size("filt")
    tok_count = row_count * col_count
    padded = padded_2(image, (("space", 1), ("filt", 2)), 3)
    conv = depthwise(padded, kernel, row_count, col_count)
    conv = conv + dw_bias[:, None, None]
    flat = conv.reshape(channels, tok_count)
    average = jnp.mean(flat, axis=0, keepdims=True)
    mean_removed = flat - average
    inverse_deviation = lax.rsqrt(
        jnp.mean(mean_removed * mean_removed, axis=0, keepdims=True) + 1e-06
    )
    standardized_input = mean_removed * inverse_deviation
    normalized_input = (
        standardized_input * layer_norm_gain[:, None] + layer_norm_bias[:, None]
    ).astype(jnp.bfloat16)
    hidden = (
        jnp.dot(w_expand, normalized_input, preferred_element_type=jnp.float32)
        + b_expand.astype(jnp.float32)[:, None]
    )
    active = gelu_exact(hidden).astype(jnp.bfloat16)
    branch = (
        lax.dot_general(
            w_reduce, active, (((0,), (0,)), ((), ())), preferred_element_type=jnp.float32
        )
        + b_reduce[:, None]
    )
    resid = image.reshape(channels, tok_count).astype(jnp.float32)
    output = (
        (resid + layer_scale[:, None] * branch)
        .astype(jnp.bfloat16)
        .reshape(channels, row_count, col_count)
    )
    cot_flat = cotangent.reshape(channels, tok_count).astype(jnp.float32)
    scaled = layer_scale[:, None] * cot_flat
    g_scale = jnp.sum(cot_flat * branch, axis=1)
    g_rbias = jnp.sum(scaled, axis=1)
    d_branch = scaled.astype(jnp.bfloat16)
    g_reduce = lax.dot_general(
        active, d_branch, (((1,), (1,)), ((), ())), preferred_element_type=jnp.float32
    )
    d_active = jnp.dot(w_reduce, d_branch, preferred_element_type=jnp.float32)
    d_hidden = (d_active * gelu_slope(hidden)).astype(jnp.bfloat16)
    g_ebias = jnp.sum(d_hidden.astype(jnp.float32), axis=1)
    g_expand = lax.dot_general(
        d_hidden, normalized_input, (((1,), (1,)), ((), ())), preferred_element_type=jnp.float32
    )
    normalized_gradient = lax.dot_general(
        w_expand, d_hidden, (((0,), (0,)), ((), ())), preferred_element_type=jnp.float32
    )
    norm_gain_gradient = jnp.sum(normalized_gradient * standardized_input, axis=1)
    g_lbias = jnp.sum(normalized_gradient, axis=1)
    standardized_gradient = normalized_gradient * layer_norm_gain[:, None]
    convolution_gradient = inverse_deviation * (
        standardized_gradient
        - jnp.mean(standardized_gradient, axis=0, keepdims=True)
        - standardized_input
        * jnp.mean(standardized_gradient * standardized_input, axis=0, keepdims=True)
    )
    convolution_gradient = convolution_gradient.astype(jnp.bfloat16).reshape(
        channels, row_count, col_count
    )
    d_float = convolution_gradient.astype(jnp.float32)
    g_dbias = jnp.sum(d_float, axis=(1, 2))
    padded_grad = padded_2(convolution_gradient, (("space", 1), ("filt", 2)), 3)
    g_kernel = kernel_terms(padded, convolution_gradient, row_count, col_count)
    factor = 1.0 / math.sqrt(tok_count * lax.axis_size("space") * lax.axis_size("filt"))
    parts = lax.axis_size("filt")
    panels = jnp.concatenate(
        [
            g_reduce.reshape(parts, panel_rows * channels),
            g_expand.reshape(parts, panel_rows * channels),
            g_ebias.reshape(parts, panel_rows),
        ],
        axis=1,
    )
    small = jnp.concatenate(
        [
            g_kernel.reshape(-1),
            g_dbias,
            norm_gain_gradient,
            g_lbias,
            g_scale,
            g_rbias,
        ]
    )
    panels, small, padded_grad = lax.optimization_barrier((panels, small, padded_grad))
    back = conv_back(padded_grad, kernel, row_count, col_count)
    image_grad = (cotangent.astype(jnp.float32) + back).astype(jnp.bfloat16)
    panel, small = grad_reduce(panels, small)
    total = jnp.concatenate([panel, small])
    total = total * factor
    cut = [panel_rows * channels, panel_rows * channels, panel_rows]
    g_reduce = total[: cut[0]].reshape(panel_rows, channels)
    g_expand = total[cut[0] : cut[0] + cut[1]].reshape(panel_rows, channels)
    g_ebias = total[cut[0] + cut[1] : sum(cut)]
    rest = total[sum(cut) :]
    ksq = kernel.shape[1] * kernel.shape[2]
    g_kernel = rest[: channels * ksq].reshape(kernel.shape)
    g_dbias, norm_gain_gradient, g_lbias, g_scale, g_rbias = (
        rest[channels * ksq + channels * i : channels * ksq + channels * (i + 1)]
        for i in range(5)
    )
    return (
        output,
        image_grad,
        g_kernel,
        g_dbias,
        norm_gain_gradient,
        g_lbias,
        g_expand,
        g_ebias,
        g_reduce,
        g_rbias,
        g_scale,
    )


def _rows(length):
    return -(-length // (8 * LANES)) * 8


def _flip(index, bit):
    return index + bit - 2 * bit * ((index // bit) % 2)


def reduce_kernel(nfilt, nspace, pr, sr, buf_ref, out_ref, *scratch):
    levels = nfilt.bit_length() - 1
    steps = nspace.bit_length() - 1
    recvs = scratch[:levels]
    stages = scratch[levels : 2 * levels]
    recv_s, send_sem, recv_sem = scratch[2 * levels :]
    s = lax.axis_index("space")
    f = lax.axis_index("filt")

    peers = []
    bit = nfilt // 2
    while bit >= 1:
        peers.append((s, _flip(f, bit)))
        bit //= 2
    for k in range(steps):
        peers.append((_flip(s, 1 << k), f))
    barrier = pltpu.get_barrier_semaphore()
    for peer in peers:
        pl.semaphore_signal(barrier, inc=1, device_id=peer, device_id_type=MESH)
    pl.semaphore_wait(barrier, len(peers))

    held = buf_ref
    count = nfilt
    bit = nfilt // 2
    sem = 0
    for level in range(levels):
        half = count // 2
        upper = (f // bit) % 2
        rows = half * pr
        peer = peers[level]
        send_panels = pltpu.make_async_remote_copy(
            src_ref=held.at[pl.ds(pl.multiple_of((1 - upper) * rows, 8), rows)],
            dst_ref=recvs[level].at[pl.ds(0, rows)],
            send_sem=send_sem.at[sem],
            recv_sem=recv_sem.at[sem],
            device_id=peer,
            device_id_type=MESH,
        )
        send_small = pltpu.make_async_remote_copy(
            src_ref=held.at[pl.ds(count * pr, sr)],
            dst_ref=recvs[level].at[pl.ds(rows, sr)],
            send_sem=send_sem.at[sem + 1],
            recv_sem=recv_sem.at[sem + 1],
            device_id=peer,
            device_id_type=MESH,
        )
        send_panels.start()
        send_small.start()
        send_panels.wait()
        send_small.wait()
        sem += 2
        stage = stages[level]
        stage[pl.ds(0, rows)] = (
            held[pl.ds(pl.multiple_of(upper * rows, 8), rows)] + recvs[level][pl.ds(0, rows)]
        )
        stage[pl.ds(rows, sr)] = held[pl.ds(count * pr, sr)] + recvs[level][pl.ds(rows, sr)]
        held = stage
        count = half
        bit //= 2

    if levels == 0:
        out_ref[...] = buf_ref[...]
    else:
        out_ref[...] = held[...]
    for k in range(steps):
        copy = pltpu.make_async_remote_copy(
            src_ref=out_ref,
            dst_ref=recv_s.at[k],
            send_sem=send_sem.at[sem],
            recv_sem=recv_sem.at[sem],
            device_id=peers[levels + k],
            device_id_type=MESH,
        )
        copy.start()
        copy.wait()
        sem += 1
        out_ref[...] = out_ref[...] + recv_s[k]


def grad_reduce(panels, small):
    nfilt = lax.axis_size("filt")
    nspace = lax.axis_size("space")
    width = panels.shape[1]
    pr = _rows(width)
    sr = _rows(small.shape[0])
    buf = jnp.concatenate(
        [
            jnp.pad(panels, ((0, 0), (0, pr * LANES - width))).reshape(nfilt * pr, LANES),
            jnp.pad(small, (0, sr * LANES - small.shape[0])).reshape(sr, LANES),
        ]
    )
    levels = nfilt.bit_length() - 1
    steps = nspace.bit_length() - 1
    scratch = []
    count = nfilt
    for _ in range(levels):
        count //= 2
        scratch.append(pltpu.VMEM((count * pr + sr, LANES), jnp.float32))
    count = nfilt
    for _ in range(levels):
        count //= 2
        scratch.append(pltpu.VMEM((count * pr + sr, LANES), jnp.float32))
    ncopies = 2 * levels + steps
    scratch += [
        pltpu.VMEM((max(steps, 1), pr + sr, LANES), jnp.float32),
        pltpu.SemaphoreType.DMA((ncopies,)),
        pltpu.SemaphoreType.DMA((ncopies,)),
    ]
    out = pl.pallas_call(
        functools.partial(reduce_kernel, nfilt, nspace, pr, sr),
        out_shape=jax.ShapeDtypeStruct((pr + sr, LANES), jnp.float32),
        in_specs=[pl.BlockSpec(memory_space=pltpu.VMEM)],
        out_specs=pl.BlockSpec(memory_space=pltpu.VMEM),
        scratch_shapes=scratch,
        compiler_params=pltpu.CompilerParams(collective_id=0, has_side_effects=True),
        cost_estimate=pl.CostEstimate(
            flops=0, transcendentals=0, bytes_accessed=200 * 1024 * 1024
        ),
    )(buf)
    panel = out[:pr].reshape(-1)[:width]
    small = out[pr:].reshape(-1)[: small.shape[0]]
    return panel, small


def solution(mesh):
    in_specs = (
        P(None, "space", "filt"),
        P(None, "space", "filt"),
        P(),
        P(),
        P(),
        P(),
        P(),
        P(),
        P(),
        P(),
        P(),
    )
    out_specs = (
        P(None, "space", "filt"),
        P(None, "space", "filt"),
        P(),
        P(),
        P(),
        P(),
        P("filt", None),
        P("filt"),
        P("filt", None),
        P(),
        P(),
    )
    return jax.shard_map(shards, mesh=mesh, in_specs=in_specs, out_specs=out_specs, check_vma=False)
```

```python
import functools
import math

import jax
import jax.numpy as jnp
from jax import lax
from jax.experimental import pallas as pl
from jax.experimental.pallas import tpu as pltpu
from jax.sharding import PartitionSpec as P

MESH = pl.DeviceIdType.MESH
LANES = 128


_DIRS = [(-1, 0), (1, 0), (0, -1), (0, 1), (-1, -1), (-1, 1), (1, -1), (1, 1)]


def _lanes(df, cols):
    if df == 0:
        return slice(0, cols)
    if df > 0:
        return slice(cols - LANES, cols)
    return slice(0, LANES)


def halo_kernel(ns, nf, cols, x_ref, *refs):
    outs = refs[:8]
    slots = refs[8:16]
    send_sem, recv_sem = refs[16:]
    s = lax.axis_index("space")
    f = lax.axis_index("filt")

    def exists(d):
        t, g = s + d[0], f + d[1]
        return (t >= 0) & (t < ns) & (g >= 0) & (g < nf)

    def desc(k):
        d = _DIRS[k]
        back = _DIRS.index((-d[0], -d[1]))
        return pltpu.make_async_remote_copy(
            src_ref=x_ref.at[:, :, _lanes(d[1], cols)],
            dst_ref=slots[back],
            send_sem=send_sem.at[k],
            recv_sem=recv_sem.at[back],
            device_id=(s + d[0], f + d[1]),
            device_id_type=MESH,
        )

    barrier = pltpu.get_barrier_semaphore()
    for k, d in enumerate(_DIRS):

        @pl.when(exists(d))
        def _():
            pl.semaphore_signal(
                barrier, inc=1, device_id=(s + d[0], f + d[1]), device_id_type=MESH
            )

    count = exists(_DIRS[0]).astype(jnp.int32)
    for d in _DIRS[1:]:
        count = count + exists(d).astype(jnp.int32)
    pl.semaphore_wait(barrier, count)

    for k, d in enumerate(_DIRS):

        @pl.when(exists(d))
        def _():
            desc(k).start()

    for k, d in enumerate(_DIRS):
        back = _DIRS.index((-d[0], -d[1]))

        @pl.when(exists(d))
        def _():
            desc(k).wait_send()
            desc(back).wait_recv()
            outs[k][...] = slots[k][...]

        @pl.when(jnp.logical_not(exists(d)))
        def _():
            outs[k][...] = jnp.zeros(outs[k].shape, outs[k].dtype)


def padded_2(x, sides, width, collective_id):
    del sides
    ns, nf = lax.axis_size("space"), lax.axis_size("filt")
    channels, rows, cols = x.shape
    shapes = [
        jax.ShapeDtypeStruct((channels, rows, _lanes(d[1], cols).stop - _lanes(d[1], cols).start), x.dtype)
        for d in _DIRS
    ]
    got = pl.pallas_call(
        functools.partial(halo_kernel, ns, nf, cols),
        out_shape=shapes,
        in_specs=[pl.BlockSpec(memory_space=pltpu.VMEM)],
        out_specs=[pl.BlockSpec(memory_space=pltpu.VMEM)] * 8,
        scratch_shapes=[pltpu.VMEM(sh.shape, sh.dtype) for sh in shapes]
        + [pltpu.SemaphoreType.DMA((8,)), pltpu.SemaphoreType.DMA((8,))],
        compiler_params=pltpu.CompilerParams(
            collective_id=collective_id, has_side_effects=True
        ),
    )(x)
    piece = dict(zip(_DIRS, got))
    hi_r, lo_r = slice(rows - width, rows), slice(0, width)

    above = piece[(-1, 0)][:, hi_r, :]
    below = piece[(1, 0)][:, lo_r, :]
    lw = piece[(0, -1)].shape[2]
    left = piece[(0, -1)][:, :, lw - width : lw]
    right = piece[(0, 1)][:, :, 0:width]
    top_left = piece[(-1, -1)][:, hi_r, lw - width : lw]
    top_right = piece[(-1, 1)][:, hi_r, 0:width]
    bottom_left = piece[(1, -1)][:, lo_r, lw - width : lw]
    bottom_right = piece[(1, 1)][:, lo_r, 0:width]
    return jnp.concatenate(
        [
            jnp.concatenate([top_left, above, top_right], axis=2),
            jnp.concatenate([left, x, right], axis=2),
            jnp.concatenate([bottom_left, below, bottom_right], axis=2),
        ],
        axis=1,
    )


def depthwise(padded, kernel, row_count, col_count):
    total = jnp.zeros((padded.shape[0], row_count, col_count), jnp.float32)
    for shift_row in range(7):
        for shift_col in range(7):
            piece = padded[
                :, shift_row : shift_row + row_count, shift_col : shift_col + col_count
            ].astype(jnp.float32)
            total = total + kernel[:, shift_row, shift_col][:, None, None] * piece
    return total


def conv_back(padded, kernel, row_count, col_count):
    total = jnp.zeros((padded.shape[0], row_count, col_count), jnp.float32)
    for shift_row in range(7):
        for shift_col in range(7):
            piece = padded[
                :,
                6 - shift_row : 6 - shift_row + row_count,
                6 - shift_col : 6 - shift_col + col_count,
            ].astype(jnp.float32)
            total = total + kernel[:, shift_row, shift_col][:, None, None] * piece
    return total


def kernel_terms(padded, convolution_gradient, row_count, col_count):
    ksize = 7
    columns = []
    for shift_col in range(ksize):
        corr = jnp.einsum(
            "crj,cij->cri",
            padded[:, :, shift_col : shift_col + col_count],
            convolution_gradient,
            preferred_element_type=jnp.float32,
        )
        total = corr[:, 0:ksize, 0]
        for row in range(1, row_count):
            total = total + corr[:, row : row + ksize, row]
        columns.append(total)
    return jnp.stack(columns, axis=2)


def gelu_exact(value):
    return value * (1.0 + jax.scipy.special.erf(value / math.sqrt(2.0))) * 0.5


def gelu_slope(value):
    return (1.0 + jax.scipy.special.erf(value / math.sqrt(2.0))) * 0.5 + value * jnp.exp(
        -0.5 * value * value
    ) / math.sqrt(2.0 * math.pi)


def shards(
    image,
    cotangent,
    kernel,
    dw_bias,
    layer_norm_gain,
    layer_norm_bias,
    w_expand,
    b_expand,
    w_reduce,
    b_reduce,
    layer_scale,
):
    channels, row_count, col_count = image.shape
    panel_rows = w_expand.shape[0] // lax.axis_size("filt")
    tok_count = row_count * col_count
    padded = padded_2(image, (("space", 1), ("filt", 2)), 3, 1)
    conv = depthwise(padded, kernel, row_count, col_count)
    conv = conv + dw_bias[:, None, None]
    flat = conv.reshape(channels, tok_count)
    average = jnp.mean(flat, axis=0, keepdims=True)
    mean_removed = flat - average
    inverse_deviation = lax.rsqrt(
        jnp.mean(mean_removed * mean_removed, axis=0, keepdims=True) + 1e-06
    )
    standardized_input = mean_removed * inverse_deviation
    normalized_input = (
        standardized_input * layer_norm_gain[:, None] + layer_norm_bias[:, None]
    ).astype(jnp.bfloat16)
    hidden = (
        jnp.dot(w_expand, normalized_input, preferred_element_type=jnp.float32)
        + b_expand.astype(jnp.float32)[:, None]
    )
    active = gelu_exact(hidden).astype(jnp.bfloat16)
    branch = (
        lax.dot_general(
            w_reduce, active, (((0,), (0,)), ((), ())), preferred_element_type=jnp.float32
        )
        + b_reduce[:, None]
    )
    resid = image.reshape(channels, tok_count).astype(jnp.float32)
    output = (
        (resid + layer_scale[:, None] * branch)
        .astype(jnp.bfloat16)
        .reshape(channels, row_count, col_count)
    )
    cot_flat = cotangent.reshape(channels, tok_count).astype(jnp.float32)
    scaled = layer_scale[:, None] * cot_flat
    g_scale = jnp.sum(cot_flat * branch, axis=1)
    g_rbias = jnp.sum(scaled, axis=1)
    d_branch = scaled.astype(jnp.bfloat16)
    g_reduce = lax.dot_general(
        active, d_branch, (((1,), (1,)), ((), ())), preferred_element_type=jnp.float32
    )
    d_active = jnp.dot(w_reduce, d_branch, preferred_element_type=jnp.float32)
    d_hidden = (d_active * gelu_slope(hidden)).astype(jnp.bfloat16)
    g_ebias = jnp.sum(d_hidden.astype(jnp.float32), axis=1)
    g_expand = lax.dot_general(
        d_hidden, normalized_input, (((1,), (1,)), ((), ())), preferred_element_type=jnp.float32
    )
    normalized_gradient = lax.dot_general(
        w_expand, d_hidden, (((0,), (0,)), ((), ())), preferred_element_type=jnp.float32
    )
    norm_gain_gradient = jnp.sum(normalized_gradient * standardized_input, axis=1)
    g_lbias = jnp.sum(normalized_gradient, axis=1)
    standardized_gradient = normalized_gradient * layer_norm_gain[:, None]
    convolution_gradient = inverse_deviation * (
        standardized_gradient
        - jnp.mean(standardized_gradient, axis=0, keepdims=True)
        - standardized_input
        * jnp.mean(standardized_gradient * standardized_input, axis=0, keepdims=True)
    )
    convolution_gradient = convolution_gradient.astype(jnp.bfloat16).reshape(
        channels, row_count, col_count
    )
    d_float = convolution_gradient.astype(jnp.float32)
    g_dbias = jnp.sum(d_float, axis=(1, 2))
    padded_grad = padded_2(convolution_gradient, (("space", 1), ("filt", 2)), 3, 2)
    g_kernel = kernel_terms(padded, convolution_gradient, row_count, col_count)
    factor = 1.0 / math.sqrt(tok_count * lax.axis_size("space") * lax.axis_size("filt"))
    parts = lax.axis_size("filt")
    panels = jnp.concatenate(
        [
            g_reduce.reshape(parts, panel_rows * channels),
            g_expand.reshape(parts, panel_rows * channels),
            g_ebias.reshape(parts, panel_rows),
        ],
        axis=1,
    )
    small = jnp.concatenate(
        [
            g_kernel.reshape(-1),
            g_dbias,
            norm_gain_gradient,
            g_lbias,
            g_scale,
            g_rbias,
        ]
    )
    panels, small, padded_grad = lax.optimization_barrier((panels, small, padded_grad))
    back = conv_back(padded_grad, kernel, row_count, col_count)
    image_grad = (cotangent.astype(jnp.float32) + back).astype(jnp.bfloat16)
    panel, small = grad_reduce(panels, small)
    total = jnp.concatenate([panel, small])
    total = total * factor
    cut = [panel_rows * channels, panel_rows * channels, panel_rows]
    g_reduce = total[: cut[0]].reshape(panel_rows, channels)
    g_expand = total[cut[0] : cut[0] + cut[1]].reshape(panel_rows, channels)
    g_ebias = total[cut[0] + cut[1] : sum(cut)]
    rest = total[sum(cut) :]
    ksq = kernel.shape[1] * kernel.shape[2]
    g_kernel = rest[: channels * ksq].reshape(kernel.shape)
    g_dbias, norm_gain_gradient, g_lbias, g_scale, g_rbias = (
        rest[channels * ksq + channels * i : channels * ksq + channels * (i + 1)]
        for i in range(5)
    )
    return (
        output,
        image_grad,
        g_kernel,
        g_dbias,
        norm_gain_gradient,
        g_lbias,
        g_expand,
        g_ebias,
        g_reduce,
        g_rbias,
        g_scale,
    )


def _rows(length):
    return -(-length // (8 * LANES)) * 8


def _flip(index, bit):
    return index + bit - 2 * bit * ((index // bit) % 2)


def reduce_kernel(nfilt, nspace, pr, sr, buf_ref, out_ref, *scratch):
    levels = nfilt.bit_length() - 1
    steps = nspace.bit_length() - 1
    recvs = scratch[:levels]
    stages = scratch[levels : 2 * levels]
    recv_s, send_sem, recv_sem = scratch[2 * levels :]
    s = lax.axis_index("space")
    f = lax.axis_index("filt")

    peers = []
    bit = nfilt // 2
    while bit >= 1:
        peers.append((s, _flip(f, bit)))
        bit //= 2
    for k in range(steps):
        peers.append((_flip(s, 1 << k), f))
    barrier = pltpu.get_barrier_semaphore()
    for peer in peers:
        pl.semaphore_signal(barrier, inc=1, device_id=peer, device_id_type=MESH)
    pl.semaphore_wait(barrier, len(peers))

    held = buf_ref
    count = nfilt
    bit = nfilt // 2
    sem = 0
    for level in range(levels):
        half = count // 2
        upper = (f // bit) % 2
        rows = half * pr
        peer = peers[level]
        send_panels = pltpu.make_async_remote_copy(
            src_ref=held.at[pl.ds(pl.multiple_of((1 - upper) * rows, 8), rows)],
            dst_ref=recvs[level].at[pl.ds(0, rows)],
            send_sem=send_sem.at[sem],
            recv_sem=recv_sem.at[sem],
            device_id=peer,
            device_id_type=MESH,
        )
        send_small = pltpu.make_async_remote_copy(
            src_ref=held.at[pl.ds(count * pr, sr)],
            dst_ref=recvs[level].at[pl.ds(rows, sr)],
            send_sem=send_sem.at[sem + 1],
            recv_sem=recv_sem.at[sem + 1],
            device_id=peer,
            device_id_type=MESH,
        )
        send_panels.start()
        send_small.start()
        send_panels.wait()
        send_small.wait()
        sem += 2
        stage = stages[level]
        stage[pl.ds(0, rows)] = (
            held[pl.ds(pl.multiple_of(upper * rows, 8), rows)] + recvs[level][pl.ds(0, rows)]
        )
        stage[pl.ds(rows, sr)] = held[pl.ds(count * pr, sr)] + recvs[level][pl.ds(rows, sr)]
        held = stage
        count = half
        bit //= 2

    if levels == 0:
        out_ref[...] = buf_ref[...]
    else:
        out_ref[...] = held[...]
    for k in range(steps):
        copy = pltpu.make_async_remote_copy(
            src_ref=out_ref,
            dst_ref=recv_s.at[k],
            send_sem=send_sem.at[sem],
            recv_sem=recv_sem.at[sem],
            device_id=peers[levels + k],
            device_id_type=MESH,
        )
        copy.start()
        copy.wait()
        sem += 1
        out_ref[...] = out_ref[...] + recv_s[k]


def grad_reduce(panels, small):
    nfilt = lax.axis_size("filt")
    nspace = lax.axis_size("space")
    width = panels.shape[1]
    pr = _rows(width)
    sr = _rows(small.shape[0])
    buf = jnp.concatenate(
        [
            jnp.pad(panels, ((0, 0), (0, pr * LANES - width))).reshape(nfilt * pr, LANES),
            jnp.pad(small, (0, sr * LANES - small.shape[0])).reshape(sr, LANES),
        ]
    )
    levels = nfilt.bit_length() - 1
    steps = nspace.bit_length() - 1
    scratch = []
    count = nfilt
    for _ in range(levels):
        count //= 2
        scratch.append(pltpu.VMEM((count * pr + sr, LANES), jnp.float32))
    count = nfilt
    for _ in range(levels):
        count //= 2
        scratch.append(pltpu.VMEM((count * pr + sr, LANES), jnp.float32))
    ncopies = 2 * levels + steps
    scratch += [
        pltpu.VMEM((max(steps, 1), pr + sr, LANES), jnp.float32),
        pltpu.SemaphoreType.DMA((ncopies,)),
        pltpu.SemaphoreType.DMA((ncopies,)),
    ]
    out = pl.pallas_call(
        functools.partial(reduce_kernel, nfilt, nspace, pr, sr),
        out_shape=jax.ShapeDtypeStruct((pr + sr, LANES), jnp.float32),
        in_specs=[pl.BlockSpec(memory_space=pltpu.VMEM)],
        out_specs=pl.BlockSpec(memory_space=pltpu.VMEM),
        scratch_shapes=scratch,
        compiler_params=pltpu.CompilerParams(collective_id=0, has_side_effects=True),
        cost_estimate=pl.CostEstimate(
            flops=0, transcendentals=0, bytes_accessed=200 * 1024 * 1024
        ),
    )(buf)
    panel = out[:pr].reshape(-1)[:width]
    small = out[pr:].reshape(-1)[: small.shape[0]]
    return panel, small


def solution(mesh):
    in_specs = (
        P(None, "space", "filt"),
        P(None, "space", "filt"),
        P(),
        P(),
        P(),
        P(),
        P(),
        P(),
        P(),
        P(),
        P(),
    )
    out_specs = (
        P(None, "space", "filt"),
        P(None, "space", "filt"),
        P(),
        P(),
        P(),
        P(),
        P("filt", None),
        P("filt"),
        P("filt", None),
        P(),
        P(),
    )
    return jax.shard_map(shards, mesh=mesh, in_specs=in_specs, out_specs=out_specs, check_vma=False)
```

```python
import functools
import math

import jax
import jax.numpy as jnp
from jax import lax
from jax.experimental import pallas as pl
from jax.experimental.pallas import tpu as pltpu
from jax.sharding import PartitionSpec as P

MESH = pl.DeviceIdType.MESH
LANES = 128


_DIRS = [(-1, 0), (1, 0), (0, -1), (0, 1), (-1, -1), (-1, 1), (1, -1), (1, 1)]


def _lanes(df, cols):
    if df == 0:
        return slice(0, cols)
    if df > 0:
        return slice(cols - LANES, cols)
    return slice(0, LANES)


def _halo_ops(ns, nf, cols, x_ref, outs, slots, send_sem, recv_sem):
    s = lax.axis_index("space")
    f = lax.axis_index("filt")

    def exists(d):
        t, g = s + d[0], f + d[1]
        return (t >= 0) & (t < ns) & (g >= 0) & (g < nf)

    def desc(k):
        d = _DIRS[k]
        back = _DIRS.index((-d[0], -d[1]))
        return pltpu.make_async_remote_copy(
            src_ref=x_ref.at[:, :, _lanes(d[1], cols)],
            dst_ref=slots[back],
            send_sem=send_sem.at[k],
            recv_sem=recv_sem.at[back],
            device_id=(s + d[0], f + d[1]),
            device_id_type=MESH,
        )

    def signal(barrier):
        count = 0
        for d in _DIRS:

            @pl.when(exists(d))
            def _():
                pl.semaphore_signal(
                    barrier, inc=1, device_id=(s + d[0], f + d[1]), device_id_type=MESH
                )

            count = count + exists(d).astype(jnp.int32)
        return count

    def start():
        for k, d in enumerate(_DIRS):

            @pl.when(exists(d))
            def _():
                desc(k).start()

    def finish():
        for k, d in enumerate(_DIRS):
            back = _DIRS.index((-d[0], -d[1]))

            @pl.when(exists(d))
            def _():
                desc(k).wait_send()
                desc(back).wait_recv()
                outs[k][...] = slots[k][...]

            @pl.when(jnp.logical_not(exists(d)))
            def _():
                outs[k][...] = jnp.zeros(outs[k].shape, outs[k].dtype)

    return signal, start, finish


def halo_kernel(ns, nf, cols, x_ref, *refs):
    signal, start, finish = _halo_ops(ns, nf, cols, x_ref, refs[:8], refs[8:16], *refs[16:])
    barrier = pltpu.get_barrier_semaphore()
    pl.semaphore_wait(barrier, signal(barrier))
    start()
    finish()


def _halo_shapes(x):
    channels, rows, cols = x.shape
    return [
        jax.ShapeDtypeStruct((channels, rows, _lanes(d[1], cols).stop - _lanes(d[1], cols).start), x.dtype)
        for d in _DIRS
    ]


def _assemble(x, got, width):
    rows = x.shape[1]
    piece = dict(zip(_DIRS, got))
    hi_r, lo_r = slice(rows - width, rows), slice(0, width)
    above = piece[(-1, 0)][:, hi_r, :]
    below = piece[(1, 0)][:, lo_r, :]
    lw = piece[(0, -1)].shape[2]
    left = piece[(0, -1)][:, :, lw - width : lw]
    right = piece[(0, 1)][:, :, 0:width]
    top_left = piece[(-1, -1)][:, hi_r, lw - width : lw]
    top_right = piece[(-1, 1)][:, hi_r, 0:width]
    bottom_left = piece[(1, -1)][:, lo_r, lw - width : lw]
    bottom_right = piece[(1, 1)][:, lo_r, 0:width]
    return jnp.concatenate(
        [
            jnp.concatenate([top_left, above, top_right], axis=2),
            jnp.concatenate([left, x, right], axis=2),
            jnp.concatenate([bottom_left, below, bottom_right], axis=2),
        ],
        axis=1,
    )


def padded_2(x, sides, width, collective_id):
    del sides
    ns, nf = lax.axis_size("space"), lax.axis_size("filt")
    shapes = _halo_shapes(x)
    got = pl.pallas_call(
        functools.partial(halo_kernel, ns, nf, x.shape[2]),
        out_shape=shapes,
        in_specs=[pl.BlockSpec(memory_space=pltpu.VMEM)],
        out_specs=[pl.BlockSpec(memory_space=pltpu.VMEM)] * 8,
        scratch_shapes=[pltpu.VMEM(sh.shape, sh.dtype) for sh in shapes]
        + [pltpu.SemaphoreType.DMA((8,)), pltpu.SemaphoreType.DMA((8,))],
        compiler_params=pltpu.CompilerParams(
            collective_id=collective_id, has_side_effects=True
        ),
    )(x)
    return _assemble(x, got, width)


def depthwise(padded, kernel, row_count, col_count):
    total = jnp.zeros((padded.shape[0], row_count, col_count), jnp.float32)
    for shift_row in range(7):
        for shift_col in range(7):
            piece = padded[
                :, shift_row : shift_row + row_count, shift_col : shift_col + col_count
            ].astype(jnp.float32)
            total = total + kernel[:, shift_row, shift_col][:, None, None] * piece
    return total


def conv_back(padded, kernel, row_count, col_count):
    total = jnp.zeros((padded.shape[0], row_count, col_count), jnp.float32)
    for shift_row in range(7):
        for shift_col in range(7):
            piece = padded[
                :,
                6 - shift_row : 6 - shift_row + row_count,
                6 - shift_col : 6 - shift_col + col_count,
            ].astype(jnp.float32)
            total = total + kernel[:, shift_row, shift_col][:, None, None] * piece
    return total


def kernel_terms(padded, convolution_gradient, row_count, col_count):
    ksize = 7
    columns = []
    for shift_col in range(ksize):
        corr = jnp.einsum(
            "crj,cij->cri",
            padded[:, :, shift_col : shift_col + col_count],
            convolution_gradient,
            preferred_element_type=jnp.float32,
        )
        total = corr[:, 0:ksize, 0]
        for row in range(1, row_count):
            total = total + corr[:, row : row + ksize, row]
        columns.append(total)
    return jnp.stack(columns, axis=2)


def gelu_exact(value):
    return value * (1.0 + jax.scipy.special.erf(value / math.sqrt(2.0))) * 0.5


def gelu_slope(value):
    return (1.0 + jax.scipy.special.erf(value / math.sqrt(2.0))) * 0.5 + value * jnp.exp(
        -0.5 * value * value
    ) / math.sqrt(2.0 * math.pi)


def shards(
    image,
    cotangent,
    kernel,
    dw_bias,
    layer_norm_gain,
    layer_norm_bias,
    w_expand,
    b_expand,
    w_reduce,
    b_reduce,
    layer_scale,
):
    channels, row_count, col_count = image.shape
    panel_rows = w_expand.shape[0] // lax.axis_size("filt")
    tok_count = row_count * col_count
    padded = padded_2(image, (("space", 1), ("filt", 2)), 3, 1)
    conv = depthwise(padded, kernel, row_count, col_count)
    conv = conv + dw_bias[:, None, None]
    flat = conv.reshape(channels, tok_count)
    average = jnp.mean(flat, axis=0, keepdims=True)
    mean_removed = flat - average
    inverse_deviation = lax.rsqrt(
        jnp.mean(mean_removed * mean_removed, axis=0, keepdims=True) + 1e-06
    )
    standardized_input = mean_removed * inverse_deviation
    normalized_input = (
        standardized_input * layer_norm_gain[:, None] + layer_norm_bias[:, None]
    ).astype(jnp.bfloat16)
    hidden = (
        jnp.dot(w_expand, normalized_input, preferred_element_type=jnp.float32)
        + b_expand.astype(jnp.float32)[:, None]
    )
    active = gelu_exact(hidden).astype(jnp.bfloat16)
    branch = (
        lax.dot_general(
            w_reduce, active, (((0,), (0,)), ((), ())), preferred_element_type=jnp.float32
        )
        + b_reduce[:, None]
    )
    resid = image.reshape(channels, tok_count).astype(jnp.float32)
    output = (
        (resid + layer_scale[:, None] * branch)
        .astype(jnp.bfloat16)
        .reshape(channels, row_count, col_count)
    )
    cot_flat = cotangent.reshape(channels, tok_count).astype(jnp.float32)
    scaled = layer_scale[:, None] * cot_flat
    g_scale = jnp.sum(cot_flat * branch, axis=1)
    g_rbias = jnp.sum(scaled, axis=1)
    d_branch = scaled.astype(jnp.bfloat16)
    g_reduce = lax.dot_general(
        active, d_branch, (((1,), (1,)), ((), ())), preferred_element_type=jnp.float32
    )
    d_active = jnp.dot(w_reduce, d_branch, preferred_element_type=jnp.float32)
    d_hidden = (d_active * gelu_slope(hidden)).astype(jnp.bfloat16)
    g_ebias = jnp.sum(d_hidden.astype(jnp.float32), axis=1)
    g_expand = lax.dot_general(
        d_hidden, normalized_input, (((1,), (1,)), ((), ())), preferred_element_type=jnp.float32
    )
    normalized_gradient = lax.dot_general(
        w_expand, d_hidden, (((0,), (0,)), ((), ())), preferred_element_type=jnp.float32
    )
    norm_gain_gradient = jnp.sum(normalized_gradient * standardized_input, axis=1)
    g_lbias = jnp.sum(normalized_gradient, axis=1)
    standardized_gradient = normalized_gradient * layer_norm_gain[:, None]
    convolution_gradient = inverse_deviation * (
        standardized_gradient
        - jnp.mean(standardized_gradient, axis=0, keepdims=True)
        - standardized_input
        * jnp.mean(standardized_gradient * standardized_input, axis=0, keepdims=True)
    )
    convolution_gradient = convolution_gradient.astype(jnp.bfloat16).reshape(
        channels, row_count, col_count
    )
    d_float = convolution_gradient.astype(jnp.float32)
    g_dbias = jnp.sum(d_float, axis=(1, 2))
    g_kernel = kernel_terms(padded, convolution_gradient, row_count, col_count)
    factor = 1.0 / math.sqrt(tok_count * lax.axis_size("space") * lax.axis_size("filt"))
    parts = lax.axis_size("filt")
    panels = jnp.concatenate(
        [
            g_reduce.reshape(parts, panel_rows * channels),
            g_expand.reshape(parts, panel_rows * channels),
            g_ebias.reshape(parts, panel_rows),
        ],
        axis=1,
    )
    small = jnp.concatenate(
        [
            g_kernel.reshape(-1),
            g_dbias,
            norm_gain_gradient,
            g_lbias,
            g_scale,
            g_rbias,
        ]
    )
    panel, small, got = grad_reduce(panels, small, convolution_gradient)
    padded_grad = _assemble(convolution_gradient, got, 3)
    back = conv_back(padded_grad, kernel, row_count, col_count)
    image_grad = (cotangent.astype(jnp.float32) + back).astype(jnp.bfloat16)
    total = jnp.concatenate([panel, small])
    total = total * factor
    cut = [panel_rows * channels, panel_rows * channels, panel_rows]
    g_reduce = total[: cut[0]].reshape(panel_rows, channels)
    g_expand = total[cut[0] : cut[0] + cut[1]].reshape(panel_rows, channels)
    g_ebias = total[cut[0] + cut[1] : sum(cut)]
    rest = total[sum(cut) :]
    ksq = kernel.shape[1] * kernel.shape[2]
    g_kernel = rest[: channels * ksq].reshape(kernel.shape)
    g_dbias, norm_gain_gradient, g_lbias, g_scale, g_rbias = (
        rest[channels * ksq + channels * i : channels * ksq + channels * (i + 1)]
        for i in range(5)
    )
    return (
        output,
        image_grad,
        g_kernel,
        g_dbias,
        norm_gain_gradient,
        g_lbias,
        g_expand,
        g_ebias,
        g_reduce,
        g_rbias,
        g_scale,
    )


def _rows(length):
    return -(-length // (8 * LANES)) * 8


def _flip(index, bit):
    return index + bit - 2 * bit * ((index // bit) % 2)


def reduce_kernel(nfilt, nspace, pr, sr, cols, buf_ref, x_ref, out_ref, *refs):
    levels = nfilt.bit_length() - 1
    steps = nspace.bit_length() - 1
    halo_outs = refs[:8]
    scratch = refs[8:]
    recvs = scratch[:levels]
    stages = scratch[levels : 2 * levels]
    recv_s, send_sem, recv_sem = scratch[2 * levels : 2 * levels + 3]
    halo = scratch[2 * levels + 3 :]
    halo_signal, halo_start, halo_finish = _halo_ops(
        nspace, nfilt, cols, x_ref, halo_outs, halo[:8], halo[8], halo[9]
    )
    s = lax.axis_index("space")
    f = lax.axis_index("filt")

    peers = []
    bit = nfilt // 2
    while bit >= 1:
        peers.append((s, _flip(f, bit)))
        bit //= 2
    for k in range(steps):
        peers.append((_flip(s, 1 << k), f))
    barrier = pltpu.get_barrier_semaphore()
    for peer in peers:
        pl.semaphore_signal(barrier, inc=1, device_id=peer, device_id_type=MESH)
    count = halo_signal(barrier)
    pl.semaphore_wait(barrier, count + len(peers))
    halo_start()

    held = buf_ref
    count = nfilt
    bit = nfilt // 2
    sem = 0
    for level in range(levels):
        half = count // 2
        upper = (f // bit) % 2
        rows = half * pr
        peer = peers[level]
        send_panels = pltpu.make_async_remote_copy(
            src_ref=held.at[pl.ds(pl.multiple_of((1 - upper) * rows, 8), rows)],
            dst_ref=recvs[level].at[pl.ds(0, rows)],
            send_sem=send_sem.at[sem],
            recv_sem=recv_sem.at[sem],
            device_id=peer,
            device_id_type=MESH,
        )
        send_small = pltpu.make_async_remote_copy(
            src_ref=held.at[pl.ds(count * pr, sr)],
            dst_ref=recvs[level].at[pl.ds(rows, sr)],
            send_sem=send_sem.at[sem + 1],
            recv_sem=recv_sem.at[sem + 1],
            device_id=peer,
            device_id_type=MESH,
        )
        send_panels.start()
        send_small.start()
        send_panels.wait()
        send_small.wait()
        sem += 2
        stage = stages[level]
        stage[pl.ds(0, rows)] = (
            held[pl.ds(pl.multiple_of(upper * rows, 8), rows)] + recvs[level][pl.ds(0, rows)]
        )
        stage[pl.ds(rows, sr)] = held[pl.ds(count * pr, sr)] + recvs[level][pl.ds(rows, sr)]
        held = stage
        count = half
        bit //= 2

    if levels == 0:
        out_ref[...] = buf_ref[...]
    else:
        out_ref[...] = held[...]
    for k in range(steps):
        copy = pltpu.make_async_remote_copy(
            src_ref=out_ref,
            dst_ref=recv_s.at[k],
            send_sem=send_sem.at[sem],
            recv_sem=recv_sem.at[sem],
            device_id=peers[levels + k],
            device_id_type=MESH,
        )
        copy.start()
        copy.wait()
        sem += 1
        out_ref[...] = out_ref[...] + recv_s[k]
    halo_finish()


def grad_reduce(panels, small, x):
    nfilt = lax.axis_size("filt")
    nspace = lax.axis_size("space")
    width = panels.shape[1]
    pr = _rows(width)
    sr = _rows(small.shape[0])
    buf = jnp.concatenate(
        [
            jnp.pad(panels, ((0, 0), (0, pr * LANES - width))).reshape(nfilt * pr, LANES),
            jnp.pad(small, (0, sr * LANES - small.shape[0])).reshape(sr, LANES),
        ]
    )
    levels = nfilt.bit_length() - 1
    steps = nspace.bit_length() - 1
    scratch = []
    count = nfilt
    for _ in range(levels):
        count //= 2
        scratch.append(pltpu.VMEM((count * pr + sr, LANES), jnp.float32))
    count = nfilt
    for _ in range(levels):
        count //= 2
        scratch.append(pltpu.VMEM((count * pr + sr, LANES), jnp.float32))
    ncopies = 2 * levels + steps
    scratch += [
        pltpu.VMEM((max(steps, 1), pr + sr, LANES), jnp.float32),
        pltpu.SemaphoreType.DMA((ncopies,)),
        pltpu.SemaphoreType.DMA((ncopies,)),
    ]
    shapes = _halo_shapes(x)
    scratch += [pltpu.VMEM(sh.shape, sh.dtype) for sh in shapes]
    scratch += [pltpu.SemaphoreType.DMA((8,)), pltpu.SemaphoreType.DMA((8,))]
    out, *got = pl.pallas_call(
        functools.partial(reduce_kernel, nfilt, nspace, pr, sr, x.shape[2]),
        out_shape=[jax.ShapeDtypeStruct((pr + sr, LANES), jnp.float32)] + shapes,
        in_specs=[pl.BlockSpec(memory_space=pltpu.VMEM)] * 2,
        out_specs=[pl.BlockSpec(memory_space=pltpu.VMEM)] * 9,
        scratch_shapes=scratch,
        compiler_params=pltpu.CompilerParams(collective_id=0, has_side_effects=True),
        cost_estimate=pl.CostEstimate(
            flops=0, transcendentals=0, bytes_accessed=200 * 1024 * 1024
        ),
    )(buf, x)
    panel = out[:pr].reshape(-1)[:width]
    small = out[pr:].reshape(-1)[: small.shape[0]]
    return panel, small, got


def solution(mesh):
    in_specs = (
        P(None, "space", "filt"),
        P(None, "space", "filt"),
        P(),
        P(),
        P(),
        P(),
        P(),
        P(),
        P(),
        P(),
        P(),
    )
    out_specs = (
        P(None, "space", "filt"),
        P(None, "space", "filt"),
        P(),
        P(),
        P(),
        P(),
        P("filt", None),
        P("filt"),
        P("filt", None),
        P(),
        P(),
    )
    return jax.shard_map(shards, mesh=mesh, in_specs=in_specs, out_specs=out_specs, check_vma=False)
```

```python
import functools
import math

import jax
import jax.numpy as jnp
from jax import lax
from jax.experimental import pallas as pl
from jax.experimental.pallas import tpu as pltpu
from jax.sharding import PartitionSpec as P

MESH = pl.DeviceIdType.MESH
LANES = 128


_DIRS = [(-1, 0), (1, 0), (0, -1), (0, 1), (-1, -1), (-1, 1), (1, -1), (1, 1)]


def _lanes(df, cols):
    if df == 0:
        return slice(0, cols)
    if df > 0:
        return slice(cols - LANES, cols)
    return slice(0, LANES)


def _halo_ops(ns, nf, cols, x_ref, outs, slots, send_sem, recv_sem):
    s = lax.axis_index("space")
    f = lax.axis_index("filt")

    def exists(d):
        t, g = s + d[0], f + d[1]
        return (t >= 0) & (t < ns) & (g >= 0) & (g < nf)

    def desc(k):
        d = _DIRS[k]
        back = _DIRS.index((-d[0], -d[1]))
        return pltpu.make_async_remote_copy(
            src_ref=x_ref.at[:, :, _lanes(d[1], cols)],
            dst_ref=slots[back],
            send_sem=send_sem.at[k],
            recv_sem=recv_sem.at[back],
            device_id=(s + d[0], f + d[1]),
            device_id_type=MESH,
        )

    def signal(barrier):
        count = 0
        for d in _DIRS:

            @pl.when(exists(d))
            def _():
                pl.semaphore_signal(
                    barrier, inc=1, device_id=(s + d[0], f + d[1]), device_id_type=MESH
                )

            count = count + exists(d).astype(jnp.int32)
        return count

    def start():
        for k, d in enumerate(_DIRS):

            @pl.when(exists(d))
            def _():
                desc(k).start()

    def finish():
        for k, d in enumerate(_DIRS):
            back = _DIRS.index((-d[0], -d[1]))

            @pl.when(exists(d))
            def _():
                desc(k).wait_send()
                desc(back).wait_recv()
                outs[k][...] = slots[k][...]

            @pl.when(jnp.logical_not(exists(d)))
            def _():
                outs[k][...] = jnp.zeros(outs[k].shape, outs[k].dtype)

    return signal, start, finish


def halo_kernel(ns, nf, cols, x_ref, *refs):
    signal, start, finish = _halo_ops(ns, nf, cols, x_ref, refs[:8], refs[8:16], *refs[16:])
    barrier = pltpu.get_barrier_semaphore()
    pl.semaphore_wait(barrier, signal(barrier))
    start()
    finish()


def _halo_shapes(x):
    channels, rows, cols = x.shape
    return [
        jax.ShapeDtypeStruct((channels, rows, _lanes(d[1], cols).stop - _lanes(d[1], cols).start), x.dtype)
        for d in _DIRS
    ]


def _assemble(x, got, width):
    rows = x.shape[1]
    piece = dict(zip(_DIRS, got))
    hi_r, lo_r = slice(rows - width, rows), slice(0, width)
    above = piece[(-1, 0)][:, hi_r, :]
    below = piece[(1, 0)][:, lo_r, :]
    lw = piece[(0, -1)].shape[2]
    left = piece[(0, -1)][:, :, lw - width : lw]
    right = piece[(0, 1)][:, :, 0:width]
    top_left = piece[(-1, -1)][:, hi_r, lw - width : lw]
    top_right = piece[(-1, 1)][:, hi_r, 0:width]
    bottom_left = piece[(1, -1)][:, lo_r, lw - width : lw]
    bottom_right = piece[(1, 1)][:, lo_r, 0:width]
    return jnp.concatenate(
        [
            jnp.concatenate([top_left, above, top_right], axis=2),
            jnp.concatenate([left, x, right], axis=2),
            jnp.concatenate([bottom_left, below, bottom_right], axis=2),
        ],
        axis=1,
    )


def padded_2(x, sides, width, collective_id):
    del sides
    ns, nf = lax.axis_size("space"), lax.axis_size("filt")
    shapes = _halo_shapes(x)
    got = pl.pallas_call(
        functools.partial(halo_kernel, ns, nf, x.shape[2]),
        out_shape=shapes,
        in_specs=[pl.BlockSpec(memory_space=pltpu.VMEM)],
        out_specs=[pl.BlockSpec(memory_space=pltpu.VMEM)] * 8,
        scratch_shapes=[pltpu.VMEM(sh.shape, sh.dtype) for sh in shapes]
        + [pltpu.SemaphoreType.DMA((8,)), pltpu.SemaphoreType.DMA((8,))],
        compiler_params=pltpu.CompilerParams(
            collective_id=collective_id, has_side_effects=True
        ),
    )(x)
    return _assemble(x, got, width)


def dw_kernel(flip, cb, x_ref, k_ref, o_ref):
    rows, channels, cols = o_ref.shape
    wide = x_ref.shape[2]

    def block(i, carry):
        ch = pl.ds(pl.multiple_of(i * cb, cb), cb)
        x = x_ref[:, ch, :]
        acc = jnp.zeros((rows, cb, cols), jnp.float32)
        for shift_col in range(7):
            c0 = 6 - shift_col if flip else shift_col
            xb = pltpu.roll(x, shift=wide - c0, axis=2) if c0 else x
            xb = xb[:, :, :cols]
            for shift_row in range(7):
                r0 = 6 - shift_row if flip else shift_row
                kv = k_ref[shift_row * 7 + shift_col, ch, :]
                acc = acc + kv[None] * xb[r0 : r0 + rows]
        o_ref[:, ch, :] = acc
        return carry

    lax.fori_loop(0, channels // cb, block, 0)


def _dw(padded, kernel, row_count, col_count, flip):
    channels = padded.shape[0]
    wide = -(-padded.shape[2] // LANES) * LANES
    x = jnp.transpose(padded, (1, 0, 2)).astype(jnp.float32)
    x = jnp.pad(x, ((0, 0), (0, 0), (0, wide - padded.shape[2])))
    taps = jnp.transpose(kernel.reshape(channels, 49), (1, 0))[:, :, None]
    cb = 8
    out = pl.pallas_call(
        functools.partial(dw_kernel, flip, cb),
        out_shape=jax.ShapeDtypeStruct((row_count, channels, col_count), jnp.float32),
        in_specs=[pl.BlockSpec(memory_space=pltpu.VMEM)] * 2,
        out_specs=pl.BlockSpec(memory_space=pltpu.VMEM),
    )(x, taps)
    return jnp.transpose(out, (1, 0, 2))


def depthwise(padded, kernel, row_count, col_count):
    return _dw(padded, kernel, row_count, col_count, False)


def conv_back(padded, kernel, row_count, col_count):
    return _dw(padded, kernel, row_count, col_count, True)


def kernel_terms(padded, convolution_gradient, row_count, col_count):
    ksize = 7
    columns = []
    for shift_col in range(ksize):
        corr = jnp.einsum(
            "crj,cij->cri",
            padded[:, :, shift_col : shift_col + col_count],
            convolution_gradient,
            preferred_element_type=jnp.float32,
        )
        total = corr[:, 0:ksize, 0]
        for row in range(1, row_count):
            total = total + corr[:, row : row + ksize, row]
        columns.append(total)
    return jnp.stack(columns, axis=2)


def gelu_exact(value):
    return value * (1.0 + jax.scipy.special.erf(value / math.sqrt(2.0))) * 0.5


def gelu_slope(value):
    return (1.0 + jax.scipy.special.erf(value / math.sqrt(2.0))) * 0.5 + value * jnp.exp(
        -0.5 * value * value
    ) / math.sqrt(2.0 * math.pi)


def shards(
    image,
    cotangent,
    kernel,
    dw_bias,
    layer_norm_gain,
    layer_norm_bias,
    w_expand,
    b_expand,
    w_reduce,
    b_reduce,
    layer_scale,
):
    channels, row_count, col_count = image.shape
    panel_rows = w_expand.shape[0] // lax.axis_size("filt")
    tok_count = row_count * col_count
    padded = padded_2(image, (("space", 1), ("filt", 2)), 3, 1)
    conv = depthwise(padded, kernel, row_count, col_count)
    conv = conv + dw_bias[:, None, None]
    flat = conv.reshape(channels, tok_count)
    average = jnp.mean(flat, axis=0, keepdims=True)
    mean_removed = flat - average
    inverse_deviation = lax.rsqrt(
        jnp.mean(mean_removed * mean_removed, axis=0, keepdims=True) + 1e-06
    )
    standardized_input = mean_removed * inverse_deviation
    normalized_input = (
        standardized_input * layer_norm_gain[:, None] + layer_norm_bias[:, None]
    ).astype(jnp.bfloat16)
    hidden = (
        jnp.dot(w_expand, normalized_input, preferred_element_type=jnp.float32)
        + b_expand.astype(jnp.float32)[:, None]
    )
    active = gelu_exact(hidden).astype(jnp.bfloat16)
    branch = (
        lax.dot_general(
            w_reduce, active, (((0,), (0,)), ((), ())), preferred_element_type=jnp.float32
        )
        + b_reduce[:, None]
    )
    resid = image.reshape(channels, tok_count).astype(jnp.float32)
    output = (
        (resid + layer_scale[:, None] * branch)
        .astype(jnp.bfloat16)
        .reshape(channels, row_count, col_count)
    )
    cot_flat = cotangent.reshape(channels, tok_count).astype(jnp.float32)
    scaled = layer_scale[:, None] * cot_flat
    g_scale = jnp.sum(cot_flat * branch, axis=1)
    g_rbias = jnp.sum(scaled, axis=1)
    d_branch = scaled.astype(jnp.bfloat16)
    g_reduce = lax.dot_general(
        active, d_branch, (((1,), (1,)), ((), ())), preferred_element_type=jnp.float32
    )
    d_active = jnp.dot(w_reduce, d_branch, preferred_element_type=jnp.float32)
    d_hidden = (d_active * gelu_slope(hidden)).astype(jnp.bfloat16)
    g_ebias = jnp.sum(d_hidden.astype(jnp.float32), axis=1)
    g_expand = lax.dot_general(
        d_hidden, normalized_input, (((1,), (1,)), ((), ())), preferred_element_type=jnp.float32
    )
    normalized_gradient = lax.dot_general(
        w_expand, d_hidden, (((0,), (0,)), ((), ())), preferred_element_type=jnp.float32
    )
    norm_gain_gradient = jnp.sum(normalized_gradient * standardized_input, axis=1)
    g_lbias = jnp.sum(normalized_gradient, axis=1)
    standardized_gradient = normalized_gradient * layer_norm_gain[:, None]
    convolution_gradient = inverse_deviation * (
        standardized_gradient
        - jnp.mean(standardized_gradient, axis=0, keepdims=True)
        - standardized_input
        * jnp.mean(standardized_gradient * standardized_input, axis=0, keepdims=True)
    )
    convolution_gradient = convolution_gradient.astype(jnp.bfloat16).reshape(
        channels, row_count, col_count
    )
    d_float = convolution_gradient.astype(jnp.float32)
    g_dbias = jnp.sum(d_float, axis=(1, 2))
    g_kernel = kernel_terms(padded, convolution_gradient, row_count, col_count)
    factor = 1.0 / math.sqrt(tok_count * lax.axis_size("space") * lax.axis_size("filt"))
    parts = lax.axis_size("filt")
    panels = jnp.concatenate(
        [
            g_reduce.reshape(parts, panel_rows * channels),
            g_expand.reshape(parts, panel_rows * channels),
            g_ebias.reshape(parts, panel_rows),
        ],
        axis=1,
    )
    small = jnp.concatenate(
        [
            g_kernel.reshape(-1),
            g_dbias,
            norm_gain_gradient,
            g_lbias,
            g_scale,
            g_rbias,
        ]
    )
    panel, small, got = grad_reduce(panels, small, convolution_gradient)
    padded_grad = _assemble(convolution_gradient, got, 3)
    back = conv_back(padded_grad, kernel, row_count, col_count)
    image_grad = (cotangent.astype(jnp.float32) + back).astype(jnp.bfloat16)
    total = jnp.concatenate([panel, small])
    total = total * factor
    cut = [panel_rows * channels, panel_rows * channels, panel_rows]
    g_reduce = total[: cut[0]].reshape(panel_rows, channels)
    g_expand = total[cut[0] : cut[0] + cut[1]].reshape(panel_rows, channels)
    g_ebias = total[cut[0] + cut[1] : sum(cut)]
    rest = total[sum(cut) :]
    ksq = kernel.shape[1] * kernel.shape[2]
    g_kernel = rest[: channels * ksq].reshape(kernel.shape)
    g_dbias, norm_gain_gradient, g_lbias, g_scale, g_rbias = (
        rest[channels * ksq + channels * i : channels * ksq + channels * (i + 1)]
        for i in range(5)
    )
    return (
        output,
        image_grad,
        g_kernel,
        g_dbias,
        norm_gain_gradient,
        g_lbias,
        g_expand,
        g_ebias,
        g_reduce,
        g_rbias,
        g_scale,
    )


def _rows(length):
    return -(-length // (8 * LANES)) * 8


def _flip(index, bit):
    return index + bit - 2 * bit * ((index // bit) % 2)


def reduce_kernel(nfilt, nspace, pr, sr, cols, buf_ref, x_ref, out_ref, *refs):
    levels = nfilt.bit_length() - 1
    steps = nspace.bit_length() - 1
    halo_outs = refs[:8]
    scratch = refs[8:]
    recvs = scratch[:levels]
    stages = scratch[levels : 2 * levels]
    recv_s, send_sem, recv_sem = scratch[2 * levels : 2 * levels + 3]
    halo = scratch[2 * levels + 3 :]
    halo_signal, halo_start, halo_finish = _halo_ops(
        nspace, nfilt, cols, x_ref, halo_outs, halo[:8], halo[8], halo[9]
    )
    s = lax.axis_index("space")
    f = lax.axis_index("filt")

    peers = []
    bit = nfilt // 2
    while bit >= 1:
        peers.append((s, _flip(f, bit)))
        bit //= 2
    for k in range(steps):
        peers.append((_flip(s, 1 << k), f))
    barrier = pltpu.get_barrier_semaphore()
    for peer in peers:
        pl.semaphore_signal(barrier, inc=1, device_id=peer, device_id_type=MESH)
    count = halo_signal(barrier)
    pl.semaphore_wait(barrier, count + len(peers))
    halo_start()

    held = buf_ref
    count = nfilt
    bit = nfilt // 2
    sem = 0
    for level in range(levels):
        half = count // 2
        upper = (f // bit) % 2
        rows = half * pr
        peer = peers[level]
        send_panels = pltpu.make_async_remote_copy(
            src_ref=held.at[pl.ds(pl.multiple_of((1 - upper) * rows, 8), rows)],
            dst_ref=recvs[level].at[pl.ds(0, rows)],
            send_sem=send_sem.at[sem],
            recv_sem=recv_sem.at[sem],
            device_id=peer,
            device_id_type=MESH,
        )
        send_small = pltpu.make_async_remote_copy(
            src_ref=held.at[pl.ds(count * pr, sr)],
            dst_ref=recvs[level].at[pl.ds(rows, sr)],
            send_sem=send_sem.at[sem + 1],
            recv_sem=recv_sem.at[sem + 1],
            device_id=peer,
            device_id_type=MESH,
        )
        send_panels.start()
        send_small.start()
        send_panels.wait()
        send_small.wait()
        sem += 2
        stage = stages[level]
        stage[pl.ds(0, rows)] = (
            held[pl.ds(pl.multiple_of(upper * rows, 8), rows)] + recvs[level][pl.ds(0, rows)]
        )
        stage[pl.ds(rows, sr)] = held[pl.ds(count * pr, sr)] + recvs[level][pl.ds(rows, sr)]
        held = stage
        count = half
        bit //= 2

    if levels == 0:
        out_ref[...] = buf_ref[...]
    else:
        out_ref[...] = held[...]
    for k in range(steps):
        copy = pltpu.make_async_remote_copy(
            src_ref=out_ref,
            dst_ref=recv_s.at[k],
            send_sem=send_sem.at[sem],
            recv_sem=recv_sem.at[sem],
            device_id=peers[levels + k],
            device_id_type=MESH,
        )
        copy.start()
        copy.wait()
        sem += 1
        out_ref[...] = out_ref[...] + recv_s[k]
    halo_finish()


def grad_reduce(panels, small, x):
    nfilt = lax.axis_size("filt")
    nspace = lax.axis_size("space")
    width = panels.shape[1]
    pr = _rows(width)
    sr = _rows(small.shape[0])
    buf = jnp.concatenate(
        [
            jnp.pad(panels, ((0, 0), (0, pr * LANES - width))).reshape(nfilt * pr, LANES),
            jnp.pad(small, (0, sr * LANES - small.shape[0])).reshape(sr, LANES),
        ]
    )
    levels = nfilt.bit_length() - 1
    steps = nspace.bit_length() - 1
    scratch = []
    count = nfilt
    for _ in range(levels):
        count //= 2
        scratch.append(pltpu.VMEM((count * pr + sr, LANES), jnp.float32))
    count = nfilt
    for _ in range(levels):
        count //= 2
        scratch.append(pltpu.VMEM((count * pr + sr, LANES), jnp.float32))
    ncopies = 2 * levels + steps
    scratch += [
        pltpu.VMEM((max(steps, 1), pr + sr, LANES), jnp.float32),
        pltpu.SemaphoreType.DMA((ncopies,)),
        pltpu.SemaphoreType.DMA((ncopies,)),
    ]
    shapes = _halo_shapes(x)
    scratch += [pltpu.VMEM(sh.shape, sh.dtype) for sh in shapes]
    scratch += [pltpu.SemaphoreType.DMA((8,)), pltpu.SemaphoreType.DMA((8,))]
    out, *got = pl.pallas_call(
        functools.partial(reduce_kernel, nfilt, nspace, pr, sr, x.shape[2]),
        out_shape=[jax.ShapeDtypeStruct((pr + sr, LANES), jnp.float32)] + shapes,
        in_specs=[pl.BlockSpec(memory_space=pltpu.VMEM)] * 2,
        out_specs=[pl.BlockSpec(memory_space=pltpu.VMEM)] * 9,
        scratch_shapes=scratch,
        compiler_params=pltpu.CompilerParams(collective_id=0, has_side_effects=True),
        cost_estimate=pl.CostEstimate(
            flops=0, transcendentals=0, bytes_accessed=200 * 1024 * 1024
        ),
    )(buf, x)
    panel = out[:pr].reshape(-1)[:width]
    small = out[pr:].reshape(-1)[: small.shape[0]]
    return panel, small, got


def solution(mesh):
    in_specs = (
        P(None, "space", "filt"),
        P(None, "space", "filt"),
        P(),
        P(),
        P(),
        P(),
        P(),
        P(),
        P(),
        P(),
        P(),
    )
    out_specs = (
        P(None, "space", "filt"),
        P(None, "space", "filt"),
        P(),
        P(),
        P(),
        P(),
        P("filt", None),
        P("filt"),
        P("filt", None),
        P(),
        P(),
    )
    return jax.shard_map(shards, mesh=mesh, in_specs=in_specs, out_specs=out_specs, check_vma=False)
```

```python
import functools
import math

import jax
import jax.numpy as jnp
from jax import lax
from jax.experimental import pallas as pl
from jax.experimental.pallas import tpu as pltpu
from jax.sharding import PartitionSpec as P

MESH = pl.DeviceIdType.MESH
LANES = 128


_DIRS = [(-1, 0), (1, 0), (0, -1), (0, 1), (-1, -1), (-1, 1), (1, -1), (1, 1)]


def _lanes(df, cols):
    if df == 0:
        return slice(0, cols)
    if df > 0:
        return slice(cols - LANES, cols)
    return slice(0, LANES)


def _halo_ops(ns, nf, cols, x_ref, outs, slots, send_sem, recv_sem):
    s = lax.axis_index("space")
    f = lax.axis_index("filt")

    def exists(d):
        t, g = s + d[0], f + d[1]
        return (t >= 0) & (t < ns) & (g >= 0) & (g < nf)

    def desc(k):
        d = _DIRS[k]
        back = _DIRS.index((-d[0], -d[1]))
        return pltpu.make_async_remote_copy(
            src_ref=x_ref.at[:, :, _lanes(d[1], cols)],
            dst_ref=slots[back],
            send_sem=send_sem.at[k],
            recv_sem=recv_sem.at[back],
            device_id=(s + d[0], f + d[1]),
            device_id_type=MESH,
        )

    def signal(barrier):
        count = 0
        for d in _DIRS:

            @pl.when(exists(d))
            def _():
                pl.semaphore_signal(
                    barrier, inc=1, device_id=(s + d[0], f + d[1]), device_id_type=MESH
                )

            count = count + exists(d).astype(jnp.int32)
        return count

    def start():
        for k, d in enumerate(_DIRS):

            @pl.when(exists(d))
            def _():
                desc(k).start()

    def finish():
        for k, d in enumerate(_DIRS):
            back = _DIRS.index((-d[0], -d[1]))

            @pl.when(exists(d))
            def _():
                desc(k).wait_send()
                desc(back).wait_recv()
                outs[k][...] = slots[k][...]

            @pl.when(jnp.logical_not(exists(d)))
            def _():
                outs[k][...] = jnp.zeros(outs[k].shape, outs[k].dtype)

    return signal, start, finish


def halo_kernel(ns, nf, cols, x_ref, *refs):
    signal, start, finish = _halo_ops(ns, nf, cols, x_ref, refs[:8], refs[8:16], *refs[16:])
    barrier = pltpu.get_barrier_semaphore()
    pl.semaphore_wait(barrier, signal(barrier))
    start()
    finish()


def _halo_shapes(x):
    channels, rows, cols = x.shape
    return [
        jax.ShapeDtypeStruct((channels, rows, _lanes(d[1], cols).stop - _lanes(d[1], cols).start), x.dtype)
        for d in _DIRS
    ]


def _assemble(x, got, width):
    rows = x.shape[1]
    piece = dict(zip(_DIRS, got))
    hi_r, lo_r = slice(rows - width, rows), slice(0, width)
    above = piece[(-1, 0)][:, hi_r, :]
    below = piece[(1, 0)][:, lo_r, :]
    lw = piece[(0, -1)].shape[2]
    left = piece[(0, -1)][:, :, lw - width : lw]
    right = piece[(0, 1)][:, :, 0:width]
    top_left = piece[(-1, -1)][:, hi_r, lw - width : lw]
    top_right = piece[(-1, 1)][:, hi_r, 0:width]
    bottom_left = piece[(1, -1)][:, lo_r, lw - width : lw]
    bottom_right = piece[(1, 1)][:, lo_r, 0:width]
    return jnp.concatenate(
        [
            jnp.concatenate([top_left, above, top_right], axis=2),
            jnp.concatenate([left, x, right], axis=2),
            jnp.concatenate([bottom_left, below, bottom_right], axis=2),
        ],
        axis=1,
    )


def padded_2(x, sides, width, collective_id):
    del sides
    ns, nf = lax.axis_size("space"), lax.axis_size("filt")
    shapes = _halo_shapes(x)
    got = pl.pallas_call(
        functools.partial(halo_kernel, ns, nf, x.shape[2]),
        out_shape=shapes,
        in_specs=[pl.BlockSpec(memory_space=pltpu.VMEM)],
        out_specs=[pl.BlockSpec(memory_space=pltpu.VMEM)] * 8,
        scratch_shapes=[pltpu.VMEM(sh.shape, sh.dtype) for sh in shapes]
        + [pltpu.SemaphoreType.DMA((8,)), pltpu.SemaphoreType.DMA((8,))],
        compiler_params=pltpu.CompilerParams(
            collective_id=collective_id, has_side_effects=True
        ),
    )(x)
    return _assemble(x, got, width)


def dw_kernel(flip, cb, x_ref, k_ref, o_ref):
    rows, channels, cols = o_ref.shape
    wide = x_ref.shape[2]

    def block(i, carry):
        ch = pl.ds(pl.multiple_of(i * cb, cb), cb)
        x = x_ref[:, ch, :]
        acc = jnp.zeros((rows, cb, cols), jnp.float32)
        for shift_col in range(7):
            c0 = 6 - shift_col if flip else shift_col
            xb = pltpu.roll(x, shift=wide - c0, axis=2) if c0 else x
            xb = xb[:, :, :cols]
            for shift_row in range(7):
                r0 = 6 - shift_row if flip else shift_row
                kv = k_ref[ch, pl.ds(shift_row * 7 + shift_col, 1)]
                acc = acc + kv[None] * xb[r0 : r0 + rows]
        o_ref[:, ch, :] = acc
        return carry

    lax.fori_loop(0, channels // cb, block, 0)


def _dw(padded, kernel, row_count, col_count, flip):
    channels = padded.shape[0]
    wide = -(-padded.shape[2] // LANES) * LANES
    x = jnp.transpose(padded, (1, 0, 2)).astype(jnp.float32)
    x = jnp.pad(x, ((0, 0), (0, 0), (0, wide - padded.shape[2])))
    taps = kernel.reshape(channels, 49)
    cb = 8
    out = pl.pallas_call(
        functools.partial(dw_kernel, flip, cb),
        out_shape=jax.ShapeDtypeStruct((row_count, channels, col_count), jnp.float32),
        in_specs=[pl.BlockSpec(memory_space=pltpu.VMEM)] * 2,
        out_specs=pl.BlockSpec(memory_space=pltpu.VMEM),
    )(x, taps)
    return jnp.transpose(out, (1, 0, 2))


def depthwise(padded, kernel, row_count, col_count):
    return _dw(padded, kernel, row_count, col_count, False)


def conv_back(padded, kernel, row_count, col_count):
    return _dw(padded, kernel, row_count, col_count, True)


def kernel_terms(padded, convolution_gradient, row_count, col_count):
    ksize = 7
    columns = []
    for shift_col in range(ksize):
        corr = jnp.einsum(
            "crj,cij->cri",
            padded[:, :, shift_col : shift_col + col_count],
            convolution_gradient,
            preferred_element_type=jnp.float32,
        )
        total = corr[:, 0:ksize, 0]
        for row in range(1, row_count):
            total = total + corr[:, row : row + ksize, row]
        columns.append(total)
    return jnp.stack(columns, axis=2)


def gelu_exact(value):
    return value * (1.0 + jax.scipy.special.erf(value / math.sqrt(2.0))) * 0.5


def gelu_slope(value):
    return (1.0 + jax.scipy.special.erf(value / math.sqrt(2.0))) * 0.5 + value * jnp.exp(
        -0.5 * value * value
    ) / math.sqrt(2.0 * math.pi)


def shards(
    image,
    cotangent,
    kernel,
    dw_bias,
    layer_norm_gain,
    layer_norm_bias,
    w_expand,
    b_expand,
    w_reduce,
    b_reduce,
    layer_scale,
):
    channels, row_count, col_count = image.shape
    panel_rows = w_expand.shape[0] // lax.axis_size("filt")
    tok_count = row_count * col_count
    padded = padded_2(image, (("space", 1), ("filt", 2)), 3, 1)
    conv = depthwise(padded, kernel, row_count, col_count)
    conv = conv + dw_bias[:, None, None]
    flat = conv.reshape(channels, tok_count)
    average = jnp.mean(flat, axis=0, keepdims=True)
    mean_removed = flat - average
    inverse_deviation = lax.rsqrt(
        jnp.mean(mean_removed * mean_removed, axis=0, keepdims=True) + 1e-06
    )
    standardized_input = mean_removed * inverse_deviation
    normalized_input = (
        standardized_input * layer_norm_gain[:, None] + layer_norm_bias[:, None]
    ).astype(jnp.bfloat16)
    hidden = (
        jnp.dot(w_expand, normalized_input, preferred_element_type=jnp.float32)
        + b_expand.astype(jnp.float32)[:, None]
    )
    active = gelu_exact(hidden).astype(jnp.bfloat16)
    branch = (
        lax.dot_general(
            w_reduce, active, (((0,), (0,)), ((), ())), preferred_element_type=jnp.float32
        )
        + b_reduce[:, None]
    )
    resid = image.reshape(channels, tok_count).astype(jnp.float32)
    output = (
        (resid + layer_scale[:, None] * branch)
        .astype(jnp.bfloat16)
        .reshape(channels, row_count, col_count)
    )
    cot_flat = cotangent.reshape(channels, tok_count).astype(jnp.float32)
    scaled = layer_scale[:, None] * cot_flat
    g_scale = jnp.sum(cot_flat * branch, axis=1)
    g_rbias = jnp.sum(scaled, axis=1)
    d_branch = scaled.astype(jnp.bfloat16)
    g_reduce = lax.dot_general(
        active, d_branch, (((1,), (1,)), ((), ())), preferred_element_type=jnp.float32
    )
    d_active = jnp.dot(w_reduce, d_branch, preferred_element_type=jnp.float32)
    d_hidden = (d_active * gelu_slope(hidden)).astype(jnp.bfloat16)
    g_ebias = jnp.sum(d_hidden.astype(jnp.float32), axis=1)
    g_expand = lax.dot_general(
        d_hidden, normalized_input, (((1,), (1,)), ((), ())), preferred_element_type=jnp.float32
    )
    normalized_gradient = lax.dot_general(
        w_expand, d_hidden, (((0,), (0,)), ((), ())), preferred_element_type=jnp.float32
    )
    norm_gain_gradient = jnp.sum(normalized_gradient * standardized_input, axis=1)
    g_lbias = jnp.sum(normalized_gradient, axis=1)
    standardized_gradient = normalized_gradient * layer_norm_gain[:, None]
    convolution_gradient = inverse_deviation * (
        standardized_gradient
        - jnp.mean(standardized_gradient, axis=0, keepdims=True)
        - standardized_input
        * jnp.mean(standardized_gradient * standardized_input, axis=0, keepdims=True)
    )
    convolution_gradient = convolution_gradient.astype(jnp.bfloat16).reshape(
        channels, row_count, col_count
    )
    d_float = convolution_gradient.astype(jnp.float32)
    g_dbias = jnp.sum(d_float, axis=(1, 2))
    g_kernel = kernel_terms(padded, convolution_gradient, row_count, col_count)
    factor = 1.0 / math.sqrt(tok_count * lax.axis_size("space") * lax.axis_size("filt"))
    parts = lax.axis_size("filt")
    panels = jnp.concatenate(
        [
            g_reduce.reshape(parts, panel_rows * channels),
            g_expand.reshape(parts, panel_rows * channels),
            g_ebias.reshape(parts, panel_rows),
        ],
        axis=1,
    )
    small = jnp.concatenate(
        [
            g_kernel.reshape(-1),
            g_dbias,
            norm_gain_gradient,
            g_lbias,
            g_scale,
            g_rbias,
        ]
    )
    panel, small, got = grad_reduce(panels, small, convolution_gradient)
    padded_grad = _assemble(convolution_gradient, got, 3)
    back = conv_back(padded_grad, kernel, row_count, col_count)
    image_grad = (cotangent.astype(jnp.float32) + back).astype(jnp.bfloat16)
    total = jnp.concatenate([panel, small])
    total = total * factor
    cut = [panel_rows * channels, panel_rows * channels, panel_rows]
    g_reduce = total[: cut[0]].reshape(panel_rows, channels)
    g_expand = total[cut[0] : cut[0] + cut[1]].reshape(panel_rows, channels)
    g_ebias = total[cut[0] + cut[1] : sum(cut)]
    rest = total[sum(cut) :]
    ksq = kernel.shape[1] * kernel.shape[2]
    g_kernel = rest[: channels * ksq].reshape(kernel.shape)
    g_dbias, norm_gain_gradient, g_lbias, g_scale, g_rbias = (
        rest[channels * ksq + channels * i : channels * ksq + channels * (i + 1)]
        for i in range(5)
    )
    return (
        output,
        image_grad,
        g_kernel,
        g_dbias,
        norm_gain_gradient,
        g_lbias,
        g_expand,
        g_ebias,
        g_reduce,
        g_rbias,
        g_scale,
    )


def _rows(length):
    return -(-length // (8 * LANES)) * 8


def _flip(index, bit):
    return index + bit - 2 * bit * ((index // bit) % 2)


def reduce_kernel(nfilt, nspace, pr, sr, cols, buf_ref, x_ref, out_ref, *refs):
    levels = nfilt.bit_length() - 1
    steps = nspace.bit_length() - 1
    halo_outs = refs[:8]
    scratch = refs[8:]
    recvs = scratch[:levels]
    stages = scratch[levels : 2 * levels]
    recv_s, send_sem, recv_sem = scratch[2 * levels : 2 * levels + 3]
    halo = scratch[2 * levels + 3 :]
    halo_signal, halo_start, halo_finish = _halo_ops(
        nspace, nfilt, cols, x_ref, halo_outs, halo[:8], halo[8], halo[9]
    )
    s = lax.axis_index("space")
    f = lax.axis_index("filt")

    peers = []
    bit = nfilt // 2
    while bit >= 1:
        peers.append((s, _flip(f, bit)))
        bit //= 2
    for k in range(steps):
        peers.append((_flip(s, 1 << k), f))
    barrier = pltpu.get_barrier_semaphore()
    for peer in peers:
        pl.semaphore_signal(barrier, inc=1, device_id=peer, device_id_type=MESH)
    count = halo_signal(barrier)
    pl.semaphore_wait(barrier, count + len(peers))
    halo_start()

    held = buf_ref
    count = nfilt
    bit = nfilt // 2
    sem = 0
    for level in range(levels):
        half = count // 2
        upper = (f // bit) % 2
        rows = half * pr
        peer = peers[level]
        send_panels = pltpu.make_async_remote_copy(
            src_ref=held.at[pl.ds(pl.multiple_of((1 - upper) * rows, 8), rows)],
            dst_ref=recvs[level].at[pl.ds(0, rows)],
            send_sem=send_sem.at[sem],
            recv_sem=recv_sem.at[sem],
            device_id=peer,
            device_id_type=MESH,
        )
        send_small = pltpu.make_async_remote_copy(
            src_ref=held.at[pl.ds(count * pr, sr)],
            dst_ref=recvs[level].at[pl.ds(rows, sr)],
            send_sem=send_sem.at[sem + 1],
            recv_sem=recv_sem.at[sem + 1],
            device_id=peer,
            device_id_type=MESH,
        )
        send_panels.start()
        send_small.start()
        send_panels.wait()
        send_small.wait()
        sem += 2
        stage = stages[level]
        stage[pl.ds(0, rows)] = (
            held[pl.ds(pl.multiple_of(upper * rows, 8), rows)] + recvs[level][pl.ds(0, rows)]
        )
        stage[pl.ds(rows, sr)] = held[pl.ds(count * pr, sr)] + recvs[level][pl.ds(rows, sr)]
        held = stage
        count = half
        bit //= 2

    if levels == 0:
        out_ref[...] = buf_ref[...]
    else:
        out_ref[...] = held[...]
    for k in range(steps):
        copy = pltpu.make_async_remote_copy(
            src_ref=out_ref,
            dst_ref=recv_s.at[k],
            send_sem=send_sem.at[sem],
            recv_sem=recv_sem.at[sem],
            device_id=peers[levels + k],
            device_id_type=MESH,
        )
        copy.start()
        copy.wait()
        sem += 1
        out_ref[...] = out_ref[...] + recv_s[k]
    halo_finish()


def grad_reduce(panels, small, x):
    nfilt = lax.axis_size("filt")
    nspace = lax.axis_size("space")
    width = panels.shape[1]
    pr = _rows(width)
    sr = _rows(small.shape[0])
    buf = jnp.concatenate(
        [
            jnp.pad(panels, ((0, 0), (0, pr * LANES - width))).reshape(nfilt * pr, LANES),
            jnp.pad(small, (0, sr * LANES - small.shape[0])).reshape(sr, LANES),
        ]
    )
    levels = nfilt.bit_length() - 1
    steps = nspace.bit_length() - 1
    scratch = []
    count = nfilt
    for _ in range(levels):
        count //= 2
        scratch.append(pltpu.VMEM((count * pr + sr, LANES), jnp.float32))
    count = nfilt
    for _ in range(levels):
        count //= 2
        scratch.append(pltpu.VMEM((count * pr + sr, LANES), jnp.float32))
    ncopies = 2 * levels + steps
    scratch += [
        pltpu.VMEM((max(steps, 1), pr + sr, LANES), jnp.float32),
        pltpu.SemaphoreType.DMA((ncopies,)),
        pltpu.SemaphoreType.DMA((ncopies,)),
    ]
    shapes = _halo_shapes(x)
    scratch += [pltpu.VMEM(sh.shape, sh.dtype) for sh in shapes]
    scratch += [pltpu.SemaphoreType.DMA((8,)), pltpu.SemaphoreType.DMA((8,))]
    out, *got = pl.pallas_call(
        functools.partial(reduce_kernel, nfilt, nspace, pr, sr, x.shape[2]),
        out_shape=[jax.ShapeDtypeStruct((pr + sr, LANES), jnp.float32)] + shapes,
        in_specs=[pl.BlockSpec(memory_space=pltpu.VMEM)] * 2,
        out_specs=[pl.BlockSpec(memory_space=pltpu.VMEM)] * 9,
        scratch_shapes=scratch,
        compiler_params=pltpu.CompilerParams(collective_id=0, has_side_effects=True),
        cost_estimate=pl.CostEstimate(
            flops=0, transcendentals=0, bytes_accessed=200 * 1024 * 1024
        ),
    )(buf, x)
    panel = out[:pr].reshape(-1)[:width]
    small = out[pr:].reshape(-1)[: small.shape[0]]
    return panel, small, got


def solution(mesh):
    in_specs = (
        P(None, "space", "filt"),
        P(None, "space", "filt"),
        P(),
        P(),
        P(),
        P(),
        P(),
        P(),
        P(),
        P(),
        P(),
    )
    out_specs = (
        P(None, "space", "filt"),
        P(None, "space", "filt"),
        P(),
        P(),
        P(),
        P(),
        P("filt", None),
        P("filt"),
        P("filt", None),
        P(),
        P(),
    )
    return jax.shard_map(shards, mesh=mesh, in_specs=in_specs, out_specs=out_specs, check_vma=False)
```

```python
import functools
import math

import jax
import jax.numpy as jnp
from jax import lax
from jax.experimental import pallas as pl
from jax.experimental.pallas import tpu as pltpu
from jax.sharding import PartitionSpec as P

MESH = pl.DeviceIdType.MESH
LANES = 128


_DIRS = [(-1, 0), (1, 0), (0, -1), (0, 1), (-1, -1), (-1, 1), (1, -1), (1, 1)]


def _lanes(df, cols):
    if df == 0:
        return slice(0, cols)
    if df > 0:
        return slice(cols - LANES, cols)
    return slice(0, LANES)


def _halo_ops(ns, nf, cols, x_ref, outs, slots, send_sem, recv_sem):
    s = lax.axis_index("space")
    f = lax.axis_index("filt")

    def exists(d):
        t, g = s + d[0], f + d[1]
        return (t >= 0) & (t < ns) & (g >= 0) & (g < nf)

    def desc(k):
        d = _DIRS[k]
        back = _DIRS.index((-d[0], -d[1]))
        return pltpu.make_async_remote_copy(
            src_ref=x_ref.at[:, :, _lanes(d[1], cols)],
            dst_ref=slots[back],
            send_sem=send_sem.at[k],
            recv_sem=recv_sem.at[back],
            device_id=(s + d[0], f + d[1]),
            device_id_type=MESH,
        )

    def signal(barrier):
        count = 0
        for d in _DIRS:

            @pl.when(exists(d))
            def _():
                pl.semaphore_signal(
                    barrier, inc=1, device_id=(s + d[0], f + d[1]), device_id_type=MESH
                )

            count = count + exists(d).astype(jnp.int32)
        return count

    def start():
        for k, d in enumerate(_DIRS):

            @pl.when(exists(d))
            def _():
                desc(k).start()

    def finish():
        for k, d in enumerate(_DIRS):
            back = _DIRS.index((-d[0], -d[1]))

            @pl.when(exists(d))
            def _():
                desc(k).wait_send()
                desc(back).wait_recv()
                outs[k][...] = slots[k][...]

            @pl.when(jnp.logical_not(exists(d)))
            def _():
                outs[k][...] = jnp.zeros(outs[k].shape, outs[k].dtype)

    return signal, start, finish


def halo_kernel(ns, nf, cols, x_ref, *refs):
    signal, start, finish = _halo_ops(ns, nf, cols, x_ref, refs[:8], refs[8:16], *refs[16:])
    barrier = pltpu.get_barrier_semaphore()
    pl.semaphore_wait(barrier, signal(barrier))
    start()
    finish()


def _halo_shapes(x):
    channels, rows, cols = x.shape
    return [
        jax.ShapeDtypeStruct((channels, rows, _lanes(d[1], cols).stop - _lanes(d[1], cols).start), x.dtype)
        for d in _DIRS
    ]


def _assemble(x, got, width):
    rows = x.shape[1]
    piece = dict(zip(_DIRS, got))
    hi_r, lo_r = slice(rows - width, rows), slice(0, width)
    above = piece[(-1, 0)][:, hi_r, :]
    below = piece[(1, 0)][:, lo_r, :]
    lw = piece[(0, -1)].shape[2]
    left = piece[(0, -1)][:, :, lw - width : lw]
    right = piece[(0, 1)][:, :, 0:width]
    top_left = piece[(-1, -1)][:, hi_r, lw - width : lw]
    top_right = piece[(-1, 1)][:, hi_r, 0:width]
    bottom_left = piece[(1, -1)][:, lo_r, lw - width : lw]
    bottom_right = piece[(1, 1)][:, lo_r, 0:width]
    return jnp.concatenate(
        [
            jnp.concatenate([top_left, above, top_right], axis=2),
            jnp.concatenate([left, x, right], axis=2),
            jnp.concatenate([bottom_left, below, bottom_right], axis=2),
        ],
        axis=1,
    )


def padded_2(x, sides, width, collective_id):
    del sides
    ns, nf = lax.axis_size("space"), lax.axis_size("filt")
    shapes = _halo_shapes(x)
    got = pl.pallas_call(
        functools.partial(halo_kernel, ns, nf, x.shape[2]),
        out_shape=shapes,
        in_specs=[pl.BlockSpec(memory_space=pltpu.VMEM)],
        out_specs=[pl.BlockSpec(memory_space=pltpu.VMEM)] * 8,
        scratch_shapes=[pltpu.VMEM(sh.shape, sh.dtype) for sh in shapes]
        + [pltpu.SemaphoreType.DMA((8,)), pltpu.SemaphoreType.DMA((8,))],
        compiler_params=pltpu.CompilerParams(
            collective_id=collective_id, has_side_effects=True
        ),
    )(x)
    return _assemble(x, got, width)


def dw_kernel(flip, cb, x_ref, k_ref, o_ref):
    rows, channels, cols = o_ref.shape
    wide = x_ref.shape[2]

    def block(i, carry):
        ch = pl.ds(pl.multiple_of(i * cb, cb), cb)
        x = x_ref[:, ch, :]
        acc = jnp.zeros((rows, cb, cols), jnp.float32)
        for shift_col in range(7):
            c0 = 6 - shift_col if flip else shift_col
            xb = pltpu.roll(x, shift=wide - c0, axis=2) if c0 else x
            xb = xb[:, :, :cols]
            for shift_row in range(7):
                r0 = 6 - shift_row if flip else shift_row
                kv = k_ref[ch, pl.ds(shift_row * 7 + shift_col, 1)]
                acc = acc + kv[None] * xb[r0 : r0 + rows]
        o_ref[:, ch, :] = acc
        return carry

    lax.fori_loop(0, channels // cb, block, 0, unroll=True)


def _dw(padded, kernel, row_count, col_count, flip):
    channels = padded.shape[0]
    wide = -(-padded.shape[2] // LANES) * LANES
    x = jnp.transpose(padded, (1, 0, 2)).astype(jnp.float32)
    x = jnp.pad(x, ((0, 0), (0, 0), (0, wide - padded.shape[2])))
    taps = kernel.reshape(channels, 49)
    cb = 8
    out = pl.pallas_call(
        functools.partial(dw_kernel, flip, cb),
        out_shape=jax.ShapeDtypeStruct((row_count, channels, col_count), jnp.float32),
        in_specs=[pl.BlockSpec(memory_space=pltpu.VMEM)] * 2,
        out_specs=pl.BlockSpec(memory_space=pltpu.VMEM),
    )(x, taps)
    return jnp.transpose(out, (1, 0, 2))


def depthwise(padded, kernel, row_count, col_count):
    return _dw(padded, kernel, row_count, col_count, False)


def conv_back(padded, kernel, row_count, col_count):
    return _dw(padded, kernel, row_count, col_count, True)


def kernel_terms(padded, convolution_gradient, row_count, col_count):
    ksize = 7
    columns = []
    for shift_col in range(ksize):
        corr = jnp.einsum(
            "crj,cij->cri",
            padded[:, :, shift_col : shift_col + col_count],
            convolution_gradient,
            preferred_element_type=jnp.float32,
        )
        total = corr[:, 0:ksize, 0]
        for row in range(1, row_count):
            total = total + corr[:, row : row + ksize, row]
        columns.append(total)
    return jnp.stack(columns, axis=2)


def gelu_exact(value):
    return value * (1.0 + jax.scipy.special.erf(value / math.sqrt(2.0))) * 0.5


def gelu_slope(value):
    return (1.0 + jax.scipy.special.erf(value / math.sqrt(2.0))) * 0.5 + value * jnp.exp(
        -0.5 * value * value
    ) / math.sqrt(2.0 * math.pi)


def shards(
    image,
    cotangent,
    kernel,
    dw_bias,
    layer_norm_gain,
    layer_norm_bias,
    w_expand,
    b_expand,
    w_reduce,
    b_reduce,
    layer_scale,
):
    channels, row_count, col_count = image.shape
    panel_rows = w_expand.shape[0] // lax.axis_size("filt")
    tok_count = row_count * col_count
    padded = padded_2(image, (("space", 1), ("filt", 2)), 3, 1)
    conv = depthwise(padded, kernel, row_count, col_count)
    conv = conv + dw_bias[:, None, None]
    flat = conv.reshape(channels, tok_count)
    average = jnp.mean(flat, axis=0, keepdims=True)
    mean_removed = flat - average
    inverse_deviation = lax.rsqrt(
        jnp.mean(mean_removed * mean_removed, axis=0, keepdims=True) + 1e-06
    )
    standardized_input = mean_removed * inverse_deviation
    normalized_input = (
        standardized_input * layer_norm_gain[:, None] + layer_norm_bias[:, None]
    ).astype(jnp.bfloat16)
    hidden = (
        jnp.dot(w_expand, normalized_input, preferred_element_type=jnp.float32)
        + b_expand.astype(jnp.float32)[:, None]
    )
    active = gelu_exact(hidden).astype(jnp.bfloat16)
    branch = (
        lax.dot_general(
            w_reduce, active, (((0,), (0,)), ((), ())), preferred_element_type=jnp.float32
        )
        + b_reduce[:, None]
    )
    resid = image.reshape(channels, tok_count).astype(jnp.float32)
    output = (
        (resid + layer_scale[:, None] * branch)
        .astype(jnp.bfloat16)
        .reshape(channels, row_count, col_count)
    )
    cot_flat = cotangent.reshape(channels, tok_count).astype(jnp.float32)
    scaled = layer_scale[:, None] * cot_flat
    g_scale = jnp.sum(cot_flat * branch, axis=1)
    g_rbias = jnp.sum(scaled, axis=1)
    d_branch = scaled.astype(jnp.bfloat16)
    g_reduce = lax.dot_general(
        active, d_branch, (((1,), (1,)), ((), ())), preferred_element_type=jnp.float32
    )
    d_active = jnp.dot(w_reduce, d_branch, preferred_element_type=jnp.float32)
    d_hidden = (d_active * gelu_slope(hidden)).astype(jnp.bfloat16)
    g_ebias = jnp.sum(d_hidden.astype(jnp.float32), axis=1)
    g_expand = lax.dot_general(
        d_hidden, normalized_input, (((1,), (1,)), ((), ())), preferred_element_type=jnp.float32
    )
    normalized_gradient = lax.dot_general(
        w_expand, d_hidden, (((0,), (0,)), ((), ())), preferred_element_type=jnp.float32
    )
    norm_gain_gradient = jnp.sum(normalized_gradient * standardized_input, axis=1)
    g_lbias = jnp.sum(normalized_gradient, axis=1)
    standardized_gradient = normalized_gradient * layer_norm_gain[:, None]
    convolution_gradient = inverse_deviation * (
        standardized_gradient
        - jnp.mean(standardized_gradient, axis=0, keepdims=True)
        - standardized_input
        * jnp.mean(standardized_gradient * standardized_input, axis=0, keepdims=True)
    )
    convolution_gradient = convolution_gradient.astype(jnp.bfloat16).reshape(
        channels, row_count, col_count
    )
    d_float = convolution_gradient.astype(jnp.float32)
    g_dbias = jnp.sum(d_float, axis=(1, 2))
    g_kernel = kernel_terms(padded, convolution_gradient, row_count, col_count)
    factor = 1.0 / math.sqrt(tok_count * lax.axis_size("space") * lax.axis_size("filt"))
    parts = lax.axis_size("filt")
    panels = jnp.concatenate(
        [
            g_reduce.reshape(parts, panel_rows * channels),
            g_expand.reshape(parts, panel_rows * channels),
            g_ebias.reshape(parts, panel_rows),
        ],
        axis=1,
    )
    small = jnp.concatenate(
        [
            g_kernel.reshape(-1),
            g_dbias,
            norm_gain_gradient,
            g_lbias,
            g_scale,
            g_rbias,
        ]
    )
    panel, small, got = grad_reduce(panels, small, convolution_gradient)
    padded_grad = _assemble(convolution_gradient, got, 3)
    back = conv_back(padded_grad, kernel, row_count, col_count)
    image_grad = (cotangent.astype(jnp.float32) + back).astype(jnp.bfloat16)
    total = jnp.concatenate([panel, small])
    total = total * factor
    cut = [panel_rows * channels, panel_rows * channels, panel_rows]
    g_reduce = total[: cut[0]].reshape(panel_rows, channels)
    g_expand = total[cut[0] : cut[0] + cut[1]].reshape(panel_rows, channels)
    g_ebias = total[cut[0] + cut[1] : sum(cut)]
    rest = total[sum(cut) :]
    ksq = kernel.shape[1] * kernel.shape[2]
    g_kernel = rest[: channels * ksq].reshape(kernel.shape)
    g_dbias, norm_gain_gradient, g_lbias, g_scale, g_rbias = (
        rest[channels * ksq + channels * i : channels * ksq + channels * (i + 1)]
        for i in range(5)
    )
    return (
        output,
        image_grad,
        g_kernel,
        g_dbias,
        norm_gain_gradient,
        g_lbias,
        g_expand,
        g_ebias,
        g_reduce,
        g_rbias,
        g_scale,
    )


def _rows(length):
    return -(-length // (8 * LANES)) * 8


def _flip(index, bit):
    return index + bit - 2 * bit * ((index // bit) % 2)


def reduce_kernel(nfilt, nspace, pr, sr, cols, buf_ref, x_ref, out_ref, *refs):
    levels = nfilt.bit_length() - 1
    steps = nspace.bit_length() - 1
    halo_outs = refs[:8]
    scratch = refs[8:]
    recvs = scratch[:levels]
    stages = scratch[levels : 2 * levels]
    recv_s, send_sem, recv_sem = scratch[2 * levels : 2 * levels + 3]
    halo = scratch[2 * levels + 3 :]
    halo_signal, halo_start, halo_finish = _halo_ops(
        nspace, nfilt, cols, x_ref, halo_outs, halo[:8], halo[8], halo[9]
    )
    s = lax.axis_index("space")
    f = lax.axis_index("filt")

    peers = []
    bit = nfilt // 2
    while bit >= 1:
        peers.append((s, _flip(f, bit)))
        bit //= 2
    for k in range(steps):
        peers.append((_flip(s, 1 << k), f))
    barrier = pltpu.get_barrier_semaphore()
    for peer in peers:
        pl.semaphore_signal(barrier, inc=1, device_id=peer, device_id_type=MESH)
    count = halo_signal(barrier)
    pl.semaphore_wait(barrier, count + len(peers))
    halo_start()

    held = buf_ref
    count = nfilt
    bit = nfilt // 2
    sem = 0
    for level in range(levels):
        half = count // 2
        upper = (f // bit) % 2
        rows = half * pr
        peer = peers[level]
        send_panels = pltpu.make_async_remote_copy(
            src_ref=held.at[pl.ds(pl.multiple_of((1 - upper) * rows, 8), rows)],
            dst_ref=recvs[level].at[pl.ds(0, rows)],
            send_sem=send_sem.at[sem],
            recv_sem=recv_sem.at[sem],
            device_id=peer,
            device_id_type=MESH,
        )
        send_small = pltpu.make_async_remote_copy(
            src_ref=held.at[pl.ds(count * pr, sr)],
            dst_ref=recvs[level].at[pl.ds(rows, sr)],
            send_sem=send_sem.at[sem + 1],
            recv_sem=recv_sem.at[sem + 1],
            device_id=peer,
            device_id_type=MESH,
        )
        send_panels.start()
        send_small.start()
        send_panels.wait()
        send_small.wait()
        sem += 2
        stage = stages[level]
        stage[pl.ds(0, rows)] = (
            held[pl.ds(pl.multiple_of(upper * rows, 8), rows)] + recvs[level][pl.ds(0, rows)]
        )
        stage[pl.ds(rows, sr)] = held[pl.ds(count * pr, sr)] + recvs[level][pl.ds(rows, sr)]
        held = stage
        count = half
        bit //= 2

    if levels == 0:
        out_ref[...] = buf_ref[...]
    else:
        out_ref[...] = held[...]
    for k in range(steps):
        copy = pltpu.make_async_remote_copy(
            src_ref=out_ref,
            dst_ref=recv_s.at[k],
            send_sem=send_sem.at[sem],
            recv_sem=recv_sem.at[sem],
            device_id=peers[levels + k],
            device_id_type=MESH,
        )
        copy.start()
        copy.wait()
        sem += 1
        out_ref[...] = out_ref[...] + recv_s[k]
    halo_finish()


def grad_reduce(panels, small, x):
    nfilt = lax.axis_size("filt")
    nspace = lax.axis_size("space")
    width = panels.shape[1]
    pr = _rows(width)
    sr = _rows(small.shape[0])
    buf = jnp.concatenate(
        [
            jnp.pad(panels, ((0, 0), (0, pr * LANES - width))).reshape(nfilt * pr, LANES),
            jnp.pad(small, (0, sr * LANES - small.shape[0])).reshape(sr, LANES),
        ]
    )
    levels = nfilt.bit_length() - 1
    steps = nspace.bit_length() - 1
    scratch = []
    count = nfilt
    for _ in range(levels):
        count //= 2
        scratch.append(pltpu.VMEM((count * pr + sr, LANES), jnp.float32))
    count = nfilt
    for _ in range(levels):
        count //= 2
        scratch.append(pltpu.VMEM((count * pr + sr, LANES), jnp.float32))
    ncopies = 2 * levels + steps
    scratch += [
        pltpu.VMEM((max(steps, 1), pr + sr, LANES), jnp.float32),
        pltpu.SemaphoreType.DMA((ncopies,)),
        pltpu.SemaphoreType.DMA((ncopies,)),
    ]
    shapes = _halo_shapes(x)
    scratch += [pltpu.VMEM(sh.shape, sh.dtype) for sh in shapes]
    scratch += [pltpu.SemaphoreType.DMA((8,)), pltpu.SemaphoreType.DMA((8,))]
    out, *got = pl.pallas_call(
        functools.partial(reduce_kernel, nfilt, nspace, pr, sr, x.shape[2]),
        out_shape=[jax.ShapeDtypeStruct((pr + sr, LANES), jnp.float32)] + shapes,
        in_specs=[pl.BlockSpec(memory_space=pltpu.VMEM)] * 2,
        out_specs=[pl.BlockSpec(memory_space=pltpu.VMEM)] * 9,
        scratch_shapes=scratch,
        compiler_params=pltpu.CompilerParams(collective_id=0, has_side_effects=True),
        cost_estimate=pl.CostEstimate(
            flops=0, transcendentals=0, bytes_accessed=200 * 1024 * 1024
        ),
    )(buf, x)
    panel = out[:pr].reshape(-1)[:width]
    small = out[pr:].reshape(-1)[: small.shape[0]]
    return panel, small, got


def solution(mesh):
    in_specs = (
        P(None, "space", "filt"),
        P(None, "space", "filt"),
        P(),
        P(),
        P(),
        P(),
        P(),
        P(),
        P(),
        P(),
        P(),
    )
    out_specs = (
        P(None, "space", "filt"),
        P(None, "space", "filt"),
        P(),
        P(),
        P(),
        P(),
        P("filt", None),
        P("filt"),
        P("filt", None),
        P(),
        P(),
    )
    return jax.shard_map(shards, mesh=mesh, in_specs=in_specs, out_specs=out_specs, check_vma=False)
```

```python
import functools
import math

import jax
import jax.numpy as jnp
from jax import lax
from jax.experimental import pallas as pl
from jax.experimental.pallas import tpu as pltpu
from jax.sharding import PartitionSpec as P

MESH = pl.DeviceIdType.MESH
LANES = 128


_DIRS = [(-1, 0), (1, 0), (0, -1), (0, 1), (-1, -1), (-1, 1), (1, -1), (1, 1)]


def _lanes(df, cols):
    if df == 0:
        return slice(0, cols)
    if df > 0:
        return slice(cols - LANES, cols)
    return slice(0, LANES)


def _halo_ops(ns, nf, cols, x_ref, outs, slots, send_sem, recv_sem):
    s = lax.axis_index("space")
    f = lax.axis_index("filt")

    def exists(d):
        t, g = s + d[0], f + d[1]
        return (t >= 0) & (t < ns) & (g >= 0) & (g < nf)

    def desc(k):
        d = _DIRS[k]
        back = _DIRS.index((-d[0], -d[1]))
        return pltpu.make_async_remote_copy(
            src_ref=x_ref.at[:, :, _lanes(d[1], cols)],
            dst_ref=slots[back],
            send_sem=send_sem.at[k],
            recv_sem=recv_sem.at[back],
            device_id=(s + d[0], f + d[1]),
            device_id_type=MESH,
        )

    def signal(barrier):
        count = 0
        for d in _DIRS:

            @pl.when(exists(d))
            def _():
                pl.semaphore_signal(
                    barrier, inc=1, device_id=(s + d[0], f + d[1]), device_id_type=MESH
                )

            count = count + exists(d).astype(jnp.int32)
        return count

    def start():
        for k, d in enumerate(_DIRS):

            @pl.when(exists(d))
            def _():
                desc(k).start()

    def finish():
        for k, d in enumerate(_DIRS):
            back = _DIRS.index((-d[0], -d[1]))

            @pl.when(exists(d))
            def _():
                desc(k).wait_send()
                desc(back).wait_recv()
                outs[k][...] = slots[k][...]

            @pl.when(jnp.logical_not(exists(d)))
            def _():
                outs[k][...] = jnp.zeros(outs[k].shape, outs[k].dtype)

    return signal, start, finish


def halo_kernel(ns, nf, cols, x_ref, *refs):
    signal, start, finish = _halo_ops(ns, nf, cols, x_ref, refs[:8], refs[8:16], *refs[16:])
    barrier = pltpu.get_barrier_semaphore()
    pl.semaphore_wait(barrier, signal(barrier))
    start()
    finish()


def _halo_shapes(x):
    channels, rows, cols = x.shape
    return [
        jax.ShapeDtypeStruct((channels, rows, _lanes(d[1], cols).stop - _lanes(d[1], cols).start), x.dtype)
        for d in _DIRS
    ]


def _assemble(x, got, width):
    rows = x.shape[0]
    piece = dict(zip(_DIRS, got))
    hi_r, lo_r = slice(rows - width, rows), slice(0, width)
    above = piece[(-1, 0)][hi_r]
    below = piece[(1, 0)][lo_r]
    lw = piece[(0, -1)].shape[2]
    left = piece[(0, -1)][:, :, lw - width : lw]
    right = piece[(0, 1)][:, :, 0:width]
    top_left = piece[(-1, -1)][hi_r, :, lw - width : lw]
    top_right = piece[(-1, 1)][hi_r, :, 0:width]
    bottom_left = piece[(1, -1)][lo_r, :, lw - width : lw]
    bottom_right = piece[(1, 1)][lo_r, :, 0:width]
    return jnp.concatenate(
        [
            jnp.concatenate([top_left, above, top_right], axis=2),
            jnp.concatenate([left, x, right], axis=2),
            jnp.concatenate([bottom_left, below, bottom_right], axis=2),
        ],
        axis=0,
    )


def padded_2(x, sides, width, collective_id):
    del sides
    ns, nf = lax.axis_size("space"), lax.axis_size("filt")
    shapes = _halo_shapes(x)
    got = pl.pallas_call(
        functools.partial(halo_kernel, ns, nf, x.shape[2]),
        out_shape=shapes,
        in_specs=[pl.BlockSpec(memory_space=pltpu.VMEM)],
        out_specs=[pl.BlockSpec(memory_space=pltpu.VMEM)] * 8,
        scratch_shapes=[pltpu.VMEM(sh.shape, sh.dtype) for sh in shapes]
        + [pltpu.SemaphoreType.DMA((8,)), pltpu.SemaphoreType.DMA((8,))],
        compiler_params=pltpu.CompilerParams(
            collective_id=collective_id, has_side_effects=True
        ),
    )(x)
    return _assemble(x, got, width)


def dw_kernel(flip, cb, x_ref, k_ref, o_ref):
    rows, channels, cols = o_ref.shape
    wide = x_ref.shape[2]

    def block(i, carry):
        ch = pl.ds(pl.multiple_of(i * cb, cb), cb)
        x = x_ref[:, ch, :]
        acc = jnp.zeros((rows, cb, cols), jnp.float32)
        for shift_col in range(7):
            c0 = 6 - shift_col if flip else shift_col
            xb = pltpu.roll(x, shift=wide - c0, axis=2) if c0 else x
            xb = xb[:, :, :cols]
            for shift_row in range(7):
                r0 = 6 - shift_row if flip else shift_row
                kv = k_ref[ch, pl.ds(shift_row * 7 + shift_col, 1)]
                acc = acc + kv[None] * xb[r0 : r0 + rows]
        o_ref[:, ch, :] = acc
        return carry

    lax.fori_loop(0, channels // cb, block, 0)


def _dw(padded, kernel, row_count, col_count, flip):
    channels = padded.shape[1]
    wide = -(-padded.shape[2] // LANES) * LANES
    x = padded.astype(jnp.float32)
    x = jnp.pad(x, ((0, 0), (0, 0), (0, wide - padded.shape[2])))
    taps = kernel.reshape(channels, 49)
    cb = 8
    out = pl.pallas_call(
        functools.partial(dw_kernel, flip, cb),
        out_shape=jax.ShapeDtypeStruct((row_count, channels, col_count), jnp.float32),
        in_specs=[pl.BlockSpec(memory_space=pltpu.VMEM)] * 2,
        out_specs=pl.BlockSpec(memory_space=pltpu.VMEM),
    )(x, taps)
    return jnp.transpose(out, (1, 0, 2))


def depthwise(padded, kernel, row_count, col_count):
    return _dw(padded, kernel, row_count, col_count, False)


def conv_back(padded, kernel, row_count, col_count):
    return _dw(padded, kernel, row_count, col_count, True)


def kernel_terms(padded, convolution_gradient, row_count, col_count):
    ksize = 7
    columns = []
    for shift_col in range(ksize):
        corr = jnp.einsum(
            "crj,cij->cri",
            padded[:, :, shift_col : shift_col + col_count],
            convolution_gradient,
            preferred_element_type=jnp.float32,
        )
        total = corr[:, 0:ksize, 0]
        for row in range(1, row_count):
            total = total + corr[:, row : row + ksize, row]
        columns.append(total)
    return jnp.stack(columns, axis=2)


def gelu_exact(value):
    return value * (1.0 + jax.scipy.special.erf(value / math.sqrt(2.0))) * 0.5


def gelu_slope(value):
    return (1.0 + jax.scipy.special.erf(value / math.sqrt(2.0))) * 0.5 + value * jnp.exp(
        -0.5 * value * value
    ) / math.sqrt(2.0 * math.pi)


def shards(
    image,
    cotangent,
    kernel,
    dw_bias,
    layer_norm_gain,
    layer_norm_bias,
    w_expand,
    b_expand,
    w_reduce,
    b_reduce,
    layer_scale,
):
    channels, row_count, col_count = image.shape
    panel_rows = w_expand.shape[0] // lax.axis_size("filt")
    tok_count = row_count * col_count
    padded_rows = padded_2(jnp.transpose(image, (1, 0, 2)), (("space", 1), ("filt", 2)), 3, 1)
    conv = depthwise(padded_rows, kernel, row_count, col_count)
    padded = jnp.transpose(padded_rows, (1, 0, 2))
    conv = conv + dw_bias[:, None, None]
    flat = conv.reshape(channels, tok_count)
    average = jnp.mean(flat, axis=0, keepdims=True)
    mean_removed = flat - average
    inverse_deviation = lax.rsqrt(
        jnp.mean(mean_removed * mean_removed, axis=0, keepdims=True) + 1e-06
    )
    standardized_input = mean_removed * inverse_deviation
    normalized_input = (
        standardized_input * layer_norm_gain[:, None] + layer_norm_bias[:, None]
    ).astype(jnp.bfloat16)
    hidden = (
        jnp.dot(w_expand, normalized_input, preferred_element_type=jnp.float32)
        + b_expand.astype(jnp.float32)[:, None]
    )
    active = gelu_exact(hidden).astype(jnp.bfloat16)
    branch = (
        lax.dot_general(
            w_reduce, active, (((0,), (0,)), ((), ())), preferred_element_type=jnp.float32
        )
        + b_reduce[:, None]
    )
    resid = image.reshape(channels, tok_count).astype(jnp.float32)
    output = (
        (resid + layer_scale[:, None] * branch)
        .astype(jnp.bfloat16)
        .reshape(channels, row_count, col_count)
    )
    cot_flat = cotangent.reshape(channels, tok_count).astype(jnp.float32)
    scaled = layer_scale[:, None] * cot_flat
    g_scale = jnp.sum(cot_flat * branch, axis=1)
    g_rbias = jnp.sum(scaled, axis=1)
    d_branch = scaled.astype(jnp.bfloat16)
    g_reduce = lax.dot_general(
        active, d_branch, (((1,), (1,)), ((), ())), preferred_element_type=jnp.float32
    )
    d_active = jnp.dot(w_reduce, d_branch, preferred_element_type=jnp.float32)
    d_hidden = (d_active * gelu_slope(hidden)).astype(jnp.bfloat16)
    g_ebias = jnp.sum(d_hidden.astype(jnp.float32), axis=1)
    g_expand = lax.dot_general(
        d_hidden, normalized_input, (((1,), (1,)), ((), ())), preferred_element_type=jnp.float32
    )
    normalized_gradient = lax.dot_general(
        w_expand, d_hidden, (((0,), (0,)), ((), ())), preferred_element_type=jnp.float32
    )
    norm_gain_gradient = jnp.sum(normalized_gradient * standardized_input, axis=1)
    g_lbias = jnp.sum(normalized_gradient, axis=1)
    standardized_gradient = normalized_gradient * layer_norm_gain[:, None]
    convolution_gradient = inverse_deviation * (
        standardized_gradient
        - jnp.mean(standardized_gradient, axis=0, keepdims=True)
        - standardized_input
        * jnp.mean(standardized_gradient * standardized_input, axis=0, keepdims=True)
    )
    convolution_gradient = convolution_gradient.astype(jnp.bfloat16).reshape(
        channels, row_count, col_count
    )
    d_float = convolution_gradient.astype(jnp.float32)
    g_dbias = jnp.sum(d_float, axis=(1, 2))
    g_kernel = kernel_terms(padded, convolution_gradient, row_count, col_count)
    factor = 1.0 / math.sqrt(tok_count * lax.axis_size("space") * lax.axis_size("filt"))
    parts = lax.axis_size("filt")
    panels = jnp.concatenate(
        [
            g_reduce.reshape(parts, panel_rows * channels),
            g_expand.reshape(parts, panel_rows * channels),
            g_ebias.reshape(parts, panel_rows),
        ],
        axis=1,
    )
    small = jnp.concatenate(
        [
            g_kernel.reshape(-1),
            g_dbias,
            norm_gain_gradient,
            g_lbias,
            g_scale,
            g_rbias,
        ]
    )
    grad_rows = jnp.transpose(convolution_gradient, (1, 0, 2))
    panel, small, got = grad_reduce(panels, small, grad_rows)
    padded_grad = _assemble(grad_rows, got, 3)
    back = conv_back(padded_grad, kernel, row_count, col_count)
    image_grad = (cotangent.astype(jnp.float32) + back).astype(jnp.bfloat16)
    total = jnp.concatenate([panel, small])
    total = total * factor
    cut = [panel_rows * channels, panel_rows * channels, panel_rows]
    g_reduce = total[: cut[0]].reshape(panel_rows, channels)
    g_expand = total[cut[0] : cut[0] + cut[1]].reshape(panel_rows, channels)
    g_ebias = total[cut[0] + cut[1] : sum(cut)]
    rest = total[sum(cut) :]
    ksq = kernel.shape[1] * kernel.shape[2]
    g_kernel = rest[: channels * ksq].reshape(kernel.shape)
    g_dbias, norm_gain_gradient, g_lbias, g_scale, g_rbias = (
        rest[channels * ksq + channels * i : channels * ksq + channels * (i + 1)]
        for i in range(5)
    )
    return (
        output,
        image_grad,
        g_kernel,
        g_dbias,
        norm_gain_gradient,
        g_lbias,
        g_expand,
        g_ebias,
        g_reduce,
        g_rbias,
        g_scale,
    )


def _rows(length):
    return -(-length // (8 * LANES)) * 8


def _flip(index, bit):
    return index + bit - 2 * bit * ((index // bit) % 2)


def reduce_kernel(nfilt, nspace, pr, sr, cols, buf_ref, x_ref, out_ref, *refs):
    levels = nfilt.bit_length() - 1
    steps = nspace.bit_length() - 1
    halo_outs = refs[:8]
    scratch = refs[8:]
    recvs = scratch[:levels]
    stages = scratch[levels : 2 * levels]
    recv_s, send_sem, recv_sem = scratch[2 * levels : 2 * levels + 3]
    halo = scratch[2 * levels + 3 :]
    halo_signal, halo_start, halo_finish = _halo_ops(
        nspace, nfilt, cols, x_ref, halo_outs, halo[:8], halo[8], halo[9]
    )
    s = lax.axis_index("space")
    f = lax.axis_index("filt")

    peers = []
    bit = nfilt // 2
    while bit >= 1:
        peers.append((s, _flip(f, bit)))
        bit //= 2
    for k in range(steps):
        peers.append((_flip(s, 1 << k), f))
    barrier = pltpu.get_barrier_semaphore()
    for peer in peers:
        pl.semaphore_signal(barrier, inc=1, device_id=peer, device_id_type=MESH)
    count = halo_signal(barrier)
    pl.semaphore_wait(barrier, count + len(peers))
    halo_start()

    held = buf_ref
    count = nfilt
    bit = nfilt // 2
    sem = 0
    for level in range(levels):
        half = count // 2
        upper = (f // bit) % 2
        rows = half * pr
        peer = peers[level]
        send_panels = pltpu.make_async_remote_copy(
            src_ref=held.at[pl.ds(pl.multiple_of((1 - upper) * rows, 8), rows)],
            dst_ref=recvs[level].at[pl.ds(0, rows)],
            send_sem=send_sem.at[sem],
            recv_sem=recv_sem.at[sem],
            device_id=peer,
            device_id_type=MESH,
        )
        send_small = pltpu.make_async_remote_copy(
            src_ref=held.at[pl.ds(count * pr, sr)],
            dst_ref=recvs[level].at[pl.ds(rows, sr)],
            send_sem=send_sem.at[sem + 1],
            recv_sem=recv_sem.at[sem + 1],
            device_id=peer,
            device_id_type=MESH,
        )
        send_panels.start()
        send_small.start()
        send_panels.wait()
        send_small.wait()
        sem += 2
        stage = stages[level]
        stage[pl.ds(0, rows)] = (
            held[pl.ds(pl.multiple_of(upper * rows, 8), rows)] + recvs[level][pl.ds(0, rows)]
        )
        stage[pl.ds(rows, sr)] = held[pl.ds(count * pr, sr)] + recvs[level][pl.ds(rows, sr)]
        held = stage
        count = half
        bit //= 2

    if levels == 0:
        out_ref[...] = buf_ref[...]
    else:
        out_ref[...] = held[...]
    for k in range(steps):
        copy = pltpu.make_async_remote_copy(
            src_ref=out_ref,
            dst_ref=recv_s.at[k],
            send_sem=send_sem.at[sem],
            recv_sem=recv_sem.at[sem],
            device_id=peers[levels + k],
            device_id_type=MESH,
        )
        copy.start()
        copy.wait()
        sem += 1
        out_ref[...] = out_ref[...] + recv_s[k]
    halo_finish()


def grad_reduce(panels, small, x):
    nfilt = lax.axis_size("filt")
    nspace = lax.axis_size("space")
    width = panels.shape[1]
    pr = _rows(width)
    sr = _rows(small.shape[0])
    buf = jnp.concatenate(
        [
            jnp.pad(panels, ((0, 0), (0, pr * LANES - width))).reshape(nfilt * pr, LANES),
            jnp.pad(small, (0, sr * LANES - small.shape[0])).reshape(sr, LANES),
        ]
    )
    levels = nfilt.bit_length() - 1
    steps = nspace.bit_length() - 1
    scratch = []
    count = nfilt
    for _ in range(levels):
        count //= 2
        scratch.append(pltpu.VMEM((count * pr + sr, LANES), jnp.float32))
    count = nfilt
    for _ in range(levels):
        count //= 2
        scratch.append(pltpu.VMEM((count * pr + sr, LANES), jnp.float32))
    ncopies = 2 * levels + steps
    scratch += [
        pltpu.VMEM((max(steps, 1), pr + sr, LANES), jnp.float32),
        pltpu.SemaphoreType.DMA((ncopies,)),
        pltpu.SemaphoreType.DMA((ncopies,)),
    ]
    shapes = _halo_shapes(x)
    scratch += [pltpu.VMEM(sh.shape, sh.dtype) for sh in shapes]
    scratch += [pltpu.SemaphoreType.DMA((8,)), pltpu.SemaphoreType.DMA((8,))]
    out, *got = pl.pallas_call(
        functools.partial(reduce_kernel, nfilt, nspace, pr, sr, x.shape[2]),
        out_shape=[jax.ShapeDtypeStruct((pr + sr, LANES), jnp.float32)] + shapes,
        in_specs=[pl.BlockSpec(memory_space=pltpu.VMEM)] * 2,
        out_specs=[pl.BlockSpec(memory_space=pltpu.VMEM)] * 9,
        scratch_shapes=scratch,
        compiler_params=pltpu.CompilerParams(collective_id=0, has_side_effects=True),
        cost_estimate=pl.CostEstimate(
            flops=0, transcendentals=0, bytes_accessed=200 * 1024 * 1024
        ),
    )(buf, x)
    panel = out[:pr].reshape(-1)[:width]
    small = out[pr:].reshape(-1)[: small.shape[0]]
    return panel, small, got


def solution(mesh):
    in_specs = (
        P(None, "space", "filt"),
        P(None, "space", "filt"),
        P(),
        P(),
        P(),
        P(),
        P(),
        P(),
        P(),
        P(),
        P(),
    )
    out_specs = (
        P(None, "space", "filt"),
        P(None, "space", "filt"),
        P(),
        P(),
        P(),
        P(),
        P("filt", None),
        P("filt"),
        P("filt", None),
        P(),
        P(),
    )
    return jax.shard_map(shards, mesh=mesh, in_specs=in_specs, out_specs=out_specs, check_vma=False)
```

```python
import functools
import math

import jax
import jax.numpy as jnp
from jax import lax
from jax.experimental import pallas as pl
from jax.experimental.pallas import tpu as pltpu
from jax.sharding import PartitionSpec as P

MESH = pl.DeviceIdType.MESH
LANES = 128


_DIRS = [(-1, 0), (1, 0), (0, -1), (0, 1), (-1, -1), (-1, 1), (1, -1), (1, 1)]


def _lanes(df, cols):
    if df == 0:
        return slice(0, cols)
    if df > 0:
        return slice(cols - LANES, cols)
    return slice(0, LANES)


def _halo_ops(ns, nf, cols, x_ref, outs, slots, send_sem, recv_sem):
    s = lax.axis_index("space")
    f = lax.axis_index("filt")

    def exists(d):
        t, g = s + d[0], f + d[1]
        return (t >= 0) & (t < ns) & (g >= 0) & (g < nf)

    def desc(k):
        d = _DIRS[k]
        back = _DIRS.index((-d[0], -d[1]))
        return pltpu.make_async_remote_copy(
            src_ref=x_ref.at[:, :, _lanes(d[1], cols)],
            dst_ref=slots[back],
            send_sem=send_sem.at[k],
            recv_sem=recv_sem.at[back],
            device_id=(s + d[0], f + d[1]),
            device_id_type=MESH,
        )

    def signal(barrier):
        count = 0
        for d in _DIRS:

            @pl.when(exists(d))
            def _():
                pl.semaphore_signal(
                    barrier, inc=1, device_id=(s + d[0], f + d[1]), device_id_type=MESH
                )

            count = count + exists(d).astype(jnp.int32)
        return count

    def start():
        for k, d in enumerate(_DIRS):

            @pl.when(exists(d))
            def _():
                desc(k).start()

    def finish():
        for k, d in enumerate(_DIRS):
            back = _DIRS.index((-d[0], -d[1]))

            @pl.when(exists(d))
            def _():
                desc(k).wait_send()
                desc(back).wait_recv()
                outs[k][...] = slots[k][...]

            @pl.when(jnp.logical_not(exists(d)))
            def _():
                outs[k][...] = jnp.zeros(outs[k].shape, outs[k].dtype)

    return signal, start, finish


def halo_kernel(ns, nf, cols, x_ref, *refs):
    signal, start, finish = _halo_ops(ns, nf, cols, x_ref, refs[:8], refs[8:16], *refs[16:])
    barrier = pltpu.get_barrier_semaphore()
    pl.semaphore_wait(barrier, signal(barrier))
    start()
    finish()


def _halo_shapes(x):
    channels, rows, cols = x.shape
    return [
        jax.ShapeDtypeStruct((channels, rows, _lanes(d[1], cols).stop - _lanes(d[1], cols).start), x.dtype)
        for d in _DIRS
    ]


def _assemble(x, got, width):
    rows = x.shape[1]
    piece = dict(zip(_DIRS, got))
    hi_r, lo_r = slice(rows - width, rows), slice(0, width)
    above = piece[(-1, 0)][:, hi_r, :]
    below = piece[(1, 0)][:, lo_r, :]
    lw = piece[(0, -1)].shape[2]
    left = piece[(0, -1)][:, :, lw - width : lw]
    right = piece[(0, 1)][:, :, 0:width]
    top_left = piece[(-1, -1)][:, hi_r, lw - width : lw]
    top_right = piece[(-1, 1)][:, hi_r, 0:width]
    bottom_left = piece[(1, -1)][:, lo_r, lw - width : lw]
    bottom_right = piece[(1, 1)][:, lo_r, 0:width]
    return jnp.concatenate(
        [
            jnp.concatenate([top_left, above, top_right], axis=2),
            jnp.concatenate([left, x, right], axis=2),
            jnp.concatenate([bottom_left, below, bottom_right], axis=2),
        ],
        axis=1,
    )


def padded_2(x, sides, width, collective_id):
    del sides
    ns, nf = lax.axis_size("space"), lax.axis_size("filt")
    shapes = _halo_shapes(x)
    got = pl.pallas_call(
        functools.partial(halo_kernel, ns, nf, x.shape[2]),
        out_shape=shapes,
        in_specs=[pl.BlockSpec(memory_space=pltpu.VMEM)],
        out_specs=[pl.BlockSpec(memory_space=pltpu.VMEM)] * 8,
        scratch_shapes=[pltpu.VMEM(sh.shape, sh.dtype) for sh in shapes]
        + [pltpu.SemaphoreType.DMA((8,)), pltpu.SemaphoreType.DMA((8,))],
        compiler_params=pltpu.CompilerParams(
            collective_id=collective_id, has_side_effects=True
        ),
    )(x)
    return _assemble(x, got, width)


def dw_kernel(flip, cb, x_ref, k_ref, o_ref):
    channels, rows, cols = o_ref.shape
    wide = x_ref.shape[2]

    def block(i, carry):
        ch = pl.ds(pl.multiple_of(i * cb, cb), cb)
        x = x_ref[:, ch, :]
        acc = jnp.zeros((rows, cb, cols), jnp.float32)
        for shift_col in range(7):
            c0 = 6 - shift_col if flip else shift_col
            xb = pltpu.roll(x, shift=wide - c0, axis=2) if c0 else x
            xb = xb[:, :, :cols]
            for shift_row in range(7):
                r0 = 6 - shift_row if flip else shift_row
                kv = k_ref[ch, pl.ds(shift_row * 7 + shift_col, 1)]
                acc = acc + kv[None] * xb[r0 : r0 + rows]
        for r in range(rows):
            o_ref[ch, r, :] = acc[r]
        return carry

    lax.fori_loop(0, channels // cb, block, 0)


def _dw(padded, kernel, row_count, col_count, flip):
    channels = padded.shape[0]
    wide = -(-padded.shape[2] // LANES) * LANES
    x = jnp.transpose(padded, (1, 0, 2)).astype(jnp.float32)
    x = jnp.pad(x, ((0, 0), (0, 0), (0, wide - padded.shape[2])))
    taps = kernel.reshape(channels, 49)
    cb = 8
    out = pl.pallas_call(
        functools.partial(dw_kernel, flip, cb),
        out_shape=jax.ShapeDtypeStruct((channels, row_count, col_count), jnp.float32),
        in_specs=[pl.BlockSpec(memory_space=pltpu.VMEM)] * 2,
        out_specs=pl.BlockSpec(memory_space=pltpu.VMEM),
    )(x, taps)
    return out


def depthwise(padded, kernel, row_count, col_count):
    return _dw(padded, kernel, row_count, col_count, False)


def conv_back(padded, kernel, row_count, col_count):
    return _dw(padded, kernel, row_count, col_count, True)


def kernel_terms(padded, convolution_gradient, row_count, col_count):
    ksize = 7
    columns = []
    for shift_col in range(ksize):
        corr = jnp.einsum(
            "crj,cij->cri",
            padded[:, :, shift_col : shift_col + col_count],
            convolution_gradient,
            preferred_element_type=jnp.float32,
        )
        total = corr[:, 0:ksize, 0]
        for row in range(1, row_count):
            total = total + corr[:, row : row + ksize, row]
        columns.append(total)
    return jnp.stack(columns, axis=2)


def gelu_exact(value):
    return value * (1.0 + jax.scipy.special.erf(value / math.sqrt(2.0))) * 0.5


def gelu_slope(value):
    return (1.0 + jax.scipy.special.erf(value / math.sqrt(2.0))) * 0.5 + value * jnp.exp(
        -0.5 * value * value
    ) / math.sqrt(2.0 * math.pi)


def shards(
    image,
    cotangent,
    kernel,
    dw_bias,
    layer_norm_gain,
    layer_norm_bias,
    w_expand,
    b_expand,
    w_reduce,
    b_reduce,
    layer_scale,
):
    channels, row_count, col_count = image.shape
    panel_rows = w_expand.shape[0] // lax.axis_size("filt")
    tok_count = row_count * col_count
    padded = padded_2(image, (("space", 1), ("filt", 2)), 3, 1)
    conv = depthwise(padded, kernel, row_count, col_count)
    conv = conv + dw_bias[:, None, None]
    flat = conv.reshape(channels, tok_count)
    average = jnp.mean(flat, axis=0, keepdims=True)
    mean_removed = flat - average
    inverse_deviation = lax.rsqrt(
        jnp.mean(mean_removed * mean_removed, axis=0, keepdims=True) + 1e-06
    )
    standardized_input = mean_removed * inverse_deviation
    normalized_input = (
        standardized_input * layer_norm_gain[:, None] + layer_norm_bias[:, None]
    ).astype(jnp.bfloat16)
    hidden = (
        jnp.dot(w_expand, normalized_input, preferred_element_type=jnp.float32)
        + b_expand.astype(jnp.float32)[:, None]
    )
    active = gelu_exact(hidden).astype(jnp.bfloat16)
    branch = (
        lax.dot_general(
            w_reduce, active, (((0,), (0,)), ((), ())), preferred_element_type=jnp.float32
        )
        + b_reduce[:, None]
    )
    resid = image.reshape(channels, tok_count).astype(jnp.float32)
    output = (
        (resid + layer_scale[:, None] * branch)
        .astype(jnp.bfloat16)
        .reshape(channels, row_count, col_count)
    )
    cot_flat = cotangent.reshape(channels, tok_count).astype(jnp.float32)
    scaled = layer_scale[:, None] * cot_flat
    g_scale = jnp.sum(cot_flat * branch, axis=1)
    g_rbias = jnp.sum(scaled, axis=1)
    d_branch = scaled.astype(jnp.bfloat16)
    g_reduce = lax.dot_general(
        active, d_branch, (((1,), (1,)), ((), ())), preferred_element_type=jnp.float32
    )
    d_active = jnp.dot(w_reduce, d_branch, preferred_element_type=jnp.float32)
    d_hidden = (d_active * gelu_slope(hidden)).astype(jnp.bfloat16)
    g_ebias = jnp.sum(d_hidden.astype(jnp.float32), axis=1)
    g_expand = lax.dot_general(
        d_hidden, normalized_input, (((1,), (1,)), ((), ())), preferred_element_type=jnp.float32
    )
    normalized_gradient = lax.dot_general(
        w_expand, d_hidden, (((0,), (0,)), ((), ())), preferred_element_type=jnp.float32
    )
    norm_gain_gradient = jnp.sum(normalized_gradient * standardized_input, axis=1)
    g_lbias = jnp.sum(normalized_gradient, axis=1)
    standardized_gradient = normalized_gradient * layer_norm_gain[:, None]
    convolution_gradient = inverse_deviation * (
        standardized_gradient
        - jnp.mean(standardized_gradient, axis=0, keepdims=True)
        - standardized_input
        * jnp.mean(standardized_gradient * standardized_input, axis=0, keepdims=True)
    )
    convolution_gradient = convolution_gradient.astype(jnp.bfloat16).reshape(
        channels, row_count, col_count
    )
    d_float = convolution_gradient.astype(jnp.float32)
    g_dbias = jnp.sum(d_float, axis=(1, 2))
    g_kernel = kernel_terms(padded, convolution_gradient, row_count, col_count)
    factor = 1.0 / math.sqrt(tok_count * lax.axis_size("space") * lax.axis_size("filt"))
    parts = lax.axis_size("filt")
    panels = jnp.concatenate(
        [
            g_reduce.reshape(parts, panel_rows * channels),
            g_expand.reshape(parts, panel_rows * channels),
            g_ebias.reshape(parts, panel_rows),
        ],
        axis=1,
    )
    small = jnp.concatenate(
        [
            g_kernel.reshape(-1),
            g_dbias,
            norm_gain_gradient,
            g_lbias,
            g_scale,
            g_rbias,
        ]
    )
    panel, small, got = grad_reduce(panels, small, convolution_gradient)
    padded_grad = _assemble(convolution_gradient, got, 3)
    back = conv_back(padded_grad, kernel, row_count, col_count)
    image_grad = (cotangent.astype(jnp.float32) + back).astype(jnp.bfloat16)
    total = jnp.concatenate([panel, small])
    total = total * factor
    cut = [panel_rows * channels, panel_rows * channels, panel_rows]
    g_reduce = total[: cut[0]].reshape(panel_rows, channels)
    g_expand = total[cut[0] : cut[0] + cut[1]].reshape(panel_rows, channels)
    g_ebias = total[cut[0] + cut[1] : sum(cut)]
    rest = total[sum(cut) :]
    ksq = kernel.shape[1] * kernel.shape[2]
    g_kernel = rest[: channels * ksq].reshape(kernel.shape)
    g_dbias, norm_gain_gradient, g_lbias, g_scale, g_rbias = (
        rest[channels * ksq + channels * i : channels * ksq + channels * (i + 1)]
        for i in range(5)
    )
    return (
        output,
        image_grad,
        g_kernel,
        g_dbias,
        norm_gain_gradient,
        g_lbias,
        g_expand,
        g_ebias,
        g_reduce,
        g_rbias,
        g_scale,
    )


def _rows(length):
    return -(-length // (8 * LANES)) * 8


def _flip(index, bit):
    return index + bit - 2 * bit * ((index // bit) % 2)


def reduce_kernel(nfilt, nspace, pr, sr, cols, buf_ref, x_ref, out_ref, *refs):
    levels = nfilt.bit_length() - 1
    steps = nspace.bit_length() - 1
    halo_outs = refs[:8]
    scratch = refs[8:]
    recvs = scratch[:levels]
    stages = scratch[levels : 2 * levels]
    recv_s, send_sem, recv_sem = scratch[2 * levels : 2 * levels + 3]
    halo = scratch[2 * levels + 3 :]
    halo_signal, halo_start, halo_finish = _halo_ops(
        nspace, nfilt, cols, x_ref, halo_outs, halo[:8], halo[8], halo[9]
    )
    s = lax.axis_index("space")
    f = lax.axis_index("filt")

    peers = []
    bit = nfilt // 2
    while bit >= 1:
        peers.append((s, _flip(f, bit)))
        bit //= 2
    for k in range(steps):
        peers.append((_flip(s, 1 << k), f))
    barrier = pltpu.get_barrier_semaphore()
    for peer in peers:
        pl.semaphore_signal(barrier, inc=1, device_id=peer, device_id_type=MESH)
    count = halo_signal(barrier)
    pl.semaphore_wait(barrier, count + len(peers))
    halo_start()

    held = buf_ref
    count = nfilt
    bit = nfilt // 2
    sem = 0
    for level in range(levels):
        half = count // 2
        upper = (f // bit) % 2
        rows = half * pr
        peer = peers[level]
        send_panels = pltpu.make_async_remote_copy(
            src_ref=held.at[pl.ds(pl.multiple_of((1 - upper) * rows, 8), rows)],
            dst_ref=recvs[level].at[pl.ds(0, rows)],
            send_sem=send_sem.at[sem],
            recv_sem=recv_sem.at[sem],
            device_id=peer,
            device_id_type=MESH,
        )
        send_small = pltpu.make_async_remote_copy(
            src_ref=held.at[pl.ds(count * pr, sr)],
            dst_ref=recvs[level].at[pl.ds(rows, sr)],
            send_sem=send_sem.at[sem + 1],
            recv_sem=recv_sem.at[sem + 1],
            device_id=peer,
            device_id_type=MESH,
        )
        send_panels.start()
        send_small.start()
        send_panels.wait()
        send_small.wait()
        sem += 2
        stage = stages[level]
        stage[pl.ds(0, rows)] = (
            held[pl.ds(pl.multiple_of(upper * rows, 8), rows)] + recvs[level][pl.ds(0, rows)]
        )
        stage[pl.ds(rows, sr)] = held[pl.ds(count * pr, sr)] + recvs[level][pl.ds(rows, sr)]
        held = stage
        count = half
        bit //= 2

    if levels == 0:
        out_ref[...] = buf_ref[...]
    else:
        out_ref[...] = held[...]
    for k in range(steps):
        copy = pltpu.make_async_remote_copy(
            src_ref=out_ref,
            dst_ref=recv_s.at[k],
            send_sem=send_sem.at[sem],
            recv_sem=recv_sem.at[sem],
            device_id=peers[levels + k],
            device_id_type=MESH,
        )
        copy.start()
        copy.wait()
        sem += 1
        out_ref[...] = out_ref[...] + recv_s[k]
    halo_finish()


def grad_reduce(panels, small, x):
    nfilt = lax.axis_size("filt")
    nspace = lax.axis_size("space")
    width = panels.shape[1]
    pr = _rows(width)
    sr = _rows(small.shape[0])
    buf = jnp.concatenate(
        [
            jnp.pad(panels, ((0, 0), (0, pr * LANES - width))).reshape(nfilt * pr, LANES),
            jnp.pad(small, (0, sr * LANES - small.shape[0])).reshape(sr, LANES),
        ]
    )
    levels = nfilt.bit_length() - 1
    steps = nspace.bit_length() - 1
    scratch = []
    count = nfilt
    for _ in range(levels):
        count //= 2
        scratch.append(pltpu.VMEM((count * pr + sr, LANES), jnp.float32))
    count = nfilt
    for _ in range(levels):
        count //= 2
        scratch.append(pltpu.VMEM((count * pr + sr, LANES), jnp.float32))
    ncopies = 2 * levels + steps
    scratch += [
        pltpu.VMEM((max(steps, 1), pr + sr, LANES), jnp.float32),
        pltpu.SemaphoreType.DMA((ncopies,)),
        pltpu.SemaphoreType.DMA((ncopies,)),
    ]
    shapes = _halo_shapes(x)
    scratch += [pltpu.VMEM(sh.shape, sh.dtype) for sh in shapes]
    scratch += [pltpu.SemaphoreType.DMA((8,)), pltpu.SemaphoreType.DMA((8,))]
    out, *got = pl.pallas_call(
        functools.partial(reduce_kernel, nfilt, nspace, pr, sr, x.shape[2]),
        out_shape=[jax.ShapeDtypeStruct((pr + sr, LANES), jnp.float32)] + shapes,
        in_specs=[pl.BlockSpec(memory_space=pltpu.VMEM)] * 2,
        out_specs=[pl.BlockSpec(memory_space=pltpu.VMEM)] * 9,
        scratch_shapes=scratch,
        compiler_params=pltpu.CompilerParams(collective_id=0, has_side_effects=True),
        cost_estimate=pl.CostEstimate(
            flops=0, transcendentals=0, bytes_accessed=200 * 1024 * 1024
        ),
    )(buf, x)
    panel = out[:pr].reshape(-1)[:width]
    small = out[pr:].reshape(-1)[: small.shape[0]]
    return panel, small, got


def solution(mesh):
    in_specs = (
        P(None, "space", "filt"),
        P(None, "space", "filt"),
        P(),
        P(),
        P(),
        P(),
        P(),
        P(),
        P(),
        P(),
        P(),
    )
    out_specs = (
        P(None, "space", "filt"),
        P(None, "space", "filt"),
        P(),
        P(),
        P(),
        P(),
        P("filt", None),
        P("filt"),
        P("filt", None),
        P(),
        P(),
    )
    return jax.shard_map(shards, mesh=mesh, in_specs=in_specs, out_specs=out_specs, check_vma=False)
```

```python
import functools
import math

import jax
import jax.numpy as jnp
from jax import lax
from jax.experimental import pallas as pl
from jax.experimental.pallas import tpu as pltpu
from jax.sharding import PartitionSpec as P

MESH = pl.DeviceIdType.MESH
LANES = 128


_DIRS = [(-1, 0), (1, 0), (0, -1), (0, 1), (-1, -1), (-1, 1), (1, -1), (1, 1)]


def _lanes(df, cols):
    if df == 0:
        return slice(0, cols)
    if df > 0:
        return slice(cols - LANES, cols)
    return slice(0, LANES)


def _halo_ops(ns, nf, cols, x_ref, outs, slots, send_sem, recv_sem):
    s = lax.axis_index("space")
    f = lax.axis_index("filt")

    def exists(d):
        t, g = s + d[0], f + d[1]
        return (t >= 0) & (t < ns) & (g >= 0) & (g < nf)

    def desc(k):
        d = _DIRS[k]
        back = _DIRS.index((-d[0], -d[1]))
        return pltpu.make_async_remote_copy(
            src_ref=x_ref.at[:, :, _lanes(d[1], cols)],
            dst_ref=slots[back],
            send_sem=send_sem.at[k],
            recv_sem=recv_sem.at[back],
            device_id=(s + d[0], f + d[1]),
            device_id_type=MESH,
        )

    def signal(barrier):
        count = 0
        for d in _DIRS:

            @pl.when(exists(d))
            def _():
                pl.semaphore_signal(
                    barrier, inc=1, device_id=(s + d[0], f + d[1]), device_id_type=MESH
                )

            count = count + exists(d).astype(jnp.int32)
        return count

    def start():
        for k, d in enumerate(_DIRS):

            @pl.when(exists(d))
            def _():
                desc(k).start()

    def finish():
        for k, d in enumerate(_DIRS):
            back = _DIRS.index((-d[0], -d[1]))

            @pl.when(exists(d))
            def _():
                desc(k).wait_send()
                desc(back).wait_recv()
                outs[k][...] = slots[k][...]

            @pl.when(jnp.logical_not(exists(d)))
            def _():
                outs[k][...] = jnp.zeros(outs[k].shape, outs[k].dtype)

    return signal, start, finish


def halo_kernel(ns, nf, cols, x_ref, *refs):
    signal, start, finish = _halo_ops(ns, nf, cols, x_ref, refs[:8], refs[8:16], *refs[16:])
    barrier = pltpu.get_barrier_semaphore()
    pl.semaphore_wait(barrier, signal(barrier))
    start()
    finish()


def _halo_shapes(x):
    channels, rows, cols = x.shape
    return [
        jax.ShapeDtypeStruct((channels, rows, _lanes(d[1], cols).stop - _lanes(d[1], cols).start), x.dtype)
        for d in _DIRS
    ]


def _assemble(x, got, width):
    rows = x.shape[1]
    piece = dict(zip(_DIRS, got))
    hi_r, lo_r = slice(rows - width, rows), slice(0, width)
    above = piece[(-1, 0)][:, hi_r, :]
    below = piece[(1, 0)][:, lo_r, :]
    lw = piece[(0, -1)].shape[2]
    left = piece[(0, -1)][:, :, lw - width : lw]
    right = piece[(0, 1)][:, :, 0:width]
    top_left = piece[(-1, -1)][:, hi_r, lw - width : lw]
    top_right = piece[(-1, 1)][:, hi_r, 0:width]
    bottom_left = piece[(1, -1)][:, lo_r, lw - width : lw]
    bottom_right = piece[(1, 1)][:, lo_r, 0:width]
    return jnp.concatenate(
        [
            jnp.concatenate([top_left, above, top_right], axis=2),
            jnp.concatenate([left, x, right], axis=2),
            jnp.concatenate([bottom_left, below, bottom_right], axis=2),
        ],
        axis=1,
    )


def padded_2(x, sides, width, collective_id):
    del sides
    ns, nf = lax.axis_size("space"), lax.axis_size("filt")
    shapes = _halo_shapes(x)
    got = pl.pallas_call(
        functools.partial(halo_kernel, ns, nf, x.shape[2]),
        out_shape=shapes,
        in_specs=[pl.BlockSpec(memory_space=pltpu.VMEM)],
        out_specs=[pl.BlockSpec(memory_space=pltpu.VMEM)] * 8,
        scratch_shapes=[pltpu.VMEM(sh.shape, sh.dtype) for sh in shapes]
        + [pltpu.SemaphoreType.DMA((8,)), pltpu.SemaphoreType.DMA((8,))],
        compiler_params=pltpu.CompilerParams(
            collective_id=collective_id, has_side_effects=True
        ),
    )(x)
    return _assemble(x, got, width)


def dw_kernel(flip, cb, x_ref, k_ref, *rest):
    cot_ref = rest[0] if len(rest) > 1 else None
    o_ref = rest[-1]
    channels, rows, cols = o_ref.shape
    wide = x_ref.shape[2]

    def block(i, carry):
        ch = pl.ds(pl.multiple_of(i * cb, cb), cb)
        x = x_ref[:, ch, :]
        acc = jnp.zeros((rows, cb, cols), jnp.float32)
        for shift_col in range(7):
            c0 = 6 - shift_col if flip else shift_col
            xb = pltpu.roll(x, shift=wide - c0, axis=2) if c0 else x
            xb = xb[:, :, :cols]
            for shift_row in range(7):
                r0 = 6 - shift_row if flip else shift_row
                kv = k_ref[ch, pl.ds(shift_row * 7 + shift_col, 1)]
                acc = acc + kv[None] * xb[r0 : r0 + rows]
        for r in range(rows):
            if cot_ref is None:
                o_ref[ch, r, :] = acc[r]
            else:
                o_ref[ch, r, :] = (cot_ref[ch, r, :].astype(jnp.float32) + acc[r]).astype(o_ref.dtype)
        return carry

    lax.fori_loop(0, channels // cb, block, 0)


def _dw(padded, kernel, row_count, col_count, flip, cot=None):
    channels = padded.shape[0]
    wide = -(-padded.shape[2] // LANES) * LANES
    x = jnp.transpose(padded, (1, 0, 2)).astype(jnp.float32)
    x = jnp.pad(x, ((0, 0), (0, 0), (0, wide - padded.shape[2])))
    taps = kernel.reshape(channels, 49)
    cb = 8
    out = pl.pallas_call(
        functools.partial(dw_kernel, flip, cb),
        out_shape=jax.ShapeDtypeStruct(
            (channels, row_count, col_count), jnp.float32 if cot is None else cot.dtype
        ),
        in_specs=[pl.BlockSpec(memory_space=pltpu.VMEM)] * (2 if cot is None else 3),
        out_specs=pl.BlockSpec(memory_space=pltpu.VMEM),
    )(x, taps, *([] if cot is None else [cot]))
    return out


def depthwise(padded, kernel, row_count, col_count):
    return _dw(padded, kernel, row_count, col_count, False)


def conv_back(padded, kernel, row_count, col_count, cot):
    return _dw(padded, kernel, row_count, col_count, True, cot)


def kernel_terms(padded, convolution_gradient, row_count, col_count):
    ksize = 7
    columns = []
    for shift_col in range(ksize):
        corr = jnp.einsum(
            "crj,cij->cri",
            padded[:, :, shift_col : shift_col + col_count],
            convolution_gradient,
            preferred_element_type=jnp.float32,
        )
        total = corr[:, 0:ksize, 0]
        for row in range(1, row_count):
            total = total + corr[:, row : row + ksize, row]
        columns.append(total)
    return jnp.stack(columns, axis=2)


def gelu_exact(value):
    return value * (1.0 + jax.scipy.special.erf(value / math.sqrt(2.0))) * 0.5


def gelu_slope(value):
    return (1.0 + jax.scipy.special.erf(value / math.sqrt(2.0))) * 0.5 + value * jnp.exp(
        -0.5 * value * value
    ) / math.sqrt(2.0 * math.pi)


def shards(
    image,
    cotangent,
    kernel,
    dw_bias,
    layer_norm_gain,
    layer_norm_bias,
    w_expand,
    b_expand,
    w_reduce,
    b_reduce,
    layer_scale,
):
    channels, row_count, col_count = image.shape
    panel_rows = w_expand.shape[0] // lax.axis_size("filt")
    tok_count = row_count * col_count
    padded = padded_2(image, (("space", 1), ("filt", 2)), 3, 1)
    conv = depthwise(padded, kernel, row_count, col_count)
    conv = conv + dw_bias[:, None, None]
    flat = conv.reshape(channels, tok_count)
    average = jnp.mean(flat, axis=0, keepdims=True)
    mean_removed = flat - average
    inverse_deviation = lax.rsqrt(
        jnp.mean(mean_removed * mean_removed, axis=0, keepdims=True) + 1e-06
    )
    standardized_input = mean_removed * inverse_deviation
    normalized_input = (
        standardized_input * layer_norm_gain[:, None] + layer_norm_bias[:, None]
    ).astype(jnp.bfloat16)
    hidden = (
        jnp.dot(w_expand, normalized_input, preferred_element_type=jnp.float32)
        + b_expand.astype(jnp.float32)[:, None]
    )
    active = gelu_exact(hidden).astype(jnp.bfloat16)
    branch = (
        lax.dot_general(
            w_reduce, active, (((0,), (0,)), ((), ())), preferred_element_type=jnp.float32
        )
        + b_reduce[:, None]
    )
    resid = image.reshape(channels, tok_count).astype(jnp.float32)
    output = (
        (resid + layer_scale[:, None] * branch)
        .astype(jnp.bfloat16)
        .reshape(channels, row_count, col_count)
    )
    cot_flat = cotangent.reshape(channels, tok_count).astype(jnp.float32)
    scaled = layer_scale[:, None] * cot_flat
    g_scale = jnp.sum(cot_flat * branch, axis=1)
    g_rbias = jnp.sum(scaled, axis=1)
    d_branch = scaled.astype(jnp.bfloat16)
    g_reduce = lax.dot_general(
        active, d_branch, (((1,), (1,)), ((), ())), preferred_element_type=jnp.float32
    )
    d_active = jnp.dot(w_reduce, d_branch, preferred_element_type=jnp.float32)
    d_hidden = (d_active * gelu_slope(hidden)).astype(jnp.bfloat16)
    g_ebias = jnp.sum(d_hidden.astype(jnp.float32), axis=1)
    g_expand = lax.dot_general(
        d_hidden, normalized_input, (((1,), (1,)), ((), ())), preferred_element_type=jnp.float32
    )
    normalized_gradient = lax.dot_general(
        w_expand, d_hidden, (((0,), (0,)), ((), ())), preferred_element_type=jnp.float32
    )
    norm_gain_gradient = jnp.sum(normalized_gradient * standardized_input, axis=1)
    g_lbias = jnp.sum(normalized_gradient, axis=1)
    standardized_gradient = normalized_gradient * layer_norm_gain[:, None]
    convolution_gradient = inverse_deviation * (
        standardized_gradient
        - jnp.mean(standardized_gradient, axis=0, keepdims=True)
        - standardized_input
        * jnp.mean(standardized_gradient * standardized_input, axis=0, keepdims=True)
    )
    convolution_gradient = convolution_gradient.astype(jnp.bfloat16).reshape(
        channels, row_count, col_count
    )
    d_float = convolution_gradient.astype(jnp.float32)
    g_dbias = jnp.sum(d_float, axis=(1, 2))
    g_kernel = kernel_terms(padded, convolution_gradient, row_count, col_count)
    factor = 1.0 / math.sqrt(tok_count * lax.axis_size("space") * lax.axis_size("filt"))
    parts = lax.axis_size("filt")
    panels = jnp.concatenate(
        [
            g_reduce.reshape(parts, panel_rows * channels),
            g_expand.reshape(parts, panel_rows * channels),
            g_ebias.reshape(parts, panel_rows),
        ],
        axis=1,
    )
    small = jnp.concatenate(
        [
            g_kernel.reshape(-1),
            g_dbias,
            norm_gain_gradient,
            g_lbias,
            g_scale,
            g_rbias,
        ]
    )
    panel, small, got = grad_reduce(panels, small, convolution_gradient)
    padded_grad = _assemble(convolution_gradient, got, 3)
    image_grad = conv_back(padded_grad, kernel, row_count, col_count, cotangent)
    total = jnp.concatenate([panel, small])
    total = total * factor
    cut = [panel_rows * channels, panel_rows * channels, panel_rows]
    g_reduce = total[: cut[0]].reshape(panel_rows, channels)
    g_expand = total[cut[0] : cut[0] + cut[1]].reshape(panel_rows, channels)
    g_ebias = total[cut[0] + cut[1] : sum(cut)]
    rest = total[sum(cut) :]
    ksq = kernel.shape[1] * kernel.shape[2]
    g_kernel = rest[: channels * ksq].reshape(kernel.shape)
    g_dbias, norm_gain_gradient, g_lbias, g_scale, g_rbias = (
        rest[channels * ksq + channels * i : channels * ksq + channels * (i + 1)]
        for i in range(5)
    )
    return (
        output,
        image_grad,
        g_kernel,
        g_dbias,
        norm_gain_gradient,
        g_lbias,
        g_expand,
        g_ebias,
        g_reduce,
        g_rbias,
        g_scale,
    )


def _rows(length):
    return -(-length // (8 * LANES)) * 8


def _flip(index, bit):
    return index + bit - 2 * bit * ((index // bit) % 2)


def reduce_kernel(nfilt, nspace, pr, sr, cols, buf_ref, x_ref, out_ref, *refs):
    levels = nfilt.bit_length() - 1
    steps = nspace.bit_length() - 1
    halo_outs = refs[:8]
    scratch = refs[8:]
    recvs = scratch[:levels]
    stages = scratch[levels : 2 * levels]
    recv_s, send_sem, recv_sem = scratch[2 * levels : 2 * levels + 3]
    halo = scratch[2 * levels + 3 :]
    halo_signal, halo_start, halo_finish = _halo_ops(
        nspace, nfilt, cols, x_ref, halo_outs, halo[:8], halo[8], halo[9]
    )
    s = lax.axis_index("space")
    f = lax.axis_index("filt")

    peers = []
    bit = nfilt // 2
    while bit >= 1:
        peers.append((s, _flip(f, bit)))
        bit //= 2
    for k in range(steps):
        peers.append((_flip(s, 1 << k), f))
    barrier = pltpu.get_barrier_semaphore()
    for peer in peers:
        pl.semaphore_signal(barrier, inc=1, device_id=peer, device_id_type=MESH)
    count = halo_signal(barrier)
    pl.semaphore_wait(barrier, count + len(peers))
    halo_start()

    held = buf_ref
    count = nfilt
    bit = nfilt // 2
    sem = 0
    for level in range(levels):
        half = count // 2
        upper = (f // bit) % 2
        rows = half * pr
        peer = peers[level]
        send_panels = pltpu.make_async_remote_copy(
            src_ref=held.at[pl.ds(pl.multiple_of((1 - upper) * rows, 8), rows)],
            dst_ref=recvs[level].at[pl.ds(0, rows)],
            send_sem=send_sem.at[sem],
            recv_sem=recv_sem.at[sem],
            device_id=peer,
            device_id_type=MESH,
        )
        send_small = pltpu.make_async_remote_copy(
            src_ref=held.at[pl.ds(count * pr, sr)],
            dst_ref=recvs[level].at[pl.ds(rows, sr)],
            send_sem=send_sem.at[sem + 1],
            recv_sem=recv_sem.at[sem + 1],
            device_id=peer,
            device_id_type=MESH,
        )
        send_panels.start()
        send_small.start()
        send_panels.wait()
        send_small.wait()
        sem += 2
        stage = stages[level]
        stage[pl.ds(0, rows)] = (
            held[pl.ds(pl.multiple_of(upper * rows, 8), rows)] + recvs[level][pl.ds(0, rows)]
        )
        stage[pl.ds(rows, sr)] = held[pl.ds(count * pr, sr)] + recvs[level][pl.ds(rows, sr)]
        held = stage
        count = half
        bit //= 2

    if levels == 0:
        out_ref[...] = buf_ref[...]
    else:
        out_ref[...] = held[...]
    for k in range(steps):
        copy = pltpu.make_async_remote_copy(
            src_ref=out_ref,
            dst_ref=recv_s.at[k],
            send_sem=send_sem.at[sem],
            recv_sem=recv_sem.at[sem],
            device_id=peers[levels + k],
            device_id_type=MESH,
        )
        copy.start()
        copy.wait()
        sem += 1
        out_ref[...] = out_ref[...] + recv_s[k]
    halo_finish()


def grad_reduce(panels, small, x):
    nfilt = lax.axis_size("filt")
    nspace = lax.axis_size("space")
    width = panels.shape[1]
    pr = _rows(width)
    sr = _rows(small.shape[0])
    buf = jnp.concatenate(
        [
            jnp.pad(panels, ((0, 0), (0, pr * LANES - width))).reshape(nfilt * pr, LANES),
            jnp.pad(small, (0, sr * LANES - small.shape[0])).reshape(sr, LANES),
        ]
    )
    levels = nfilt.bit_length() - 1
    steps = nspace.bit_length() - 1
    scratch = []
    count = nfilt
    for _ in range(levels):
        count //= 2
        scratch.append(pltpu.VMEM((count * pr + sr, LANES), jnp.float32))
    count = nfilt
    for _ in range(levels):
        count //= 2
        scratch.append(pltpu.VMEM((count * pr + sr, LANES), jnp.float32))
    ncopies = 2 * levels + steps
    scratch += [
        pltpu.VMEM((max(steps, 1), pr + sr, LANES), jnp.float32),
        pltpu.SemaphoreType.DMA((ncopies,)),
        pltpu.SemaphoreType.DMA((ncopies,)),
    ]
    shapes = _halo_shapes(x)
    scratch += [pltpu.VMEM(sh.shape, sh.dtype) for sh in shapes]
    scratch += [pltpu.SemaphoreType.DMA((8,)), pltpu.SemaphoreType.DMA((8,))]
    out, *got = pl.pallas_call(
        functools.partial(reduce_kernel, nfilt, nspace, pr, sr, x.shape[2]),
        out_shape=[jax.ShapeDtypeStruct((pr + sr, LANES), jnp.float32)] + shapes,
        in_specs=[pl.BlockSpec(memory_space=pltpu.VMEM)] * 2,
        out_specs=[pl.BlockSpec(memory_space=pltpu.VMEM)] * 9,
        scratch_shapes=scratch,
        compiler_params=pltpu.CompilerParams(collective_id=0, has_side_effects=True),
        cost_estimate=pl.CostEstimate(
            flops=0, transcendentals=0, bytes_accessed=200 * 1024 * 1024
        ),
    )(buf, x)
    panel = out[:pr].reshape(-1)[:width]
    small = out[pr:].reshape(-1)[: small.shape[0]]
    return panel, small, got


def solution(mesh):
    in_specs = (
        P(None, "space", "filt"),
        P(None, "space", "filt"),
        P(),
        P(),
        P(),
        P(),
        P(),
        P(),
        P(),
        P(),
        P(),
    )
    out_specs = (
        P(None, "space", "filt"),
        P(None, "space", "filt"),
        P(),
        P(),
        P(),
        P(),
        P("filt", None),
        P("filt"),
        P("filt", None),
        P(),
        P(),
    )
    return jax.shard_map(shards, mesh=mesh, in_specs=in_specs, out_specs=out_specs, check_vma=False)
```

```python
import functools
import math

import jax
import jax.numpy as jnp
from jax import lax
from jax.experimental import pallas as pl
from jax.experimental.pallas import tpu as pltpu
from jax.sharding import PartitionSpec as P

MESH = pl.DeviceIdType.MESH
LANES = 128


_DIRS = [(-1, 0), (1, 0), (0, -1), (0, 1), (-1, -1), (-1, 1), (1, -1), (1, 1)]


def _lanes(df, cols):
    if df == 0:
        return slice(0, cols)
    if df > 0:
        return slice(cols - LANES, cols)
    return slice(0, LANES)


def _halo_ops(ns, nf, cols, x_ref, outs, slots, send_sem, recv_sem):
    s = lax.axis_index("space")
    f = lax.axis_index("filt")

    def exists(d):
        t, g = s + d[0], f + d[1]
        return (t >= 0) & (t < ns) & (g >= 0) & (g < nf)

    def desc(k):
        d = _DIRS[k]
        back = _DIRS.index((-d[0], -d[1]))
        return pltpu.make_async_remote_copy(
            src_ref=x_ref.at[:, :, _lanes(d[1], cols)],
            dst_ref=slots[back],
            send_sem=send_sem.at[k],
            recv_sem=recv_sem.at[back],
            device_id=(s + d[0], f + d[1]),
            device_id_type=MESH,
        )

    def signal(barrier):
        count = 0
        for d in _DIRS:

            @pl.when(exists(d))
            def _():
                pl.semaphore_signal(
                    barrier, inc=1, device_id=(s + d[0], f + d[1]), device_id_type=MESH
                )

            count = count + exists(d).astype(jnp.int32)
        return count

    def start():
        for k, d in enumerate(_DIRS):

            @pl.when(exists(d))
            def _():
                desc(k).start()

    def finish():
        for k, d in enumerate(_DIRS):
            back = _DIRS.index((-d[0], -d[1]))

            @pl.when(exists(d))
            def _():
                desc(k).wait_send()
                desc(back).wait_recv()
                outs[k][...] = slots[k][...]

            @pl.when(jnp.logical_not(exists(d)))
            def _():
                outs[k][...] = jnp.zeros(outs[k].shape, outs[k].dtype)

    return signal, start, finish


def halo_kernel(ns, nf, cols, x_ref, *refs):
    signal, start, finish = _halo_ops(ns, nf, cols, x_ref, refs[:8], refs[8:16], *refs[16:])
    barrier = pltpu.get_barrier_semaphore()
    pl.semaphore_wait(barrier, signal(barrier))
    start()
    finish()


def _halo_shapes(x):
    channels, rows, cols = x.shape
    return [
        jax.ShapeDtypeStruct((channels, rows, _lanes(d[1], cols).stop - _lanes(d[1], cols).start), x.dtype)
        for d in _DIRS
    ]


def _assemble(x, got, width):
    rows = x.shape[1]
    piece = dict(zip(_DIRS, got))
    hi_r, lo_r = slice(rows - width, rows), slice(0, width)
    above = piece[(-1, 0)][:, hi_r, :]
    below = piece[(1, 0)][:, lo_r, :]
    lw = piece[(0, -1)].shape[2]
    left = piece[(0, -1)][:, :, lw - width : lw]
    right = piece[(0, 1)][:, :, 0:width]
    top_left = piece[(-1, -1)][:, hi_r, lw - width : lw]
    top_right = piece[(-1, 1)][:, hi_r, 0:width]
    bottom_left = piece[(1, -1)][:, lo_r, lw - width : lw]
    bottom_right = piece[(1, 1)][:, lo_r, 0:width]
    return jnp.concatenate(
        [
            jnp.concatenate([top_left, above, top_right], axis=2),
            jnp.concatenate([left, x, right], axis=2),
            jnp.concatenate([bottom_left, below, bottom_right], axis=2),
        ],
        axis=1,
    )


def padded_2(x, sides, width, collective_id):
    del sides
    ns, nf = lax.axis_size("space"), lax.axis_size("filt")
    shapes = _halo_shapes(x)
    got = pl.pallas_call(
        functools.partial(halo_kernel, ns, nf, x.shape[2]),
        out_shape=shapes,
        in_specs=[pl.BlockSpec(memory_space=pltpu.VMEM)],
        out_specs=[pl.BlockSpec(memory_space=pltpu.VMEM)] * 8,
        scratch_shapes=[pltpu.VMEM(sh.shape, sh.dtype) for sh in shapes]
        + [pltpu.SemaphoreType.DMA((8,)), pltpu.SemaphoreType.DMA((8,))],
        compiler_params=pltpu.CompilerParams(
            collective_id=collective_id, has_side_effects=True
        ),
    )(x)
    return _assemble(x, got, width)


def dw_kernel(flip, cb, x_ref, k_ref, *rest):
    cot_ref = rest[0] if len(rest) > 1 else None
    o_ref = rest[-1]
    channels, rows, cols = o_ref.shape
    wide = x_ref.shape[2]

    def block(i, carry):
        ch = pl.ds(pl.multiple_of(i * cb, cb), cb)
        x = x_ref[:, ch, :].astype(jnp.float32)
        acc = jnp.zeros((rows, cb, cols), jnp.float32)
        for shift_col in range(7):
            c0 = 6 - shift_col if flip else shift_col
            xb = pltpu.roll(x, shift=wide - c0, axis=2) if c0 else x
            xb = xb[:, :, :cols]
            for shift_row in range(7):
                r0 = 6 - shift_row if flip else shift_row
                kv = k_ref[ch, pl.ds(shift_row * 7 + shift_col, 1)]
                acc = acc + kv[None] * xb[r0 : r0 + rows]
        for r in range(rows):
            if cot_ref is None:
                o_ref[ch, r, :] = acc[r]
            else:
                o_ref[ch, r, :] = (cot_ref[ch, r, :].astype(jnp.float32) + acc[r]).astype(o_ref.dtype)
        return carry

    lax.fori_loop(0, channels // cb, block, 0)


def _dw(padded, kernel, row_count, col_count, flip, cot=None):
    channels = padded.shape[0]
    wide = -(-padded.shape[2] // LANES) * LANES
    x = jnp.transpose(padded, (1, 0, 2))
    x = jnp.pad(x, ((0, 0), (0, 0), (0, wide - padded.shape[2])))
    taps = kernel.reshape(channels, 49)
    cb = 8
    out = pl.pallas_call(
        functools.partial(dw_kernel, flip, cb),
        out_shape=jax.ShapeDtypeStruct(
            (channels, row_count, col_count), jnp.float32 if cot is None else cot.dtype
        ),
        in_specs=[pl.BlockSpec(memory_space=pltpu.VMEM)] * (2 if cot is None else 3),
        out_specs=pl.BlockSpec(memory_space=pltpu.VMEM),
    )(x, taps, *([] if cot is None else [cot]))
    return out


def depthwise(padded, kernel, row_count, col_count):
    return _dw(padded, kernel, row_count, col_count, False)


def conv_back(padded, kernel, row_count, col_count, cot):
    return _dw(padded, kernel, row_count, col_count, True, cot)


def kernel_terms(padded, convolution_gradient, row_count, col_count):
    ksize = 7
    columns = []
    for shift_col in range(ksize):
        corr = jnp.einsum(
            "crj,cij->cri",
            padded[:, :, shift_col : shift_col + col_count],
            convolution_gradient,
            preferred_element_type=jnp.float32,
        )
        total = corr[:, 0:ksize, 0]
        for row in range(1, row_count):
            total = total + corr[:, row : row + ksize, row]
        columns.append(total)
    return jnp.stack(columns, axis=2)


def gelu_exact(value):
    return value * (1.0 + jax.scipy.special.erf(value / math.sqrt(2.0))) * 0.5


def gelu_slope(value):
    return (1.0 + jax.scipy.special.erf(value / math.sqrt(2.0))) * 0.5 + value * jnp.exp(
        -0.5 * value * value
    ) / math.sqrt(2.0 * math.pi)


def shards(
    image,
    cotangent,
    kernel,
    dw_bias,
    layer_norm_gain,
    layer_norm_bias,
    w_expand,
    b_expand,
    w_reduce,
    b_reduce,
    layer_scale,
):
    channels, row_count, col_count = image.shape
    panel_rows = w_expand.shape[0] // lax.axis_size("filt")
    tok_count = row_count * col_count
    padded = padded_2(image, (("space", 1), ("filt", 2)), 3, 1)
    conv = depthwise(padded, kernel, row_count, col_count)
    conv = conv + dw_bias[:, None, None]
    flat = conv.reshape(channels, tok_count)
    average = jnp.mean(flat, axis=0, keepdims=True)
    mean_removed = flat - average
    inverse_deviation = lax.rsqrt(
        jnp.mean(mean_removed * mean_removed, axis=0, keepdims=True) + 1e-06
    )
    standardized_input = mean_removed * inverse_deviation
    normalized_input = (
        standardized_input * layer_norm_gain[:, None] + layer_norm_bias[:, None]
    ).astype(jnp.bfloat16)
    hidden = (
        jnp.dot(w_expand, normalized_input, preferred_element_type=jnp.float32)
        + b_expand.astype(jnp.float32)[:, None]
    )
    active = gelu_exact(hidden).astype(jnp.bfloat16)
    branch = (
        lax.dot_general(
            w_reduce, active, (((0,), (0,)), ((), ())), preferred_element_type=jnp.float32
        )
        + b_reduce[:, None]
    )
    resid = image.reshape(channels, tok_count).astype(jnp.float32)
    output = (
        (resid + layer_scale[:, None] * branch)
        .astype(jnp.bfloat16)
        .reshape(channels, row_count, col_count)
    )
    cot_flat = cotangent.reshape(channels, tok_count).astype(jnp.float32)
    scaled = layer_scale[:, None] * cot_flat
    g_scale = jnp.sum(cot_flat * branch, axis=1)
    g_rbias = jnp.sum(scaled, axis=1)
    d_branch = scaled.astype(jnp.bfloat16)
    g_reduce = lax.dot_general(
        active, d_branch, (((1,), (1,)), ((), ())), preferred_element_type=jnp.float32
    )
    d_active = jnp.dot(w_reduce, d_branch, preferred_element_type=jnp.float32)
    d_hidden = (d_active * gelu_slope(hidden)).astype(jnp.bfloat16)
    g_ebias = jnp.sum(d_hidden.astype(jnp.float32), axis=1)
    g_expand = lax.dot_general(
        d_hidden, normalized_input, (((1,), (1,)), ((), ())), preferred_element_type=jnp.float32
    )
    normalized_gradient = lax.dot_general(
        w_expand, d_hidden, (((0,), (0,)), ((), ())), preferred_element_type=jnp.float32
    )
    norm_gain_gradient = jnp.sum(normalized_gradient * standardized_input, axis=1)
    g_lbias = jnp.sum(normalized_gradient, axis=1)
    standardized_gradient = normalized_gradient * layer_norm_gain[:, None]
    convolution_gradient = inverse_deviation * (
        standardized_gradient
        - jnp.mean(standardized_gradient, axis=0, keepdims=True)
        - standardized_input
        * jnp.mean(standardized_gradient * standardized_input, axis=0, keepdims=True)
    )
    convolution_gradient = convolution_gradient.astype(jnp.bfloat16).reshape(
        channels, row_count, col_count
    )
    d_float = convolution_gradient.astype(jnp.float32)
    g_dbias = jnp.sum(d_float, axis=(1, 2))
    g_kernel = kernel_terms(padded, convolution_gradient, row_count, col_count)
    factor = 1.0 / math.sqrt(tok_count * lax.axis_size("space") * lax.axis_size("filt"))
    parts = lax.axis_size("filt")
    panels = jnp.concatenate(
        [
            g_reduce.reshape(parts, panel_rows * channels),
            g_expand.reshape(parts, panel_rows * channels),
            g_ebias.reshape(parts, panel_rows),
        ],
        axis=1,
    )
    small = jnp.concatenate(
        [
            g_kernel.reshape(-1),
            g_dbias,
            norm_gain_gradient,
            g_lbias,
            g_scale,
            g_rbias,
        ]
    )
    panel, small, got = grad_reduce(panels, small, convolution_gradient)
    padded_grad = _assemble(convolution_gradient, got, 3)
    image_grad = conv_back(padded_grad, kernel, row_count, col_count, cotangent)
    total = jnp.concatenate([panel, small])
    total = total * factor
    cut = [panel_rows * channels, panel_rows * channels, panel_rows]
    g_reduce = total[: cut[0]].reshape(panel_rows, channels)
    g_expand = total[cut[0] : cut[0] + cut[1]].reshape(panel_rows, channels)
    g_ebias = total[cut[0] + cut[1] : sum(cut)]
    rest = total[sum(cut) :]
    ksq = kernel.shape[1] * kernel.shape[2]
    g_kernel = rest[: channels * ksq].reshape(kernel.shape)
    g_dbias, norm_gain_gradient, g_lbias, g_scale, g_rbias = (
        rest[channels * ksq + channels * i : channels * ksq + channels * (i + 1)]
        for i in range(5)
    )
    return (
        output,
        image_grad,
        g_kernel,
        g_dbias,
        norm_gain_gradient,
        g_lbias,
        g_expand,
        g_ebias,
        g_reduce,
        g_rbias,
        g_scale,
    )


def _rows(length):
    return -(-length // (8 * LANES)) * 8


def _flip(index, bit):
    return index + bit - 2 * bit * ((index // bit) % 2)


def reduce_kernel(nfilt, nspace, pr, sr, cols, buf_ref, x_ref, out_ref, *refs):
    levels = nfilt.bit_length() - 1
    steps = nspace.bit_length() - 1
    halo_outs = refs[:8]
    scratch = refs[8:]
    recvs = scratch[:levels]
    stages = scratch[levels : 2 * levels]
    recv_s, send_sem, recv_sem = scratch[2 * levels : 2 * levels + 3]
    halo = scratch[2 * levels + 3 :]
    halo_signal, halo_start, halo_finish = _halo_ops(
        nspace, nfilt, cols, x_ref, halo_outs, halo[:8], halo[8], halo[9]
    )
    s = lax.axis_index("space")
    f = lax.axis_index("filt")

    peers = []
    bit = nfilt // 2
    while bit >= 1:
        peers.append((s, _flip(f, bit)))
        bit //= 2
    for k in range(steps):
        peers.append((_flip(s, 1 << k), f))
    barrier = pltpu.get_barrier_semaphore()
    for peer in peers:
        pl.semaphore_signal(barrier, inc=1, device_id=peer, device_id_type=MESH)
    count = halo_signal(barrier)
    pl.semaphore_wait(barrier, count + len(peers))
    halo_start()

    held = buf_ref
    count = nfilt
    bit = nfilt // 2
    sem = 0
    for level in range(levels):
        half = count // 2
        upper = (f // bit) % 2
        rows = half * pr
        peer = peers[level]
        send_panels = pltpu.make_async_remote_copy(
            src_ref=held.at[pl.ds(pl.multiple_of((1 - upper) * rows, 8), rows)],
            dst_ref=recvs[level].at[pl.ds(0, rows)],
            send_sem=send_sem.at[sem],
            recv_sem=recv_sem.at[sem],
            device_id=peer,
            device_id_type=MESH,
        )
        send_small = pltpu.make_async_remote_copy(
            src_ref=held.at[pl.ds(count * pr, sr)],
            dst_ref=recvs[level].at[pl.ds(rows, sr)],
            send_sem=send_sem.at[sem + 1],
            recv_sem=recv_sem.at[sem + 1],
            device_id=peer,
            device_id_type=MESH,
        )
        send_panels.start()
        send_small.start()
        send_panels.wait()
        send_small.wait()
        sem += 2
        stage = stages[level]
        stage[pl.ds(0, rows)] = (
            held[pl.ds(pl.multiple_of(upper * rows, 8), rows)] + recvs[level][pl.ds(0, rows)]
        )
        stage[pl.ds(rows, sr)] = held[pl.ds(count * pr, sr)] + recvs[level][pl.ds(rows, sr)]
        held = stage
        count = half
        bit //= 2

    if levels == 0:
        out_ref[...] = buf_ref[...]
    else:
        out_ref[...] = held[...]
    for k in range(steps):
        copy = pltpu.make_async_remote_copy(
            src_ref=out_ref,
            dst_ref=recv_s.at[k],
            send_sem=send_sem.at[sem],
            recv_sem=recv_sem.at[sem],
            device_id=peers[levels + k],
            device_id_type=MESH,
        )
        copy.start()
        copy.wait()
        sem += 1
        out_ref[...] = out_ref[...] + recv_s[k]
    halo_finish()


def grad_reduce(panels, small, x):
    nfilt = lax.axis_size("filt")
    nspace = lax.axis_size("space")
    width = panels.shape[1]
    pr = _rows(width)
    sr = _rows(small.shape[0])
    buf = jnp.concatenate(
        [
            jnp.pad(panels, ((0, 0), (0, pr * LANES - width))).reshape(nfilt * pr, LANES),
            jnp.pad(small, (0, sr * LANES - small.shape[0])).reshape(sr, LANES),
        ]
    )
    levels = nfilt.bit_length() - 1
    steps = nspace.bit_length() - 1
    scratch = []
    count = nfilt
    for _ in range(levels):
        count //= 2
        scratch.append(pltpu.VMEM((count * pr + sr, LANES), jnp.float32))
    count = nfilt
    for _ in range(levels):
        count //= 2
        scratch.append(pltpu.VMEM((count * pr + sr, LANES), jnp.float32))
    ncopies = 2 * levels + steps
    scratch += [
        pltpu.VMEM((max(steps, 1), pr + sr, LANES), jnp.float32),
        pltpu.SemaphoreType.DMA((ncopies,)),
        pltpu.SemaphoreType.DMA((ncopies,)),
    ]
    shapes = _halo_shapes(x)
    scratch += [pltpu.VMEM(sh.shape, sh.dtype) for sh in shapes]
    scratch += [pltpu.SemaphoreType.DMA((8,)), pltpu.SemaphoreType.DMA((8,))]
    out, *got = pl.pallas_call(
        functools.partial(reduce_kernel, nfilt, nspace, pr, sr, x.shape[2]),
        out_shape=[jax.ShapeDtypeStruct((pr + sr, LANES), jnp.float32)] + shapes,
        in_specs=[pl.BlockSpec(memory_space=pltpu.VMEM)] * 2,
        out_specs=[pl.BlockSpec(memory_space=pltpu.VMEM)] * 9,
        scratch_shapes=scratch,
        compiler_params=pltpu.CompilerParams(collective_id=0, has_side_effects=True),
        cost_estimate=pl.CostEstimate(
            flops=0, transcendentals=0, bytes_accessed=200 * 1024 * 1024
        ),
    )(buf, x)
    panel = out[:pr].reshape(-1)[:width]
    small = out[pr:].reshape(-1)[: small.shape[0]]
    return panel, small, got


def solution(mesh):
    in_specs = (
        P(None, "space", "filt"),
        P(None, "space", "filt"),
        P(),
        P(),
        P(),
        P(),
        P(),
        P(),
        P(),
        P(),
        P(),
    )
    out_specs = (
        P(None, "space", "filt"),
        P(None, "space", "filt"),
        P(),
        P(),
        P(),
        P(),
        P("filt", None),
        P("filt"),
        P("filt", None),
        P(),
        P(),
    )
    return jax.shard_map(shards, mesh=mesh, in_specs=in_specs, out_specs=out_specs, check_vma=False)
```

```python
import functools
import math

import jax
import jax.numpy as jnp
from jax import lax
from jax.experimental import pallas as pl
from jax.experimental.pallas import tpu as pltpu
from jax.sharding import PartitionSpec as P

MESH = pl.DeviceIdType.MESH
LANES = 128


_DIRS = [(-1, 0), (1, 0), (0, -1), (0, 1), (-1, -1), (-1, 1), (1, -1), (1, 1)]


def _lanes(df, cols):
    if df == 0:
        return slice(0, cols)
    if df > 0:
        return slice(cols - LANES, cols)
    return slice(0, LANES)


def _halo_ops(ns, nf, cols, x_ref, outs, slots, send_sem, recv_sem):
    s = lax.axis_index("space")
    f = lax.axis_index("filt")

    def exists(d):
        t, g = s + d[0], f + d[1]
        return (t >= 0) & (t < ns) & (g >= 0) & (g < nf)

    def desc(k):
        d = _DIRS[k]
        back = _DIRS.index((-d[0], -d[1]))
        return pltpu.make_async_remote_copy(
            src_ref=x_ref.at[:, :, _lanes(d[1], cols)],
            dst_ref=slots[back],
            send_sem=send_sem.at[k],
            recv_sem=recv_sem.at[back],
            device_id=(s + d[0], f + d[1]),
            device_id_type=MESH,
        )

    def signal(barrier):
        count = 0
        for d in _DIRS:

            @pl.when(exists(d))
            def _():
                pl.semaphore_signal(
                    barrier, inc=1, device_id=(s + d[0], f + d[1]), device_id_type=MESH
                )

            count = count + exists(d).astype(jnp.int32)
        return count

    def start():
        for k, d in enumerate(_DIRS):

            @pl.when(exists(d))
            def _():
                desc(k).start()

    def finish():
        for k, d in enumerate(_DIRS):
            back = _DIRS.index((-d[0], -d[1]))

            @pl.when(exists(d))
            def _():
                desc(k).wait_send()
                desc(back).wait_recv()
                outs[k][...] = slots[k][...]

            @pl.when(jnp.logical_not(exists(d)))
            def _():
                outs[k][...] = jnp.zeros(outs[k].shape, outs[k].dtype)

    return signal, start, finish


def halo_kernel(ns, nf, cols, x_ref, *refs):
    signal, start, finish = _halo_ops(ns, nf, cols, x_ref, refs[:8], refs[8:16], *refs[16:])
    barrier = pltpu.get_barrier_semaphore()
    pl.semaphore_wait(barrier, signal(barrier))
    start()
    finish()


def _halo_shapes(x):
    channels, rows, cols = x.shape
    return [
        jax.ShapeDtypeStruct((channels, rows, _lanes(d[1], cols).stop - _lanes(d[1], cols).start), x.dtype)
        for d in _DIRS
    ]


def _assemble(x, got, width):
    rows = x.shape[1]
    piece = dict(zip(_DIRS, got))
    hi_r, lo_r = slice(rows - width, rows), slice(0, width)
    above = piece[(-1, 0)][:, hi_r, :]
    below = piece[(1, 0)][:, lo_r, :]
    lw = piece[(0, -1)].shape[2]
    left = piece[(0, -1)][:, :, lw - width : lw]
    right = piece[(0, 1)][:, :, 0:width]
    top_left = piece[(-1, -1)][:, hi_r, lw - width : lw]
    top_right = piece[(-1, 1)][:, hi_r, 0:width]
    bottom_left = piece[(1, -1)][:, lo_r, lw - width : lw]
    bottom_right = piece[(1, 1)][:, lo_r, 0:width]
    return jnp.concatenate(
        [
            jnp.concatenate([top_left, above, top_right], axis=2),
            jnp.concatenate([left, x, right], axis=2),
            jnp.concatenate([bottom_left, below, bottom_right], axis=2),
        ],
        axis=1,
    )


def padded_2(x, sides, width, collective_id):
    del sides
    ns, nf = lax.axis_size("space"), lax.axis_size("filt")
    shapes = _halo_shapes(x)
    got = pl.pallas_call(
        functools.partial(halo_kernel, ns, nf, x.shape[2]),
        out_shape=shapes,
        in_specs=[pl.BlockSpec(memory_space=pltpu.VMEM)],
        out_specs=[pl.BlockSpec(memory_space=pltpu.VMEM)] * 8,
        scratch_shapes=[pltpu.VMEM(sh.shape, sh.dtype) for sh in shapes]
        + [pltpu.SemaphoreType.DMA((8,)), pltpu.SemaphoreType.DMA((8,))],
        compiler_params=pltpu.CompilerParams(
            collective_id=collective_id, has_side_effects=True
        ),
    )(x)
    return _assemble(x, got, width)


def dw_kernel(flip, cb, x_ref, k_ref, *rest):
    cot_ref = rest[0] if len(rest) > 1 else None
    o_ref = rest[-1]
    channels, rows, cols = o_ref.shape
    wide = x_ref.shape[2]

    def block(i, carry):
        ch = pl.ds(pl.multiple_of(i * cb, cb), cb)
        x = x_ref[:, ch, :].astype(jnp.float32)
        acc = jnp.zeros((rows, cb, cols), jnp.float32)
        for shift_col in range(7):
            c0 = 6 - shift_col if flip else shift_col
            xb = pltpu.roll(x, shift=wide - c0, axis=2) if c0 else x
            xb = xb[:, :, :cols]
            for shift_row in range(7):
                r0 = 6 - shift_row if flip else shift_row
                kv = k_ref[ch, pl.ds(shift_row * 7 + shift_col, 1)]
                acc = acc + kv[None] * xb[r0 : r0 + rows]
        for r in range(rows):
            if cot_ref is None:
                o_ref[ch, r, :] = acc[r]
            else:
                o_ref[ch, r, :] = (cot_ref[ch, r, :].astype(jnp.float32) + acc[r]).astype(o_ref.dtype)
        return carry

    lax.fori_loop(0, channels // cb, block, 0)


def _dw(padded, kernel, row_count, col_count, flip, cot=None):
    channels = padded.shape[0]
    wide = -(-padded.shape[2] // LANES) * LANES
    x = jnp.transpose(padded, (1, 0, 2))
    x = jnp.pad(x, ((0, 0), (0, 0), (0, wide - padded.shape[2])))
    taps = kernel.reshape(channels, 49)
    cb = 16
    out = pl.pallas_call(
        functools.partial(dw_kernel, flip, cb),
        out_shape=jax.ShapeDtypeStruct(
            (channels, row_count, col_count), jnp.float32 if cot is None else cot.dtype
        ),
        in_specs=[pl.BlockSpec(memory_space=pltpu.VMEM)] * (2 if cot is None else 3),
        out_specs=pl.BlockSpec(memory_space=pltpu.VMEM),
    )(x, taps, *([] if cot is None else [cot]))
    return out


def depthwise(padded, kernel, row_count, col_count):
    return _dw(padded, kernel, row_count, col_count, False)


def conv_back(padded, kernel, row_count, col_count, cot):
    return _dw(padded, kernel, row_count, col_count, True, cot)


def kernel_terms(padded, convolution_gradient, row_count, col_count):
    ksize = 7
    columns = []
    for shift_col in range(ksize):
        corr = jnp.einsum(
            "crj,cij->cri",
            padded[:, :, shift_col : shift_col + col_count],
            convolution_gradient,
            preferred_element_type=jnp.float32,
        )
        total = corr[:, 0:ksize, 0]
        for row in range(1, row_count):
            total = total + corr[:, row : row + ksize, row]
        columns.append(total)
    return jnp.stack(columns, axis=2)


def gelu_exact(value):
    return value * (1.0 + jax.scipy.special.erf(value / math.sqrt(2.0))) * 0.5


def gelu_slope(value):
    return (1.0 + jax.scipy.special.erf(value / math.sqrt(2.0))) * 0.5 + value * jnp.exp(
        -0.5 * value * value
    ) / math.sqrt(2.0 * math.pi)


def shards(
    image,
    cotangent,
    kernel,
    dw_bias,
    layer_norm_gain,
    layer_norm_bias,
    w_expand,
    b_expand,
    w_reduce,
    b_reduce,
    layer_scale,
):
    channels, row_count, col_count = image.shape
    panel_rows = w_expand.shape[0] // lax.axis_size("filt")
    tok_count = row_count * col_count
    padded = padded_2(image, (("space", 1), ("filt", 2)), 3, 1)
    conv = depthwise(padded, kernel, row_count, col_count)
    conv = conv + dw_bias[:, None, None]
    flat = conv.reshape(channels, tok_count)
    average = jnp.mean(flat, axis=0, keepdims=True)
    mean_removed = flat - average
    inverse_deviation = lax.rsqrt(
        jnp.mean(mean_removed * mean_removed, axis=0, keepdims=True) + 1e-06
    )
    standardized_input = mean_removed * inverse_deviation
    normalized_input = (
        standardized_input * layer_norm_gain[:, None] + layer_norm_bias[:, None]
    ).astype(jnp.bfloat16)
    hidden = (
        jnp.dot(w_expand, normalized_input, preferred_element_type=jnp.float32)
        + b_expand.astype(jnp.float32)[:, None]
    )
    active = gelu_exact(hidden).astype(jnp.bfloat16)
    branch = (
        lax.dot_general(
            w_reduce, active, (((0,), (0,)), ((), ())), preferred_element_type=jnp.float32
        )
        + b_reduce[:, None]
    )
    resid = image.reshape(channels, tok_count).astype(jnp.float32)
    output = (
        (resid + layer_scale[:, None] * branch)
        .astype(jnp.bfloat16)
        .reshape(channels, row_count, col_count)
    )
    cot_flat = cotangent.reshape(channels, tok_count).astype(jnp.float32)
    scaled = layer_scale[:, None] * cot_flat
    g_scale = jnp.sum(cot_flat * branch, axis=1)
    g_rbias = jnp.sum(scaled, axis=1)
    d_branch = scaled.astype(jnp.bfloat16)
    g_reduce = lax.dot_general(
        active, d_branch, (((1,), (1,)), ((), ())), preferred_element_type=jnp.float32
    )
    d_active = jnp.dot(w_reduce, d_branch, preferred_element_type=jnp.float32)
    d_hidden = (d_active * gelu_slope(hidden)).astype(jnp.bfloat16)
    g_ebias = jnp.sum(d_hidden.astype(jnp.float32), axis=1)
    g_expand = lax.dot_general(
        d_hidden, normalized_input, (((1,), (1,)), ((), ())), preferred_element_type=jnp.float32
    )
    normalized_gradient = lax.dot_general(
        w_expand, d_hidden, (((0,), (0,)), ((), ())), preferred_element_type=jnp.float32
    )
    norm_gain_gradient = jnp.sum(normalized_gradient * standardized_input, axis=1)
    g_lbias = jnp.sum(normalized_gradient, axis=1)
    standardized_gradient = normalized_gradient * layer_norm_gain[:, None]
    convolution_gradient = inverse_deviation * (
        standardized_gradient
        - jnp.mean(standardized_gradient, axis=0, keepdims=True)
        - standardized_input
        * jnp.mean(standardized_gradient * standardized_input, axis=0, keepdims=True)
    )
    convolution_gradient = convolution_gradient.astype(jnp.bfloat16).reshape(
        channels, row_count, col_count
    )
    d_float = convolution_gradient.astype(jnp.float32)
    g_dbias = jnp.sum(d_float, axis=(1, 2))
    g_kernel = kernel_terms(padded, convolution_gradient, row_count, col_count)
    factor = 1.0 / math.sqrt(tok_count * lax.axis_size("space") * lax.axis_size("filt"))
    parts = lax.axis_size("filt")
    panels = jnp.concatenate(
        [
            g_reduce.reshape(parts, panel_rows * channels),
            g_expand.reshape(parts, panel_rows * channels),
            g_ebias.reshape(parts, panel_rows),
        ],
        axis=1,
    )
    small = jnp.concatenate(
        [
            g_kernel.reshape(-1),
            g_dbias,
            norm_gain_gradient,
            g_lbias,
            g_scale,
            g_rbias,
        ]
    )
    panel, small, got = grad_reduce(panels, small, convolution_gradient)
    padded_grad = _assemble(convolution_gradient, got, 3)
    image_grad = conv_back(padded_grad, kernel, row_count, col_count, cotangent)
    total = jnp.concatenate([panel, small])
    total = total * factor
    cut = [panel_rows * channels, panel_rows * channels, panel_rows]
    g_reduce = total[: cut[0]].reshape(panel_rows, channels)
    g_expand = total[cut[0] : cut[0] + cut[1]].reshape(panel_rows, channels)
    g_ebias = total[cut[0] + cut[1] : sum(cut)]
    rest = total[sum(cut) :]
    ksq = kernel.shape[1] * kernel.shape[2]
    g_kernel = rest[: channels * ksq].reshape(kernel.shape)
    g_dbias, norm_gain_gradient, g_lbias, g_scale, g_rbias = (
        rest[channels * ksq + channels * i : channels * ksq + channels * (i + 1)]
        for i in range(5)
    )
    return (
        output,
        image_grad,
        g_kernel,
        g_dbias,
        norm_gain_gradient,
        g_lbias,
        g_expand,
        g_ebias,
        g_reduce,
        g_rbias,
        g_scale,
    )


def _rows(length):
    return -(-length // (8 * LANES)) * 8


def _flip(index, bit):
    return index + bit - 2 * bit * ((index // bit) % 2)


def reduce_kernel(nfilt, nspace, pr, sr, cols, buf_ref, x_ref, out_ref, *refs):
    levels = nfilt.bit_length() - 1
    steps = nspace.bit_length() - 1
    halo_outs = refs[:8]
    scratch = refs[8:]
    recvs = scratch[:levels]
    stages = scratch[levels : 2 * levels]
    recv_s, send_sem, recv_sem = scratch[2 * levels : 2 * levels + 3]
    halo = scratch[2 * levels + 3 :]
    halo_signal, halo_start, halo_finish = _halo_ops(
        nspace, nfilt, cols, x_ref, halo_outs, halo[:8], halo[8], halo[9]
    )
    s = lax.axis_index("space")
    f = lax.axis_index("filt")

    peers = []
    bit = nfilt // 2
    while bit >= 1:
        peers.append((s, _flip(f, bit)))
        bit //= 2
    for k in range(steps):
        peers.append((_flip(s, 1 << k), f))
    barrier = pltpu.get_barrier_semaphore()
    for peer in peers:
        pl.semaphore_signal(barrier, inc=1, device_id=peer, device_id_type=MESH)
    count = halo_signal(barrier)
    pl.semaphore_wait(barrier, count + len(peers))
    halo_start()

    held = buf_ref
    count = nfilt
    bit = nfilt // 2
    sem = 0
    for level in range(levels):
        half = count // 2
        upper = (f // bit) % 2
        rows = half * pr
        peer = peers[level]
        send_panels = pltpu.make_async_remote_copy(
            src_ref=held.at[pl.ds(pl.multiple_of((1 - upper) * rows, 8), rows)],
            dst_ref=recvs[level].at[pl.ds(0, rows)],
            send_sem=send_sem.at[sem],
            recv_sem=recv_sem.at[sem],
            device_id=peer,
            device_id_type=MESH,
        )
        send_small = pltpu.make_async_remote_copy(
            src_ref=held.at[pl.ds(count * pr, sr)],
            dst_ref=recvs[level].at[pl.ds(rows, sr)],
            send_sem=send_sem.at[sem + 1],
            recv_sem=recv_sem.at[sem + 1],
            device_id=peer,
            device_id_type=MESH,
        )
        send_panels.start()
        send_small.start()
        send_panels.wait()
        send_small.wait()
        sem += 2
        stage = stages[level]
        stage[pl.ds(0, rows)] = (
            held[pl.ds(pl.multiple_of(upper * rows, 8), rows)] + recvs[level][pl.ds(0, rows)]
        )
        stage[pl.ds(rows, sr)] = held[pl.ds(count * pr, sr)] + recvs[level][pl.ds(rows, sr)]
        held = stage
        count = half
        bit //= 2

    if levels == 0:
        out_ref[...] = buf_ref[...]
    else:
        out_ref[...] = held[...]
    for k in range(steps):
        copy = pltpu.make_async_remote_copy(
            src_ref=out_ref,
            dst_ref=recv_s.at[k],
            send_sem=send_sem.at[sem],
            recv_sem=recv_sem.at[sem],
            device_id=peers[levels + k],
            device_id_type=MESH,
        )
        copy.start()
        copy.wait()
        sem += 1
        out_ref[...] = out_ref[...] + recv_s[k]
    halo_finish()


def grad_reduce(panels, small, x):
    nfilt = lax.axis_size("filt")
    nspace = lax.axis_size("space")
    width = panels.shape[1]
    pr = _rows(width)
    sr = _rows(small.shape[0])
    buf = jnp.concatenate(
        [
            jnp.pad(panels, ((0, 0), (0, pr * LANES - width))).reshape(nfilt * pr, LANES),
            jnp.pad(small, (0, sr * LANES - small.shape[0])).reshape(sr, LANES),
        ]
    )
    levels = nfilt.bit_length() - 1
    steps = nspace.bit_length() - 1
    scratch = []
    count = nfilt
    for _ in range(levels):
        count //= 2
        scratch.append(pltpu.VMEM((count * pr + sr, LANES), jnp.float32))
    count = nfilt
    for _ in range(levels):
        count //= 2
        scratch.append(pltpu.VMEM((count * pr + sr, LANES), jnp.float32))
    ncopies = 2 * levels + steps
    scratch += [
        pltpu.VMEM((max(steps, 1), pr + sr, LANES), jnp.float32),
        pltpu.SemaphoreType.DMA((ncopies,)),
        pltpu.SemaphoreType.DMA((ncopies,)),
    ]
    shapes = _halo_shapes(x)
    scratch += [pltpu.VMEM(sh.shape, sh.dtype) for sh in shapes]
    scratch += [pltpu.SemaphoreType.DMA((8,)), pltpu.SemaphoreType.DMA((8,))]
    out, *got = pl.pallas_call(
        functools.partial(reduce_kernel, nfilt, nspace, pr, sr, x.shape[2]),
        out_shape=[jax.ShapeDtypeStruct((pr + sr, LANES), jnp.float32)] + shapes,
        in_specs=[pl.BlockSpec(memory_space=pltpu.VMEM)] * 2,
        out_specs=[pl.BlockSpec(memory_space=pltpu.VMEM)] * 9,
        scratch_shapes=scratch,
        compiler_params=pltpu.CompilerParams(collective_id=0, has_side_effects=True),
        cost_estimate=pl.CostEstimate(
            flops=0, transcendentals=0, bytes_accessed=200 * 1024 * 1024
        ),
    )(buf, x)
    panel = out[:pr].reshape(-1)[:width]
    small = out[pr:].reshape(-1)[: small.shape[0]]
    return panel, small, got


def solution(mesh):
    in_specs = (
        P(None, "space", "filt"),
        P(None, "space", "filt"),
        P(),
        P(),
        P(),
        P(),
        P(),
        P(),
        P(),
        P(),
        P(),
    )
    out_specs = (
        P(None, "space", "filt"),
        P(None, "space", "filt"),
        P(),
        P(),
        P(),
        P(),
        P("filt", None),
        P("filt"),
        P("filt", None),
        P(),
        P(),
    )
    return jax.shard_map(shards, mesh=mesh, in_specs=in_specs, out_specs=out_specs, check_vma=False)
```
